32 devices in a mesh: dp: 4 (over z), head: 8 (over y, x, core).
Axes of the slice: x: 2, y: 2, z: 4, core: 2. Of those that a mesh axis runs over, the one named last changes fastest.
Arguments:
- hidden_in: bfloat16 [8192, 1024], P(('dp', 'head')), may hold values from -6 to 6
- frame_cond: bfloat16 [32, 1024], P(('dp', 'head')), may hold values from -6 to 6
- query_weight: bfloat16 [1024, 1024], replicated, may hold values from -0.1875 to 0.1875
- key_weight: bfloat16 [1024, 1024], replicated, may hold values from -0.1875 to 0.1875
- value_weight: bfloat16 [1024, 1024], replicated, may hold values from -0.1875 to 0.1875
- output_weight: bfloat16 [1024, 1024], replicated, may hold values from -1.5 to 1.5
- up_weight: bfloat16 [1024, 4096], replicated, may hold values from -0.1875 to 0.1875
- down_weight: bfloat16 [4096, 1024], replicated, may hold values from -0.09375 to 0.09375
- modulation_weight: bfloat16 [1024, 6144], replicated, may hold values from -0.1875 to 0.1875
- clip_lengths: int32 [4, 3], P('dp'), may hold values from 1 to 4, 8 in all within a row
- patch_valid: int32 [8192], P('dp'), may hold values 0 or 1
- cotangent: bfloat16 [8192, 1024], P(('dp', 'head')), may hold values from -6 to 6
Outputs:
- block_out: bfloat16 [8192, 1024], P(('dp', 'head'))
- grad_input: float32 [8192, 1024], P(('dp', 'head'))
- grad_cond: float32 [32, 1024], P(('dp', 'head'))
- grad_query_weight: float32 [1024, 1024], P(('dp', 'head'))
- grad_key_weight: float32 [1024, 1024], P(('dp', 'head'))
- grad_value_weight: float32 [1024, 1024], P(('dp', 'head'))
- grad_output_weight: float32 [1024, 1024], P(('dp', 'head'))
- grad_up_weight: float32 [1024, 4096], P(('dp', 'head'))
- grad_down_weight: float32 [4096, 1024], P(('dp', 'head'))
- grad_modulation_weight: float32 [1024, 6144], P(('dp', 'head'))
- frame_rms: float32 [32, 3], P(('dp', 'head'))
The draws below stay inside these ranges and needn't reach their ends.
Inputs may be any that keep to these rules, and one draw needn't show every extreme that they name: `clip_lengths`: row g lists in order the frame counts of the 3 clips packed into the 8 frames of data group g; each row sums to 8 and its longest clip has exactly 4 frames.
All inputs are finite; a program needn't handle non-finite values. No bound on the sum of `patch_valid` on one device may be relied on, other than what follows from the above.
Results may differ from the reference program's by a relative error of at most 0.012.
The reference program's roundings to bfloat16 on the way count: a program that leaves them out, or rounds other values in their place, can miss the bound.
Values may be sent and summed in bfloat16 or wider, within the bound.
A program may use at most 192 MiB of HBM per device.

```python
import math
import jax
import jax.numpy as jnp
import numpy as np
from jax import lax

D = 1024
HEADS = 16
HEAD_DIM = 64
FF = 4096
PATCHES = 256
CLIPS = 3
FR_DEV = 1
TOK_DEV = 256
TOKENS = 8192
FRAMES = 32
N_DP = 4
N_HEAD = 8


def set_ends(drawn, own_key, least, top_value):
    longest = drawn.shape.index(max(drawn.shape))
    spots = []
    for shift in (0, 1):
        where = [jax.random.randint(jax.random.fold_in(own_key, axis), (), 0, length) for axis, length in enumerate(drawn.shape)]
        where[longest] = (where[longest] + shift) % drawn.shape[longest]
        spots.append(tuple(where))
    return drawn.at[spots[0]].set(least).at[spots[1]].set(top_value)


def shard_levels(rng, dims, pieces, smallest, high):
    loudness, own = 1.0, jax.random.fold_in(rng, 6)
    for dim, parts in pieces:
        heights = jnp.exp(jax.random.uniform(jax.random.fold_in(own, dim), (parts,), jnp.float32, smallest / len(pieces), high / len(pieces)))
        loudness = loudness * jnp.repeat(heights, dims[dim] // parts).reshape([-1 if axis == dim else 1 for axis in range(len(dims))])
    return loudness


def length_profile(count, total, reach, lean):
    weights = [(1 << 20) // math.isqrt(grade ** lean) + 1 for grade in range(2, count + 1)]
    spare, counts = total - reach - (count - 1), [1] * (count - 1)
    while spare > 0:
        movable = [i for i in range(count - 1) if counts[i] < reach]
        whole, left = sum([weights[i] for i in movable]), spare
        for i in movable:
            more = min(reach - counts[i], max(1, left * weights[i] // whole), spare)
            counts[i] = counts[i] + more
            spare = spare - more
    return np.array([reach] + counts)


def ragged(key, count, total, most, slope):
    if count == 2:
        one = jax.random.randint(key, (), max(1, total - most), min(most, total - 1) + 1)
        return jnp.stack([one, total - one])
    tallies = jnp.asarray(length_profile(count, total, most, slope), jnp.int32)
    pairs = (count - 1) // 2
    giver, taker = tallies[1:1 + 2 * pairs:2], tallies[2:2 + 2 * pairs:2]
    room = jnp.minimum(giver - 1, most - taker)
    shifted = jax.random.randint(jax.random.fold_in(key, 1), (pairs,), 0, 1 << 20) % (room + 1)
    tallies = tallies.at[1:1 + 2 * pairs:2].set(giver - shifted).at[2:2 + 2 * pairs:2].set(taker + shifted)
    return tallies[jax.random.permutation(jax.random.fold_in(key, 2), count)]


def centred(key, shape, scale, limit, shards=(), kind=jnp.bfloat16):
    entries = scale * jax.random.normal(key, shape, jnp.float32)
    if shards:
        entries = entries * shard_levels(key, shape, shards, -0.22, 0.18)
    return jnp.clip(entries, -limit, limit).astype(kind)


def setup_inputs(seed: int = 0) -> dict:
    key_of = jax.random.split(jax.random.key(seed), 13)
    return {
        "hidden_in": centred(key_of[0], (TOKENS, D), 1.0, 6.0, ((0, 32),)),
        "frame_cond": centred(key_of[1], (FRAMES, D), 1.0, 6.0, ((0, 32),)),
        "query_weight": centred(key_of[2], (D, D), D ** -0.5, 0.1875),
        "key_weight": centred(key_of[3], (D, D), D ** -0.5, 0.1875),
        "value_weight": centred(key_of[4], (D, D), D ** -0.5, 0.1875),
        "output_weight": centred(key_of[5], (D, D), (D // 64) ** -0.5, 1.5),
        "up_weight": centred(key_of[6], (D, FF), D ** -0.5, 0.1875),
        "down_weight": centred(key_of[7], (FF, D), FF ** -0.5, 0.09375),
        "modulation_weight": centred(key_of[8], (D, 6 * D), D ** -0.5, 0.1875),
        "clip_lengths": jax.vmap(lambda own: ragged(own, CLIPS, FR_DEV * N_HEAD, FR_DEV * N_HEAD // 2, 2))(jax.random.split(key_of[9], N_DP)).reshape((N_DP, CLIPS)).astype(jnp.int32),
        "patch_valid": set_ends((jax.random.randint(key_of[10], (TOKENS,), 0, 8) < 7).astype(jnp.int32), jax.random.fold_in(key_of[10], 1), 0, 1),
        "cotangent": centred(key_of[11], (TOKENS, D), 1.0, 6.0, ((0, 32),)),
    }


@jax.custom_vjp
def low(v):
    return lax.optimization_barrier(v.astype(jnp.bfloat16)).astype(jnp.float32)

@jax.custom_vjp
def low_back(v):
    return v

def low_keep(v):
    return (low(v), None)

def low_pass(kept, grad):
    return (grad,)

def back_keep(v):
    return (v, None)

def back_low(kept, grad):
    return (low(grad),)
low.defvjp(low_keep, low_pass)
low_back.defvjp(back_keep, back_low)
EPSILON = 1e-06
MASKED = -1e+30
HIGHEST = lax.Precision.HIGHEST

def rms_normed(values):
    return values * lax.rsqrt(lax.optimization_barrier(jnp.mean(values * values, axis=-1, keepdims=True)) + EPSILON)

def frequencies(half_dim):
    return jnp.exp(jnp.arange(half_dim, dtype=jnp.float32) * (-math.log(10000.0) / half_dim))

def rotate(values, angles):
    half_dim = values.shape[-1] // 2
    cosine = jnp.cos(angles)[:, None, :]
    sine_part = jnp.sin(angles)[:, None, :]
    first_half = values[..., :half_dim]
    second = values[..., half_dim:]
    return jnp.concatenate([first_half * cosine - second * sine_part, first_half * sine_part + second * cosine], axis=-1)

def group_layout(lengths, token_count, patches):
    frame_of = (jnp.arange(token_count, dtype=jnp.int32) // patches).astype(jnp.int32)
    clip_ends = jnp.cumsum(lengths).astype(jnp.int32)
    starts = (clip_ends - lengths).astype(jnp.int32)
    clip_of = lax.optimization_barrier(jnp.sum((frame_of[:, None] >= clip_ends[None, :]).astype(jnp.int32), axis=1)).astype(jnp.int32)
    picked = clip_of[:, None] == jnp.arange(lengths.shape[0], dtype=jnp.int32)[None, :]
    position = frame_of - lax.optimization_barrier(jnp.sum(jnp.where(picked, starts[None, :], 0), axis=1)).astype(jnp.int32)
    return (clip_of, frame_of, position.astype(jnp.int32))

def allowed_block(row_start, row_count, clip_of, frame_of, valid_mask):
    key_count = clip_of.shape[0]
    key_index = jnp.arange(key_count, dtype=jnp.int32)
    row_index = row_start + jnp.arange(row_count, dtype=jnp.int32)
    clip_rows = lax.dynamic_slice_in_dim(clip_of, row_start, row_count)
    frame_rows = lax.dynamic_slice_in_dim(frame_of, row_start, row_count)
    same_clip = clip_rows[:, None] == clip_of[None, :]
    causal = frame_of[None, :] <= frame_rows[:, None]
    usable = (valid_mask[None, :] == 1) | (row_index[:, None] == key_index[None, :])
    return same_clip & causal & usable

def attention(queries, all_keys, all_values, clip_of, frame_of, valid_mask, scaling):
    token_count = queries.shape[0]
    block_rows = min(512, token_count)

    def one_block(row_start):
        query_rows = lax.dynamic_slice_in_dim(queries, row_start, block_rows, 0)
        scores = jnp.einsum('qhd,khd->hqk', query_rows, all_keys, precision=HIGHEST) * scaling
        scores = low_back(scores)
        permitted = allowed_block(row_start, block_rows, clip_of, frame_of, valid_mask)
        scores = jnp.where(permitted[None], scores, MASKED)
        soft_probs = low(jax.nn.softmax(scores, axis=-1))
        return jnp.einsum('hqk,khd->qhd', soft_probs, all_values, precision=HIGHEST)
    starts = jnp.arange(0, token_count, block_rows, dtype=jnp.int32)
    blocks = lax.map(jax.checkpoint(one_block), starts)
    return blocks.reshape(queries.shape)

def frame_stats(values, valid_f, frame_count):
    sums = lax.optimization_barrier(jnp.sum(values * values, axis=1)) * valid_f
    per_frame = lax.optimization_barrier(jnp.sum(sums.reshape(frame_count, -1), axis=1))
    return jnp.sqrt(per_frame / (PATCHES * D) + EPSILON)

def layer_group(tokens, condition, query_weight, key_weight, value_weight, output_weight, up_weight, down_weight, modulation_weight, clip_of, frame_of, position, valid_mask):
    frame_count = condition.shape[0]
    cond_act = low(jax.nn.silu(condition))
    modulation = low_back(jnp.dot(cond_act, modulation_weight, precision=HIGHEST))
    per_token = jnp.repeat(modulation, PATCHES, axis=0)
    shift_one, scale_one, gate_one, shift_two, scale_two, gate_two = jnp.split(per_token, 6, axis=1)
    normed_one = low(rms_normed(tokens) * (1.0 + scale_one) + shift_one)
    angles = position.astype(jnp.float32)[:, None] * frequencies(HEAD_DIM // 2)[None, :]

    def project_rotated(weight_matrix):
        raw_proj = low_back(jnp.dot(normed_one, weight_matrix, precision=HIGHEST))
        return low_back(low(rotate(raw_proj.reshape(-1, HEADS, HEAD_DIM), angles)))
    queries = project_rotated(query_weight)
    all_keys = project_rotated(key_weight)
    all_values = low_back(low(jnp.dot(normed_one, value_weight, precision=HIGHEST))).reshape(-1, HEADS, HEAD_DIM)
    scaling = 1.0 / math.sqrt(HEAD_DIM)
    attended = attention(queries, all_keys, all_values, clip_of, frame_of, valid_mask, scaling).reshape(-1, D)
    attended = low_back(low(attended))
    branch_attn = low_back(jnp.dot(attended, output_weight, precision=HIGHEST))
    middle = tokens + gate_one * branch_attn
    normed_two = low(rms_normed(middle) * (1.0 + scale_two) + shift_two)
    hidden = low_back(jnp.dot(normed_two, up_weight, precision=HIGHEST))
    active = low(jax.nn.gelu(hidden))
    branch_mlp = low_back(jnp.dot(active, down_weight, precision=HIGHEST))
    result = middle + gate_two * branch_mlp
    valid_f = valid_mask.astype(jnp.float32)
    statistics = jnp.stack([frame_stats(gate_one * branch_attn, valid_f, frame_count), frame_stats(gate_two * branch_mlp, valid_f, frame_count), frame_stats(result, valid_f, frame_count)], axis=1)
    return (result, statistics)

def reference(hidden_in, frame_cond, query_weight, key_weight, value_weight, output_weight, up_weight, down_weight, modulation_weight, clip_lengths, patch_valid, cotangent):
    group_tokens = TOK_DEV * N_HEAD
    group_frames = FR_DEV * N_HEAD
    tokens = hidden_in.astype(jnp.float32).reshape(N_DP, group_tokens, D)
    conditions = frame_cond.astype(jnp.float32).reshape(N_DP, group_frames, D)
    cotangents = cotangent.astype(jnp.float32).reshape(N_DP, group_tokens, D)
    valid_all = patch_valid.reshape(N_DP, group_tokens)
    matrices = (query_weight.astype(jnp.float32), key_weight.astype(jnp.float32), value_weight.astype(jnp.float32), output_weight.astype(jnp.float32), up_weight.astype(jnp.float32), down_weight.astype(jnp.float32), modulation_weight.astype(jnp.float32))

    def group_step(totals, inputs):
        group_in, group_cond, group_cot, group_valid, group_lengths = inputs
        clip_of, frame_of, position = group_layout(group_lengths, group_tokens, PATCHES)

        def forward(token_arg, cond_arg, *weight_args):
            return layer_group(token_arg, cond_arg, *weight_args, clip_of, frame_of, position, group_valid)
        result, pull_back, statistics = jax.vjp(forward, group_in, group_cond, *matrices, has_aux=True)
        gradients = pull_back(group_cot)
        totals = tuple((summed + added for summed, added in zip(totals, gradients[2:])))
        return (totals, (result, gradients[0], gradients[1], statistics))
    zero_grads = tuple((jnp.zeros_like(matrix) for matrix in matrices))
    totals, (results, grad_in, grad_cond, statistics) = lax.scan(group_step, zero_grads, (tokens, conditions, cotangents, valid_all, clip_lengths))
    return (results.reshape(TOKENS, D).astype(jnp.bfloat16), grad_in.reshape(TOKENS, D), grad_cond.reshape(FRAMES, D), totals[0], totals[1], totals[2], totals[3], totals[4], totals[5], totals[6], statistics.reshape(FRAMES, 3))
```

```python
import math

import jax
import jax.numpy as jnp
from jax import lax
from jax.experimental import pallas as pl
from jax.experimental.pallas import tpu as pltpu
from jax.sharding import PartitionSpec as P

HEADS = 16
HEAD_DIM = 64
PATCHES = 256


EPSILON = 1e-06
MASKED = -1e30


def rms_normed(values):
    return values * lax.rsqrt(jnp.mean(values * values, axis=-1, keepdims=True) + EPSILON)


def modulate(values, shift, scaling):
    return rms_normed(values) * (1.0 + scaling) + shift


def frequencies(half_dim):
    return jnp.exp(jnp.arange(half_dim, dtype=jnp.float32) * (-math.log(10000.0) / half_dim))


def rotate(values, angles):
    half_dim = values.shape[-1] // 2
    cosine = jnp.cos(angles)[:, None, :]
    sine_part = jnp.sin(angles)[:, None, :]
    first_half = values[..., :half_dim]
    second = values[..., half_dim:]
    return jnp.concatenate(
        [first_half * cosine - second * sine_part, first_half * sine_part + second * cosine],
        axis=-1,
    )


def group_layout(lengths, token_count, patches):
    frame_of = jnp.arange(token_count, dtype=jnp.int32) // patches
    clip_ends = jnp.cumsum(lengths)
    starts = clip_ends - lengths
    clip_of = jnp.sum((frame_of[:, None] >= clip_ends[None, :]).astype(jnp.int32), axis=1)
    picked = clip_of[:, None] == jnp.arange(lengths.shape[0], dtype=jnp.int32)[None, :]
    position = frame_of - jnp.sum(jnp.where(picked, starts[None, :], 0), axis=1)
    return (clip_of, frame_of, position)


def inner_rows(left, right):
    return lax.dot_general(
        left, right, (((0,), (0,)), ((), ())), preferred_element_type=jnp.float32
    )


def times_transposed(left, right):
    return lax.dot_general(
        left, right, (((1,), (1,)), ((), ())), preferred_element_type=jnp.float32
    )


def frame_stats(values, valid_f):
    sums = jnp.sum(values * values, axis=2) * valid_f
    return jnp.sqrt(jnp.sum(sums, axis=1) / (values.shape[1] * values.shape[2]) + EPSILON)


def dot_nt(left, right):
    return lax.dot_general(
        left, right, (((1,), (1,)), ((), ())), preferred_element_type=jnp.float32
    )


def dot_nn(left, right):
    return lax.dot_general(
        left, right, (((1,), (0,)), ((), ())), preferred_element_type=jnp.float32
    )


def head_parts(block):
    lane = lax.broadcasted_iota(jnp.int32, block.shape, 1)
    zero = jnp.zeros_like(block)
    return jnp.where(lane < HEAD_DIM, block, zero), jnp.where(lane < HEAD_DIM, zero, block)


def key_bias(bias_ref, key_frame, frame):
    half = bias_ref[pl.ds(key_frame * PATCHES, PATCHES), :]
    bias = jnp.concatenate([half, half], axis=1)
    row = lax.broadcasted_iota(jnp.int32, bias.shape, 0)
    column = lax.broadcasted_iota(jnp.int32, bias.shape, 1)
    own = (row == column) & (key_frame == frame)
    return jnp.where(own, 0.0, bias)


def attend_forward_kernel(first_ref, q_ref, k_ref, v_ref, bias_ref, o_ref, lse_ref, scores):
    frames = q_ref.shape[0] // PATCHES

    def one_frame(frame, _):
        rows = pl.ds(frame * PATCHES, PATCHES)
        parts = head_parts(q_ref[rows, :] * jnp.bfloat16(0.125))
        first = first_ref[frame]

        def score(key_frame, tops):
            keys = k_ref[pl.ds(key_frame * PATCHES, PATCHES), :]
            bias = key_bias(bias_ref, key_frame, frame)
            new = []
            for head in range(2):
                value = dot_nt(keys, parts[head]) + bias
                scores[head, key_frame - first] = value
                new.append(jnp.maximum(tops[head], jnp.max(value, axis=0, keepdims=True)))
            return tuple(new)

        low = jnp.full((1, PATCHES), MASKED, jnp.float32)
        tops = lax.fori_loop(first, frame + 1, score, (low, low))

        def exponent(key_frame, totals):
            new = []
            for head in range(2):
                value = jnp.exp(scores[head, key_frame - first] - tops[head])
                scores[head, key_frame - first] = value
                new.append(totals[head] + jnp.sum(value, axis=0, keepdims=True))
            return tuple(new)

        zero = jnp.zeros((1, PATCHES), jnp.float32)
        totals = lax.fori_loop(first, frame + 1, exponent, (zero, zero))
        inverse = [1.0 / total for total in totals]

        def weigh(key_frame, sums):
            turned = v_ref[pl.ds(key_frame * PATCHES, PATCHES), :].T
            new = []
            for head in range(2):
                probs = (scores[head, key_frame - first] * inverse[head]).astype(jnp.bfloat16)
                new.append(
                    sums[head]
                    + dot_nn(turned[head * HEAD_DIM : (head + 1) * HEAD_DIM, :], probs)
                )
            return tuple(new)

        empty = jnp.zeros((HEAD_DIM, PATCHES), jnp.float32)
        sums = lax.fori_loop(first, frame + 1, weigh, (empty, empty))
        o_ref[rows, :] = jnp.concatenate(sums, axis=0).T.astype(jnp.bfloat16)
        for head in range(2):
            lse_ref[frame, head : head + 1, :] = tops[head] + jnp.log(totals[head])
        return 0

    lax.fori_loop(0, frames, one_frame, 0)


def attend_backward_kernel(
    first_ref,
    q_ref,
    k_ref,
    v_ref,
    o_ref,
    do_ref,
    bias_ref,
    lse_ref,
    dq_ref,
    dk_ref,
    dv_ref,
    dk_sum,
    dv_sum,
):
    frames = q_ref.shape[0] // PATCHES
    dk_sum[...] = jnp.zeros_like(dk_sum)
    dv_sum[...] = jnp.zeros_like(dv_sum)

    def one_frame(frame, _):
        rows = pl.ds(frame * PATCHES, PATCHES)
        q_parts = head_parts(q_ref[rows, :] * jnp.bfloat16(0.125))
        grads = do_ref[rows, :]
        do_parts = head_parts(grads)
        product = (grads.astype(jnp.float32) * o_ref[rows, :].astype(jnp.float32)).T
        deltas = [
            jnp.sum(product[h * HEAD_DIM : (h + 1) * HEAD_DIM, :], axis=0, keepdims=True)
            for h in range(2)
        ]
        lses = [lse_ref[frame, h : h + 1, :] for h in range(2)]
        first = first_ref[frame]

        def one_block(key_frame, sums):
            where = pl.ds(key_frame * PATCHES, PATCHES)
            keys = k_ref[where, :]
            values = v_ref[where, :]
            turned = keys.T
            bias = key_bias(bias_ref, key_frame, frame)
            dv = dv_sum[where, :]
            dk = dk_sum[where, :]
            new = []
            for head in range(2):
                probs = jnp.exp(dot_nt(keys, q_parts[head]) + bias - lses[head])
                prob_grad = dot_nt(values, do_parts[head])
                score_grad = (probs * (prob_grad - deltas[head])).astype(jnp.bfloat16)
                dv = dv + dot_nn(probs.astype(jnp.bfloat16), do_parts[head])
                dk = dk + dot_nn(score_grad, q_parts[head])
                new.append(
                    sums[head]
                    + dot_nn(turned[head * HEAD_DIM : (head + 1) * HEAD_DIM, :], score_grad)
                )
            dv_sum[where, :] = dv
            dk_sum[where, :] = dk
            return tuple(new)

        empty = jnp.zeros((HEAD_DIM, PATCHES), jnp.float32)
        sums = lax.fori_loop(first, frame + 1, one_block, (empty, empty))
        dq_ref[rows, :] = (jnp.concatenate(sums, axis=0).T * 0.125).astype(jnp.bfloat16)
        return 0

    lax.fori_loop(0, frames, one_frame, 0)
    dk_ref[...] = dk_sum[...].astype(jnp.bfloat16)
    dv_ref[...] = dv_sum[...].astype(jnp.bfloat16)


IN_SMEM = pl.BlockSpec(memory_space=pltpu.SMEM)
IN_VMEM = pl.BlockSpec(memory_space=pltpu.VMEM)
IN_PLACE = pl.BlockSpec(memory_space=pl.ANY)
MESH_ID = pl.DeviceIdType.MESH


def attend_forward(first, queries, keys, values, bias):
    tokens, width = queries.shape
    frames = tokens // PATCHES
    return pl.pallas_call(
        attend_forward_kernel,
        out_shape=(
            jax.ShapeDtypeStruct((tokens, width), jnp.bfloat16),
            jax.ShapeDtypeStruct((frames, 2, PATCHES), jnp.float32),
        ),
        in_specs=[IN_SMEM] + [IN_VMEM] * 4,
        out_specs=(IN_VMEM, IN_VMEM),
        scratch_shapes=[pltpu.VMEM((2, 4, PATCHES, PATCHES), jnp.float32)],
        name="attend_forward",
    )(first, queries, keys, values, bias)


def attend_backward(first, queries, keys, values, attended, grads, bias, lse):
    tokens, width = queries.shape
    shape = jax.ShapeDtypeStruct((tokens, width), jnp.bfloat16)
    return pl.pallas_call(
        attend_backward_kernel,
        out_shape=(shape, shape, shape),
        in_specs=[IN_SMEM] + [IN_VMEM] * 7,
        out_specs=(IN_VMEM, IN_VMEM, IN_VMEM),
        scratch_shapes=[pltpu.VMEM((tokens, width), jnp.float32)] * 2,
        name="attend_backward",
    )(first, queries, keys, values, attended, grads, bias, lse)


def position_bits():
    head = lax.axis_index("head")
    core = lax.rem(head, 2)
    second = lax.rem(lax.div(head, 2), 2)
    third = lax.div(head, 4)
    return head, core, second, third


def scatter_kernel(n_dp, units, *refs):
    n_in = 6
    terms = refs[:n_in]
    row_ref = refs[n_in]
    outs = refs[n_in + 1 : 2 * n_in + 1]
    rows_ref = refs[2 * n_in + 1]
    (
        own,
        from_core,
        from_first,
        from_second,
        from_dp,
        load_sem,
        core_send,
        core_recv,
        first_send,
        first_recv,
        second_send,
        second_recv,
        dp_send,
        dp_recv,
        row_load,
        row_send,
        row_recv,
        row_dp_send,
        row_dp_recv,
    ) = refs[2 * n_in + 2 :]
    group = lax.axis_index("dp")
    head, core, xbit, ybit = position_bits()
    core_peer = head + 1 - 2 * core
    x_peer = head + 2 - 4 * xbit
    y_peer = head + 4 - 8 * ybit
    dp_peers = [lax.rem(group + hop, n_dp) for hop in range(1, n_dp)]

    barrier = pltpu.get_barrier_semaphore()
    for peer in (core_peer, x_peer, y_peer):
        pl.semaphore_signal(barrier, inc=1, device_id=(group, peer), device_id_type=MESH_ID)
    for peer in dp_peers:
        pl.semaphore_signal(barrier, inc=1, device_id=(peer, head), device_id_type=MESH_ID)
    pl.semaphore_wait(barrier, 3 + len(dp_peers))

    def term_part(unit, side):
        which, row, column = units[unit][:3]
        rows, columns = own.shape[4], own.shape[5]
        return terms[which].at[:, :, :, side, pl.ds(row, rows), pl.ds(column, columns)]

    def remote(source, target, send, receive, where):
        return pltpu.make_async_remote_copy(
            src_ref=source,
            dst_ref=target,
            send_sem=send,
            recv_sem=receive,
            device_id=where,
            device_id_type=MESH_ID,
        )

    def load(unit):
        return pltpu.make_async_copy(term_part(unit, core), own.at[unit], load_sem.at[unit])

    def core_copy(unit):
        return remote(
            term_part(unit, 1 - core),
            from_core.at[unit],
            core_send.at[unit],
            core_recv.at[unit],
            (group, core_peer),
        )

    def x_leads(unit):
        return units[unit][3] == 0

    def first_copy(unit):
        if x_leads(unit):
            source, peer = own.at[unit, :, :, 1 - xbit], x_peer
        else:
            source, peer = own.at[unit, :, 1 - ybit], y_peer
        return remote(
            source, from_first.at[unit], first_send.at[unit], first_recv.at[unit], (group, peer)
        )

    def second_copy(unit):
        if x_leads(unit):
            source, peer = own.at[unit, :, 1 - ybit, xbit], y_peer
        else:
            source, peer = own.at[unit, :, ybit, 1 - xbit], x_peer
        return remote(
            source, from_second.at[unit], second_send.at[unit], second_recv.at[unit], (group, peer)
        )

    def dp_copy(unit, hop):
        peer = dp_peers[hop]
        return remote(
            own.at[unit, peer, ybit, xbit],
            from_dp.at[unit, hop],
            dp_send.at[unit, hop],
            dp_recv.at[unit, hop],
            (peer, head),
        )

    def added(left, right):
        return (left.astype(jnp.float32) + right.astype(jnp.float32)).astype(jnp.bfloat16)

    def take_core(unit):
        load(unit).wait()
        core_copy(unit).wait()

        def body(index, _):
            at_dp = lax.div(index, 4)
            at_y = lax.rem(lax.div(index, 2), 2)
            at_x = lax.rem(index, 2)
            own[unit, at_dp, at_y, at_x] = added(
                own[unit, at_dp, at_y, at_x], from_core[unit, at_dp, at_y, at_x]
            )
            return 0

        lax.fori_loop(0, n_dp * 4, body, 0)
        first_copy(unit).start()

    def take_first(unit):
        first_copy(unit).wait()

        def body(index, _):
            at_dp = lax.div(index, 2)
            other = lax.rem(index, 2)
            at_y, at_x = (other, xbit) if x_leads(unit) else (ybit, other)
            own[unit, at_dp, at_y, at_x] = added(
                own[unit, at_dp, at_y, at_x], from_first[unit, at_dp, other]
            )
            return 0

        lax.fori_loop(0, n_dp * 2, body, 0)
        second_copy(unit).start()

    def take_second(unit):
        second_copy(unit).wait()

        def body(at_dp, _):
            own[unit, at_dp, ybit, xbit] = added(
                own[unit, at_dp, ybit, xbit], from_second[unit, at_dp]
            )
            return 0

        lax.fori_loop(0, n_dp, body, 0)
        for hop in range(n_dp - 1):
            dp_copy(unit, hop).start()

    def take_dp(unit):
        which, row, column = units[unit][:3]
        rows, columns = own.shape[4], own.shape[5]
        for hop in range(n_dp - 1):
            dp_copy(unit, hop).wait()
        total = own[unit, group, ybit, xbit].astype(jnp.float32)
        for hop in range(n_dp - 1):
            total = total + from_dp[unit, hop].astype(jnp.float32)
        outs[which][row : row + rows, column : column + columns] = total

    mine = rows_ref.at[group, ybit, xbit, core]
    row_copy = pltpu.make_async_copy(row_ref, mine, row_load)
    row_copy.start()
    row_copy.wait()
    row_dp = [
        remote(mine, mine, row_dp_send.at[hop], row_dp_recv.at[hop], (dp_peers[hop], head))
        for hop in range(n_dp - 1)
    ]
    for copy in row_dp:
        copy.start()
    y_part = rows_ref.at[:, ybit, xbit, core]
    x_part = rows_ref.at[:, :, xbit, core]
    core_part = rows_ref.at[:, :, :, core]
    row_y = remote(y_part, y_part, row_send.at[0], row_recv.at[0], (group, y_peer))
    row_x = remote(x_part, x_part, row_send.at[1], row_recv.at[1], (group, x_peer))
    row_core = remote(core_part, core_part, row_send.at[2], row_recv.at[2], (group, core_peer))

    count = len(units)
    for unit in range(count):
        core_copy(unit).start()
        load(unit).start()
    for step in range(count + 3):
        if step < count:
            take_core(step)
        if 0 <= step - 1 < count:
            take_first(step - 1)
        if 0 <= step - 2 < count:
            take_second(step - 2)
        if 0 <= step - 3:
            take_dp(step - 3)
        if step == 1:
            for copy in row_dp:
                copy.wait()
            row_y.start()
        if step == 3:
            row_y.wait()
            row_x.start()
        if step == 5:
            row_x.wait()
            row_core.start()
        if step == 7:
            row_core.wait()


def scatter_sums(n_dp, terms, factors):
    devices = n_dp * 8
    rows = min(term.shape[0] for term in terms) // devices
    columns = min(term.shape[1] for term in terms)
    units = []
    for which, term in enumerate(terms):
        for row in range(0, term.shape[0] // devices, rows):
            for column in range(0, term.shape[1], columns):
                units.append((which, row, column, len(units) % 2))
    count = len(units)
    views = [
        term.reshape(n_dp, 2, 2, 2, term.shape[0] // devices, term.shape[1]) for term in terms
    ]
    out_shapes = [
        jax.ShapeDtypeStruct((term.shape[0] // devices, term.shape[1]), jnp.float32)
        for term in terms
    ]
    dma = pltpu.SemaphoreType.DMA
    results = pl.pallas_call(
        lambda *refs: scatter_kernel(n_dp, units, *refs),
        out_shape=(*out_shapes, jax.ShapeDtypeStruct((n_dp, 2, 2, 2, *factors.shape), factors.dtype)),
        in_specs=[IN_PLACE] * (len(terms) + 1),
        out_specs=tuple([IN_VMEM] * (len(terms) + 1)),
        scratch_shapes=[
            pltpu.VMEM((count, n_dp, 2, 2, rows, columns), jnp.bfloat16),
            pltpu.VMEM((count, n_dp, 2, 2, rows, columns), jnp.bfloat16),
            pltpu.VMEM((count, n_dp, 2, rows, columns), jnp.bfloat16),
            pltpu.VMEM((count, n_dp, rows, columns), jnp.bfloat16),
            pltpu.VMEM((count, n_dp - 1, rows, columns), jnp.bfloat16),
            dma((count,)),
            dma((count,)),
            dma((count,)),
            dma((count,)),
            dma((count,)),
            dma((count,)),
            dma((count,)),
            dma((count, n_dp - 1)),
            dma((count, n_dp - 1)),
            dma,
            dma((3,)),
            dma((3,)),
            dma((n_dp - 1,)),
            dma((n_dp - 1,)),
        ],
        compiler_params=pltpu.CompilerParams(
            collective_id=0, has_side_effects=True, vmem_limit_bytes=60 * 1024 * 1024
        ),
        name="scatter_sums",
    )(*views, factors)
    return results[:-1], results[-1]


def per_device(
    hidden_in,
    frame_cond,
    query_weight,
    key_weight,
    value_weight,
    output_weight,
    up_weight,
    down_weight,
    modulation_weight,
    clip_lengths,
    patch_valid,
    cotangent,
):
    tok_dev, model_width = hidden_in.shape
    frames_dev = frame_cond.shape[0]
    group_tokens = patch_valid.shape[0]
    head_index = lax.axis_index("head")
    clip_of, frame_of, position = group_layout(clip_lengths[0], group_tokens, PATCHES)
    local_start = head_index * tok_dev
    local_position = lax.dynamic_slice_in_dim(position, local_start, tok_dev)
    local_valid = (
        lax.dynamic_slice_in_dim(patch_valid, local_start, tok_dev)
        .astype(jnp.float32)
        .reshape(frames_dev, PATCHES)
    )
    angles = local_position.astype(jnp.float32)[:, None] * frequencies(HEAD_DIM // 2)[None, :]
    cond_value = frame_cond.astype(jnp.float32)
    cond_act = jax.nn.silu(cond_value).astype(jnp.bfloat16)
    modulation = jnp.dot(cond_act, modulation_weight, preferred_element_type=jnp.float32).reshape(
        frames_dev, 1, 6 * model_width
    )
    shift_one, scale_one, gate_one, shift_two, scale_two, gate_two = jnp.split(
        modulation, 6, axis=2
    )
    tokens = hidden_in.astype(jnp.float32).reshape(frames_dev, PATCHES, model_width)
    normed_one = (
        modulate(tokens, shift_one, scale_one).astype(jnp.bfloat16).reshape(tok_dev, model_width)
    )
    query_raw = jnp.dot(normed_one, query_weight, preferred_element_type=jnp.float32)
    key_raw = jnp.dot(normed_one, key_weight, preferred_element_type=jnp.float32)
    query_send = (
        rotate(query_raw.reshape(tok_dev, HEADS, HEAD_DIM), angles)
        .reshape(tok_dev, model_width)
        .astype(jnp.bfloat16)
    )
    key_send = (
        rotate(key_raw.reshape(tok_dev, HEADS, HEAD_DIM), angles)
        .reshape(tok_dev, model_width)
        .astype(jnp.bfloat16)
    )
    value_send = jnp.dot(normed_one, value_weight, preferred_element_type=jnp.float32).astype(
        jnp.bfloat16
    )
    head_query, head_key, head_value = (
        lax.all_to_all(query_send, "head", split_axis=1, concat_axis=0, tiled=True),
        lax.all_to_all(key_send, "head", split_axis=1, concat_axis=0, tiled=True),
        lax.all_to_all(value_send, "head", split_axis=1, concat_axis=0, tiled=True),
    )
    first_frames = (frame_of - position)[::PATCHES]
    bias = jnp.broadcast_to(
        jnp.where(patch_valid == 1, 0.0, MASKED).astype(jnp.float32)[:, None],
        (group_tokens, 128),
    )
    attended_send, logsum = attend_forward(first_frames, head_query, head_key, head_value, bias)
    frame_attended = lax.all_to_all(attended_send, "head", split_axis=0, concat_axis=1, tiled=True)
    branch_attn = jnp.dot(
        frame_attended, output_weight, preferred_element_type=jnp.float32
    ).reshape(frames_dev, PATCHES, model_width)
    middle = tokens + gate_one * branch_attn
    normed_two = (
        modulate(middle, shift_two, scale_two).astype(jnp.bfloat16).reshape(tok_dev, model_width)
    )
    hidden = jnp.dot(normed_two, up_weight, preferred_element_type=jnp.float32)
    active = jax.nn.gelu(hidden).astype(jnp.bfloat16)
    branch_mlp = jnp.dot(active, down_weight, preferred_element_type=jnp.float32).reshape(
        frames_dev, PATCHES, model_width
    )
    result = middle + gate_two * branch_mlp
    statistics = jnp.stack(
        [
            frame_stats(gate_one * branch_attn, local_valid),
            frame_stats(gate_two * branch_mlp, local_valid),
            frame_stats(result, local_valid),
        ],
        axis=1,
    )
    out_grad = cotangent.astype(jnp.float32).reshape(frames_dev, PATCHES, model_width)
    gate_two_grad = jnp.sum(out_grad * branch_mlp, axis=1, keepdims=True)
    mlp_grad = (gate_two * out_grad).reshape(tok_dev, model_width).astype(jnp.bfloat16)
    down_term = inner_rows(active, mlp_grad)
    active_grad = times_transposed(mlp_grad, down_weight)
    hidden_grad = jax.vjp(jax.nn.gelu, hidden)[1](active_grad)[0].astype(jnp.bfloat16)
    up_term = inner_rows(normed_two, hidden_grad)
    normed_two_grad = times_transposed(hidden_grad, up_weight).reshape(
        frames_dev, PATCHES, model_width
    )
    middle_part, shift_two_grad, scale_two_grad = jax.vjp(modulate, middle, shift_two, scale_two)[
        1
    ](normed_two_grad)
    middle_grad = out_grad + middle_part
    gate_one_grad = jnp.sum(middle_grad * branch_attn, axis=1, keepdims=True)
    attn_grad = (gate_one * middle_grad).reshape(tok_dev, model_width).astype(jnp.bfloat16)
    output_term = inner_rows(frame_attended, attn_grad)
    attended_grad = times_transposed(attn_grad, output_weight).astype(jnp.bfloat16)
    head_grad = lax.all_to_all(attended_grad, "head", split_axis=1, concat_axis=0, tiled=True)
    query_grad, key_grad, value_grad = attend_backward(
        first_frames, head_query, head_key, head_value, attended_send, head_grad, bias, logsum
    )
    back_query, back_key, back_value = (
        lax.all_to_all(
            query_grad,
            "head",
            split_axis=0,
            concat_axis=1,
            tiled=True,
        ),
        lax.all_to_all(
            key_grad,
            "head",
            split_axis=0,
            concat_axis=1,
            tiled=True,
        ),
        lax.all_to_all(
            value_grad,
            "head",
            split_axis=0,
            concat_axis=1,
            tiled=True,
        ),
    )
    query_raw_grad = (
        rotate(back_query.astype(jnp.float32).reshape(tok_dev, HEADS, HEAD_DIM), -angles)
        .reshape(tok_dev, model_width)
        .astype(jnp.bfloat16)
    )
    key_raw_grad = (
        rotate(back_key.astype(jnp.float32).reshape(tok_dev, HEADS, HEAD_DIM), -angles)
        .reshape(tok_dev, model_width)
        .astype(jnp.bfloat16)
    )
    query_term = inner_rows(normed_one, query_raw_grad)
    key_term = inner_rows(normed_one, key_raw_grad)
    value_term = inner_rows(normed_one, back_value)
    normed_one_grad = (
        times_transposed(query_raw_grad, query_weight)
        + times_transposed(key_raw_grad, key_weight)
        + times_transposed(back_value, value_weight)
    )
    token_part, shift_one_grad, scale_one_grad = jax.vjp(modulate, tokens, shift_one, scale_one)[1](
        normed_one_grad.reshape(frames_dev, PATCHES, model_width)
    )
    grad_input = (middle_grad + token_part).reshape(tok_dev, model_width)
    modulation_grad = (
        jnp.concatenate(
            [
                shift_one_grad,
                scale_one_grad,
                gate_one_grad,
                shift_two_grad,
                scale_two_grad,
                gate_two_grad,
            ],
            axis=2,
        )
        .reshape(frames_dev, 6 * model_width)
        .astype(jnp.bfloat16)
    )
    cond_act_grad = times_transposed(modulation_grad, modulation_weight)
    grad_cond = jax.vjp(jax.nn.silu, cond_value)[1](cond_act_grad)[0]
    n_dp = lax.axis_size("dp")
    factors = jnp.concatenate([cond_act, modulation_grad], axis=1).reshape(-1, 128)
    terms = [query_term, key_term, value_term, output_term, up_term, down_term]
    grad_sums, gathered = scatter_sums(
        n_dp, [term.astype(jnp.bfloat16) for term in terms], factors
    )
    device = lax.axis_index("dp") * lax.axis_size("head") + head_index
    gathered = gathered.reshape(n_dp * 8 * frames_dev, 7 * model_width)
    share = model_width // (n_dp * 8)
    grad_modulation = inner_rows(
        lax.dynamic_slice_in_dim(gathered, device * share, share, 1), gathered[:, model_width:]
    )
    return (
        result.reshape(tok_dev, model_width).astype(jnp.bfloat16),
        grad_input,
        grad_cond,
        grad_sums[0],
        grad_sums[1],
        grad_sums[2],
        grad_sums[3],
        grad_sums[4],
        grad_sums[5],
        grad_modulation,
        statistics,
    )


def solution(mesh):
    in_specs = (
        P(("dp", "head"), None),
        P(("dp", "head"), None),
        P(),
        P(),
        P(),
        P(),
        P(),
        P(),
        P(),
        P("dp", None),
        P("dp"),
        P(("dp", "head"), None),
    )
    out_specs = (
        P(("dp", "head"), None),
        P(("dp", "head"), None),
        P(("dp", "head"), None),
        P(("dp", "head"), None),
        P(("dp", "head"), None),
        P(("dp", "head"), None),
        P(("dp", "head"), None),
        P(("dp", "head"), None),
        P(("dp", "head"), None),
        P(("dp", "head"), None),
        P(("dp", "head"), None),
    )
    return jax.shard_map(
        per_device, mesh=mesh, in_specs=in_specs, out_specs=out_specs, check_vma=False
    )
```

```python
import math

import jax
import jax.numpy as jnp
from jax import lax
from jax.experimental import pallas as pl
from jax.experimental.pallas import tpu as pltpu
from jax.sharding import PartitionSpec as P

HEADS = 16
HEAD_DIM = 64
PATCHES = 256


EPSILON = 1e-06
MASKED = -1e30


def rms_normed(values):
    return values * lax.rsqrt(jnp.mean(values * values, axis=-1, keepdims=True) + EPSILON)


def modulate(values, shift, scaling):
    return rms_normed(values) * (1.0 + scaling) + shift


def frequencies(half_dim):
    return jnp.exp(jnp.arange(half_dim, dtype=jnp.float32) * (-math.log(10000.0) / half_dim))


def rotate(values, angles):
    half_dim = values.shape[-1] // 2
    cosine = jnp.cos(angles)[:, None, :]
    sine_part = jnp.sin(angles)[:, None, :]
    first_half = values[..., :half_dim]
    second = values[..., half_dim:]
    return jnp.concatenate(
        [first_half * cosine - second * sine_part, first_half * sine_part + second * cosine],
        axis=-1,
    )


def group_layout(lengths, token_count, patches):
    frame_of = jnp.arange(token_count, dtype=jnp.int32) // patches
    clip_ends = jnp.cumsum(lengths)
    starts = clip_ends - lengths
    clip_of = jnp.sum((frame_of[:, None] >= clip_ends[None, :]).astype(jnp.int32), axis=1)
    picked = clip_of[:, None] == jnp.arange(lengths.shape[0], dtype=jnp.int32)[None, :]
    position = frame_of - jnp.sum(jnp.where(picked, starts[None, :], 0), axis=1)
    return (clip_of, frame_of, position)


def inner_rows(left, right):
    return lax.dot_general(
        left, right, (((0,), (0,)), ((), ())), preferred_element_type=jnp.float32
    )


def times_transposed(left, right):
    return lax.dot_general(
        left, right, (((1,), (1,)), ((), ())), preferred_element_type=jnp.float32
    )


def frame_stats(values, valid_f):
    sums = jnp.sum(values * values, axis=2) * valid_f
    return jnp.sqrt(jnp.sum(sums, axis=1) / (values.shape[1] * values.shape[2]) + EPSILON)


def dot_nt(left, right):
    return lax.dot_general(
        left, right, (((1,), (1,)), ((), ())), preferred_element_type=jnp.float32
    )


def dot_nn(left, right):
    return lax.dot_general(
        left, right, (((1,), (0,)), ((), ())), preferred_element_type=jnp.float32
    )


def head_parts(block):
    lane = lax.broadcasted_iota(jnp.int32, block.shape, 1)
    zero = jnp.zeros_like(block)
    return jnp.where(lane < HEAD_DIM, block, zero), jnp.where(lane < HEAD_DIM, zero, block)


def key_bias(bias_ref, key_frame, frame):
    half = bias_ref[pl.ds(key_frame * PATCHES, PATCHES), :]
    bias = jnp.concatenate([half, half], axis=1)
    row = lax.broadcasted_iota(jnp.int32, bias.shape, 0)
    column = lax.broadcasted_iota(jnp.int32, bias.shape, 1)
    own = (row == column) & (key_frame == frame)
    return jnp.where(own, 0.0, bias)


def attend_forward_kernel(first_ref, q_ref, k_ref, v_ref, bias_ref, o_ref, lse_ref, scores):
    frames = q_ref.shape[0] // PATCHES

    def one_frame(frame, _):
        rows = pl.ds(frame * PATCHES, PATCHES)
        parts = head_parts(q_ref[rows, :] * jnp.bfloat16(0.125))
        first = first_ref[frame]

        def score(key_frame, tops):
            keys = k_ref[pl.ds(key_frame * PATCHES, PATCHES), :]
            bias = key_bias(bias_ref, key_frame, frame)
            new = []
            for head in range(2):
                value = dot_nt(keys, parts[head]) + bias
                scores[head, key_frame - first] = value
                new.append(jnp.maximum(tops[head], jnp.max(value, axis=0, keepdims=True)))
            return tuple(new)

        low = jnp.full((1, PATCHES), MASKED, jnp.float32)
        tops = lax.fori_loop(first, frame + 1, score, (low, low))

        def exponent(key_frame, totals):
            new = []
            for head in range(2):
                value = jnp.exp(scores[head, key_frame - first] - tops[head])
                scores[head, key_frame - first] = value
                new.append(totals[head] + jnp.sum(value, axis=0, keepdims=True))
            return tuple(new)

        zero = jnp.zeros((1, PATCHES), jnp.float32)
        totals = lax.fori_loop(first, frame + 1, exponent, (zero, zero))
        inverse = [1.0 / total for total in totals]

        def weigh(key_frame, sums):
            turned = v_ref[pl.ds(key_frame * PATCHES, PATCHES), :].T
            new = []
            for head in range(2):
                probs = (scores[head, key_frame - first] * inverse[head]).astype(jnp.bfloat16)
                new.append(
                    sums[head]
                    + dot_nn(turned[head * HEAD_DIM : (head + 1) * HEAD_DIM, :], probs)
                )
            return tuple(new)

        empty = jnp.zeros((HEAD_DIM, PATCHES), jnp.float32)
        sums = lax.fori_loop(first, frame + 1, weigh, (empty, empty))
        o_ref[rows, :] = jnp.concatenate(sums, axis=0).T.astype(jnp.bfloat16)
        for head in range(2):
            lse_ref[frame, head : head + 1, :] = tops[head] + jnp.log(totals[head])
        return 0

    lax.fori_loop(0, frames, one_frame, 0)


IN_SMEM = pl.BlockSpec(memory_space=pltpu.SMEM)
IN_VMEM = pl.BlockSpec(memory_space=pltpu.VMEM)
IN_PLACE = pl.BlockSpec(memory_space=pl.ANY)
MESH_ID = pl.DeviceIdType.MESH


def attend_forward(first, queries, keys, values, bias):
    tokens, width = queries.shape
    frames = tokens // PATCHES
    return pl.pallas_call(
        attend_forward_kernel,
        out_shape=(
            jax.ShapeDtypeStruct((tokens, width), jnp.bfloat16),
            jax.ShapeDtypeStruct((frames, 2, PATCHES), jnp.float32),
        ),
        in_specs=[IN_SMEM] + [IN_VMEM] * 4,
        out_specs=(IN_VMEM, IN_VMEM),
        scratch_shapes=[pltpu.VMEM((2, 4, PATCHES, PATCHES), jnp.float32)],
        name="attend_forward",
    )(first, queries, keys, values, bias)


SLOTS = 17
BLOCK = 256


def peer_head(head, flips):
    core = lax.rem(head, 2)
    second = lax.rem(lax.div(head, 2), 2)
    third = lax.div(head, 4)
    if flips % 2:
        core = 1 - core
    if flips // 2 % 2:
        second = 1 - second
    if flips // 4:
        third = 1 - third
    return 4 * third + 2 * second + core


def remote(source, target, send, receive, where):
    return pltpu.make_async_remote_copy(
        src_ref=source,
        dst_ref=target,
        send_sem=send,
        recv_sem=receive,
        device_id=where,
        device_id_type=MESH_ID,
    )


def gelu_and_slope(value):
    square = value * value
    inner = 0.7978845608028654 * value * (1.0 + 0.044715 * square)
    bend = jnp.tanh(inner)
    half = 0.5 * (1.0 + bend)
    slope = half + 0.5 * value * (1.0 - bend * bend) * (
        0.7978845608028654 * (1.0 + 0.134145 * square)
    )
    return value * half, slope


def turn_pairs(values, column):
    lane = lax.rem(lax.broadcasted_iota(jnp.int32, values.shape, 1), HEAD_DIM)
    up = pltpu.roll(values, 128 - HEAD_DIM // 2, 1)
    down = pltpu.roll(values, HEAD_DIM // 2, 1)
    return jnp.where(lane < HEAD_DIM // 2, up, down)


def back_kernel(n_dp, *refs):
    (
        table,
        att_own,
        q_ref,
        k_ref,
        v_ref,
        lse_ref,
        bias_ref,
        x_ref,
        cot_ref,
        n1_ref,
        mod_ref,
        cond_ref,
        valid_ref,
        wo_hbm,
        up_hbm,
        down_hbm,
        wq_hbm,
        wk_hbm,
        wv_hbm,
        block_ref,
        gin_ref,
        stat_ref,
        gq_ref,
        gk_ref,
        gv_ref,
        go_ref,
        gup_ref,
        gdown_ref,
        rows_ref,
        att_fr,
        do_own,
        back,
        from_core,
        from_first,
        from_second,
        from_dp,
        core_out,
        da_send,
        lhs,
        n2,
        dmlp,
        dhid,
        dattn,
        ba,
        mid,
        wo,
        load_sem,
        a2a_send,
        a2a_recv,
        core_send,
        core_recv,
        first_send,
        first_recv,
        second_send,
        second_recv,
        dp_send,
        dp_recv,
        row_send,
        row_recv,
        row_dp_send,
        row_dp_recv,
    ) = refs
    tokens, width = x_ref.shape
    frames = q_ref.shape[0]
    hidden_width = up_hbm.shape[1]
    tiles = hidden_width // width
    chunks = width // BLOCK
    small = width // (n_dp * 8)
    large = hidden_width // (n_dp * 8)
    half_rows = n_dp * 4 * small
    group = lax.axis_index("dp")
    head = lax.axis_index("head")
    core = lax.rem(head, 2)
    xbit = lax.rem(lax.div(head, 2), 2)
    ybit = lax.div(head, 4)
    core_peer, x_peer, y_peer = peer_head(head, 1), peer_head(head, 2), peer_head(head, 4)
    dp_peers = [lax.rem(group + hop, n_dp) for hop in range(1, n_dp)]
    others = range(1, 8)

    barrier = pltpu.get_barrier_semaphore()
    for flips in others:
        pl.semaphore_signal(
            barrier, inc=1, device_id=(group, peer_head(head, flips)), device_id_type=MESH_ID
        )
    for peer in dp_peers:
        pl.semaphore_signal(barrier, inc=1, device_id=(peer, head), device_id_type=MESH_ID)

    wo_load = pltpu.make_async_copy(wo_hbm, wo, load_sem.at[0])
    wo_load.start()
    pl.semaphore_wait(barrier, 7 + len(dp_peers))

    own_rows = pl.ds(head * tokens, tokens)
    own_lanes = pl.ds(head * 128, 128)

    def att_copy(flips):
        peer = peer_head(head, flips)
        return remote(
            att_own.at[pl.ds(peer * tokens, tokens), :],
            att_fr.at[:, own_lanes],
            a2a_send.at[0, flips],
            a2a_recv.at[0, flips],
            (group, peer),
        )

    def grad_copy(flips):
        peer = peer_head(head, flips)
        return remote(
            da_send.at[:, pl.ds(peer * 128, 128)],
            do_own.at[head],
            a2a_send.at[1, flips],
            a2a_recv.at[1, flips],
            (group, peer),
        )

    first_up = large // small
    first_out = first_up + tiles
    count = first_out + 4

    def slot_of(unit):
        return unit if unit < first_out + 1 else unit - first_out - 1

    def lhs_of(unit):
        if unit < first_up:
            return unit
        if unit < first_out:
            return first_up
        return first_up + 1 if unit == first_out else first_up + 2

    def core_copy(unit):
        return remote(
            core_out.at[unit % 2],
            from_core.at[slot_of(unit)],
            core_send.at[unit],
            core_recv.at[unit],
            (group, core_peer),
        )

    def x_leads(unit):
        return unit % 2 == 0

    def first_copy(unit):
        slot = slot_of(unit)
        if x_leads(unit):
            source, peer = from_core.at[slot, :, :, 1 - xbit], x_peer
        else:
            source, peer = from_core.at[slot, :, 1 - ybit], y_peer
        return remote(
            source, from_first.at[slot], first_send.at[unit], first_recv.at[unit], (group, peer)
        )

    def second_copy(unit):
        slot = slot_of(unit)
        if x_leads(unit):
            source, peer = from_core.at[slot, :, 1 - ybit, xbit], y_peer
        else:
            source, peer = from_core.at[slot, :, ybit, 1 - xbit], x_peer
        return remote(
            source, from_second.at[slot], second_send.at[unit], second_recv.at[unit], (group, peer)
        )

    def dp_copy(unit, hop):
        peer = dp_peers[hop]
        return remote(
            from_core.at[slot_of(unit), peer, ybit, xbit],
            from_dp.at[unit, hop],
            dp_send.at[unit, hop],
            dp_recv.at[unit, hop],
            (peer, head),
        )

    def added(left, right):
        return (left.astype(jnp.float32) + right.astype(jnp.float32)).astype(jnp.bfloat16)

    def produce(unit, right):
        if unit >= 2:
            core_copy(unit - 2).wait_send()
        left = lhs_of(unit)

        def body(chunk, _):
            lanes = pl.ds(pl.multiple_of(chunk * BLOCK, BLOCK), BLOCK)
            value = dot_nn(lhs[left, 1 - core], right(chunk)).astype(jnp.bfloat16)
            core_out[unit % 2, :, :, :, :, lanes] = value.reshape(n_dp, 2, 2, small, BLOCK)
            return 0

        lax.fori_loop(0, chunks, body, 0)
        core_copy(unit).start()

    def take_core(unit, right):
        core_copy(unit).wait_recv()
        left, slot = lhs_of(unit), slot_of(unit)

        def body(chunk, _):
            lanes = pl.ds(pl.multiple_of(chunk * BLOCK, BLOCK), BLOCK)
            value = dot_nn(lhs[left, core], right(chunk))
            came = from_core[slot, :, :, :, :, lanes].reshape(half_rows, BLOCK)
            value = (value + came.astype(jnp.float32)).astype(jnp.bfloat16)
            from_core[slot, :, :, :, :, lanes] = value.reshape(n_dp, 2, 2, small, BLOCK)
            return 0

        lax.fori_loop(0, chunks, body, 0)
        first_copy(unit).start()

    def take_first(unit):
        first_copy(unit).wait()
        slot = slot_of(unit)

        def body(index, _):
            at_dp = lax.div(index, 2)
            other = lax.rem(index, 2)
            at_y, at_x = (other, xbit) if x_leads(unit) else (ybit, other)
            from_core[slot, at_dp, at_y, at_x] = added(
                from_core[slot, at_dp, at_y, at_x], from_first[slot, at_dp, other]
            )
            return 0

        lax.fori_loop(0, n_dp * 2, body, 0)
        second_copy(unit).start()

    def take_second(unit):
        second_copy(unit).wait()
        slot = slot_of(unit)

        def body(at_dp, _):
            from_core[slot, at_dp, ybit, xbit] = added(
                from_core[slot, at_dp, ybit, xbit], from_second[slot, at_dp]
            )
            return 0

        lax.fori_loop(0, n_dp, body, 0)
        for hop in range(n_dp - 1):
            dp_copy(unit, hop).start()

    def take_dp(unit):
        for hop in range(n_dp - 1):
            dp_copy(unit, hop).wait()
        total = from_core[slot_of(unit), group, ybit, xbit].astype(jnp.float32)
        for hop in range(n_dp - 1):
            total = total + from_dp[unit, hop].astype(jnp.float32)
        if unit < first_up:
            gdown_ref[unit * small : (unit + 1) * small, :] = total
        elif unit < first_out:
            place = (unit - first_up) * width
            gup_ref[:, place : place + width] = total
        else:
            (go_ref, gv_ref, gq_ref, gk_ref)[unit - first_out][...] = total

    def turned_rows(index, source):
        for chunk in range(chunks):
            value = source[:, chunk * BLOCK : (chunk + 1) * BLOCK].T
            value = value.reshape(BLOCK // (2 * small), 2, small, tokens)
            for side in range(2):
                lhs[index, side, chunk * BLOCK // 2 : (chunk + 1) * BLOCK // 2, :] = value[
                    :, side
                ].reshape(BLOCK // 2, tokens)

    shift_one, scale_one, gate_one = (mod_ref[row : row + 1, :] for row in range(3))
    shift_two, scale_two, gate_two = (mod_ref[row : row + 1, :] for row in range(3, 6))
    step_rows = 32
    steps = tokens // step_rows

    def row_block(index):
        return pl.ds(pl.multiple_of(index * step_rows, step_rows), step_rows)

    def lane_block(chunk):
        return pl.ds(pl.multiple_of(chunk * BLOCK, BLOCK), BLOCK)

    def masked_square(values, rows):
        sums = jnp.sum(values * values, axis=1, keepdims=True) * valid_ref[rows, :1]
        return jnp.sum(sums, axis=0, keepdims=True)

    one = jnp.zeros((1, 1), jnp.float32)
    row_zero = jnp.zeros((1, width), jnp.float32)

    for flips in others:
        att_copy(flips).start()
    att_fr[:, own_lanes] = att_own[own_rows, :]

    def down_right(chunk):
        return dmlp[:, lane_block(chunk)]

    def up_right(unit):
        def value(chunk):
            start = (unit - first_up) * width + chunk * BLOCK
            return dhid[:, pl.ds(pl.multiple_of(start, BLOCK), BLOCK)]

        return value

    def mlp_right(unit):
        return down_right if unit < first_up else up_right(unit)

    def out_right(chunk):
        return dattn[:, lane_block(chunk)]

    def mlp_part(up, down, act, dn2):
        up_loads = [
            pltpu.make_async_copy(
                up_hbm.at[:, pl.ds(tile * width, width)],
                up.at[:, pl.ds(tile * width, width)],
                load_sem.at[1 + tile],
            )
            for tile in range(tiles)
        ]
        down_loads = [
            pltpu.make_async_copy(
                down_hbm.at[pl.ds(tile * width, width), :],
                down.at[pl.ds(tile * width, width), :],
                load_sem.at[1 + tiles + tile],
            )
            for tile in range(tiles)
        ]
        for tile in range(tiles):
            up_loads[tile].start()
            down_loads[tile].start()

        turned_rows(first_up + 2, n1_ref)
        wo_load.wait()
        for flips in others:
            att_copy(flips).wait()
        turned_rows(first_up + 1, att_fr)

        def project(chunk, _):
            lanes = lane_block(chunk)
            ba[:, lanes] = dot_nn(att_fr[...], wo[:, lanes])
            return 0

        lax.fori_loop(0, chunks, project, 0)

        def second_norm(index, total):
            rows = row_block(index)
            branch = gate_one * ba[rows, :]
            value = x_ref[rows, :].astype(jnp.float32) + branch
            mid[rows, :] = value
            scale = lax.rsqrt(jnp.mean(value * value, axis=1, keepdims=True) + EPSILON)
            n2[rows, :] = (value * scale * (1.0 + scale_two) + shift_two).astype(jnp.bfloat16)
            dmlp[rows, :] = (gate_two * cot_ref[rows, :].astype(jnp.float32)).astype(jnp.bfloat16)
            return total + masked_square(branch, rows)

        stat_attn = lax.fori_loop(0, steps, second_norm, one)
        turned_rows(first_up, n2)

        pairs = BLOCK // (2 * large)

        def feed(index, _):
            @pl.when(lax.rem(index, chunks) == 0)
            def _():
                tile = lax.div(index, chunks)
                pltpu.make_async_copy(
                    up_hbm.at[:, pl.ds(0, width)],
                    up.at[:, pl.ds(0, width)],
                    load_sem.at[1 + tile],
                ).wait()
                pltpu.make_async_copy(
                    down_hbm.at[pl.ds(0, width), :],
                    down.at[pl.ds(0, width), :],
                    load_sem.at[1 + tiles + tile],
                ).wait()

            lanes = lane_block(index)
            active, slope = gelu_and_slope(dot_nn(n2[...], up[:, lanes]))
            active = active.astype(jnp.bfloat16)
            act[:, lanes] = active
            grad = dot_nt(dmlp[...], down[lanes, :])
            dhid[:, lanes] = (grad * slope).astype(jnp.bfloat16)
            turned = active.T.reshape(pairs, 2, first_up, small, tokens)
            where = pl.ds(pl.multiple_of(index * pairs * small, pairs * small), pairs * small)
            for unit in range(first_up):
                for side in range(2):
                    lhs[unit, side, where, :] = turned[:, side, unit].reshape(
                        pairs * small, tokens
                    )
            return 0

        lax.fori_loop(0, hidden_width // BLOCK, feed, 0)

        produce(0, mlp_right(0))
        produce(1, mlp_right(1))

        def to_normed(chunk, _):
            lanes = lane_block(chunk)
            dn2[:, lanes] = dot_nt(dhid[...], up[lanes, :])
            return 0

        lax.fori_loop(0, chunks, to_normed, 0)
        take_core(0, mlp_right(0))
        take_core(1, mlp_right(1))

        def second_norm_back(index, sums):
            shift_sum, scale_sum, gate_sum = sums
            rows = row_block(index)
            value = mid[rows, :]
            scale = lax.rsqrt(jnp.mean(value * value, axis=1, keepdims=True) + EPSILON)
            normed = value * scale
            grad = dn2[rows, :]
            shift_sum = shift_sum + jnp.sum(grad, axis=0, keepdims=True)
            scale_sum = scale_sum + jnp.sum(grad * normed, axis=0, keepdims=True)
            inner = grad * (1.0 + scale_two)
            mean = jnp.mean(inner * normed, axis=1, keepdims=True)
            total = cot_ref[rows, :].astype(jnp.float32) + scale * (inner - normed * mean)
            dn2[rows, :] = total
            gate_sum = gate_sum + jnp.sum(total * ba[rows, :], axis=0, keepdims=True)
            dattn[rows, :] = (gate_one * total).astype(jnp.bfloat16)
            return shift_sum, scale_sum, gate_sum

        shift_two_grad, scale_two_grad, gate_one_grad = lax.fori_loop(
            0, steps, second_norm_back, (row_zero, row_zero, row_zero)
        )

        def to_attended(chunk, _):
            lanes = lane_block(chunk)
            da_send[:, lanes] = dot_nt(dattn[...], wo[lanes, :]).astype(jnp.bfloat16)
            return 0

        lax.fori_loop(0, chunks, to_attended, 0)
        for flips in others:
            grad_copy(flips).start()
        do_own[head] = da_send[:, own_lanes]

        produce(2, mlp_right(2))
        produce(3, mlp_right(3))

        def branch_out(chunk, _):
            lanes = lane_block(chunk)
            ba[:, lanes] = dot_nn(act[...], down[:, lanes])
            return 0

        lax.fori_loop(0, chunks, branch_out, 0)
        take_core(2, mlp_right(2))
        take_core(3, mlp_right(3))

        def outputs(index, sums):
            gate_sum, stat_mlp, stat_out = sums
            rows = row_block(index)
            raw = ba[rows, :]
            branch = gate_two * raw
            value = mid[rows, :] + branch
            block_ref[rows, :] = value.astype(jnp.bfloat16)
            gate_sum = gate_sum + jnp.sum(
                cot_ref[rows, :].astype(jnp.float32) * raw, axis=0, keepdims=True
            )
            stat_mlp = stat_mlp + masked_square(branch, rows)
            stat_out = stat_out + masked_square(value, rows)
            mid[rows, :] = dn2[rows, :]
            return gate_sum, stat_mlp, stat_out

        gate_two_grad, stat_mlp, stat_out = lax.fori_loop(0, steps, outputs, (row_zero, one, one))
        lane = lax.broadcasted_iota(jnp.int32, stat_ref.shape, 1)
        stats = jnp.where(lane == 0, stat_attn, jnp.where(lane == 1, stat_mlp, stat_out))
        stat_ref[...] = jnp.sqrt(stats / (tokens * width) + EPSILON)
        for row, vector in (
            (3, gate_one_grad),
            (4, shift_two_grad),
            (5, scale_two_grad),
            (6, gate_two_grad),
        ):
            gin_ref[row : row + 1, :] = vector
        produce(4, mlp_right(4))
        produce(5, mlp_right(5))

    pl.run_scoped(
        mlp_part,
        pltpu.VMEM((width, hidden_width), jnp.bfloat16),
        pltpu.VMEM((hidden_width, width), jnp.bfloat16),
        pltpu.VMEM((tokens, hidden_width), jnp.bfloat16),
        pltpu.VMEM((tokens, width), jnp.float32),
    )
    saved_rows = [gin_ref[row : row + 1, :] for row in range(3, 7)]

    def attention_part(wqkv, dq_slots, dk_slots, dv_slots, qkv_send, dq_raw, dk_raw, deltas):
        qkv_loads = [
            pltpu.make_async_copy(source, wqkv.at[place], load_sem.at[1 + 2 * tiles + place])
            for place, source in enumerate((wq_hbm, wk_hbm, wv_hbm))
        ]
        for copy in qkv_loads:
            copy.start()
        take_first(0)
        take_first(1)
        for flips in others:
            grad_copy(flips).wait()
        for slots in (dq_slots, dk_slots, dv_slots):
            slots[SLOTS] = jnp.zeros(slots.shape[1:], jnp.float32)

        def frame_delta(frame, _):
            rows = pl.ds(pl.multiple_of(frame * tokens, tokens), tokens)
            product = (
                do_own[frame].astype(jnp.float32) * att_own[rows, :].astype(jnp.float32)
            ).T
            for part in range(2):
                deltas[frame, part : part + 1, :] = jnp.sum(
                    product[part * HEAD_DIM : (part + 1) * HEAD_DIM, :], axis=0, keepdims=True
                )
            return 0

        lax.fori_loop(0, frames, frame_delta, 0)

        side_work = {
            1: lambda: take_core(4, mlp_right(4)),
            2: lambda: take_core(5, mlp_right(5)),
            3: lambda: produce(6, mlp_right(6)),
            4: lambda: take_second(0),
            5: lambda: take_second(1),
            6: lambda: take_first(2),
            7: lambda: take_first(3),
            8: lambda: take_core(6, mlp_right(6)),
            9: lambda: produce(7, mlp_right(7)),
            10: lambda: take_dp(0),
            11: lambda: take_dp(1),
            12: lambda: take_second(2),
            13: lambda: take_second(3),
            14: lambda: take_first(4),
            15: lambda: take_core(7, mlp_right(7)),
            16: lambda: take_dp(2),
        }

        def one_slot(index, _):
            frame = table[index]
            key_frame = table[SLOTS + index]
            q_parts = head_parts(q_ref[frame] * jnp.bfloat16(0.125))
            do_parts = head_parts(do_own[frame])
            keys = k_ref[key_frame]
            values = v_ref[key_frame]
            turned = keys.T
            half = bias_ref[key_frame]
            row = lax.broadcasted_iota(jnp.int32, (tokens, tokens), 0)
            column = lax.broadcasted_iota(jnp.int32, (tokens, tokens), 1)
            same = table[2 * SLOTS + 8 * frames + index].astype(jnp.float32)
            keep = 1.0 - jnp.where(row == column, 1.0, 0.0) * same
            bias = jnp.concatenate([half, half], axis=1) * keep
            dv = dk = None
            dq = []
            for part in range(2):
                lse = lse_ref[frame, part : part + 1, :]
                delta = deltas[frame, part : part + 1, :]
                probs = jnp.exp(dot_nt(keys, q_parts[part]) + bias - lse)
                prob_grad = dot_nt(values, do_parts[part])
                score_grad = (probs * (prob_grad - delta)).astype(jnp.bfloat16)
                dv_part = dot_nn(probs.astype(jnp.bfloat16), do_parts[part])
                dk_part = dot_nn(score_grad, q_parts[part])
                dv = dv_part if dv is None else dv + dv_part
                dk = dk_part if dk is None else dk + dk_part
                dq.append(
                    dot_nn(turned[part * HEAD_DIM : (part + 1) * HEAD_DIM, :], score_grad)
                )
            dv_slots[index] = dv
            dk_slots[index] = dk
            dq_slots[index] = jnp.concatenate(dq, axis=0)
            for place, work in side_work.items():
                pl.when(index == place)(work)
            return 0

        lax.fori_loop(0, SLOTS, one_slot, 0)

        def summed(slots, start, frame):
            total = slots[table[start + 4 * frame]]
            for way in range(1, 4):
                total = total + slots[table[start + 4 * frame + way]]
            return total

        def combine(frame):
            dq = summed(dq_slots, 2 * SLOTS, frame).T * 0.125
            qkv_send[frame, 0] = dq.astype(jnp.bfloat16)
            dk = summed(dk_slots, 2 * SLOTS + 4 * frames, frame)
            qkv_send[frame, 1] = dk.astype(jnp.bfloat16)
            dv = summed(dv_slots, 2 * SLOTS + 4 * frames, frame)
            qkv_send[frame, 2] = dv.astype(jnp.bfloat16)

        def qkv_copy(flips):
            peer = peer_head(head, flips)
            return remote(
                qkv_send.at[peer],
                back.at[:, :, own_lanes],
                a2a_send.at[2, flips],
                a2a_recv.at[2, flips],
                (group, peer),
            )

        def combine_loop(frame, _):
            combine(frame)
            return 0

        lax.fori_loop(0, frames, combine_loop, 0)
        for flips in others:
            qkv_copy(flips).start()
        back[:, :, own_lanes] = qkv_send[head]

        produce(8, out_right)
        take_second(4)
        take_first(5)
        take_core(8, out_right)
        take_dp(3)
        for copy in qkv_loads:
            copy.wait()
        for flips in others:
            qkv_copy(flips).wait()

        def rope_back(chunk, _):
            lanes = pl.ds(pl.multiple_of(chunk * 128, 128), 128)
            cosine = mod_ref[6:7, lanes]
            sine = mod_ref[7:8, lanes]
            for place, target in ((0, dq_raw), (1, dk_raw)):
                value = back[place, :, lanes].astype(jnp.float32)
                target[:, lanes] = (value * cosine + turn_pairs(value, lanes) * sine).astype(
                    jnp.bfloat16
                )
            return 0

        lax.fori_loop(0, width // 128, rope_back, 0)

        def value_right(chunk):
            return back[2, :, lane_block(chunk)]

        def query_right(chunk):
            return dq_raw[:, lane_block(chunk)]

        def key_right(chunk):
            return dk_raw[:, lane_block(chunk)]

        rights = {9: value_right, 10: query_right, 11: key_right}
        produce(9, value_right)
        produce(10, query_right)
        take_core(9, value_right)
        take_core(10, query_right)
        produce(11, key_right)
        take_core(11, key_right)

        def to_first(chunk, _):
            lanes = lane_block(chunk)
            ba[:, lanes] = (
                dot_nt(dq_raw[...], wqkv[0, lanes, :])
                + dot_nt(dk_raw[...], wqkv[1, lanes, :])
                + dot_nt(back[2], wqkv[2, lanes, :])
            )
            return 0

        lax.fori_loop(0, chunks, to_first, 0)

        def first_norm_back(index, sums):
            shift_sum, scale_sum = sums
            rows = row_block(index)
            value = x_ref[rows, :].astype(jnp.float32)
            scale = lax.rsqrt(jnp.mean(value * value, axis=1, keepdims=True) + EPSILON)
            normed = value * scale
            grad = ba[rows, :]
            shift_sum = shift_sum + jnp.sum(grad, axis=0, keepdims=True)
            scale_sum = scale_sum + jnp.sum(grad * normed, axis=0, keepdims=True)
            inner = grad * (1.0 + scale_one)
            mean = jnp.mean(inner * normed, axis=1, keepdims=True)
            gin_ref[rows, :] = mid[rows, :] + scale * (inner - normed * mean)
            return shift_sum, scale_sum

        shift_one_grad, scale_one_grad = lax.fori_loop(
            0, steps, first_norm_back, (row_zero, row_zero)
        )
        vectors = jnp.concatenate(
            [
                cond_ref[...].astype(jnp.float32),
                shift_one_grad,
                scale_one_grad,
                *saved_rows,
                row_zero,
            ],
            axis=0,
        )
        rows_ref[group, ybit, xbit, core] = vectors.astype(jnp.bfloat16)

    pl.run_scoped(
        attention_part,
        pltpu.VMEM((3, width, width), jnp.bfloat16),
        pltpu.VMEM((SLOTS + 1, 128, tokens), jnp.float32),
        pltpu.VMEM((SLOTS + 1, tokens, 128), jnp.float32),
        pltpu.VMEM((SLOTS + 1, tokens, 128), jnp.float32),
        pltpu.VMEM((frames, 3, tokens, 128), jnp.bfloat16),
        pltpu.VMEM((tokens, width), jnp.bfloat16),
        pltpu.VMEM((tokens, width), jnp.bfloat16),
        pltpu.VMEM((frames, 2, tokens), jnp.float32),
    )

    mine = rows_ref.at[group, ybit, xbit, core]
    row_dp = [
        remote(mine, mine, row_dp_send.at[hop], row_dp_recv.at[hop], (dp_peers[hop], head))
        for hop in range(n_dp - 1)
    ]
    y_part = rows_ref.at[:, ybit, xbit, core]
    x_part = rows_ref.at[:, :, xbit, core]
    core_part = rows_ref.at[:, :, :, core]
    row_y = remote(y_part, y_part, row_send.at[0], row_recv.at[0], (group, y_peer))
    row_x = remote(x_part, x_part, row_send.at[1], row_recv.at[1], (group, x_peer))
    row_core = remote(core_part, core_part, row_send.at[2], row_recv.at[2], (group, core_peer))
    for copy in row_dp:
        copy.start()

    take_first(6)
    take_second(5)
    take_dp(4)
    for copy in row_dp:
        copy.wait()
    row_y.start()
    take_first(7)
    take_second(6)
    take_dp(5)
    row_y.wait()
    row_x.start()
    take_first(8)
    take_second(7)
    take_dp(6)
    row_x.wait()
    row_core.start()
    take_first(9)
    take_second(8)
    take_dp(7)
    row_core.wait()
    take_first(10)
    take_second(9)
    take_dp(8)
    take_first(11)
    take_second(10)
    take_dp(9)
    take_second(11)
    take_dp(10)
    take_dp(11)
    core_copy(count - 2).wait_send()
    core_copy(count - 1).wait_send()


def back_part(n_dp, table, attended, queries, keys, values, lse, bias, hidden, cotangent, normed,
              modulation, cond_act, valid, weights):
    tokens, width = hidden.shape
    frames = attended.shape[0] // tokens
    hidden_width = weights[1].shape[1]
    devices = n_dp * 8
    small, large = width // devices, hidden_width // devices
    first_up = large // small
    tiles = hidden_width // width
    units = first_up + tiles + 4
    slots = units - 3
    dma = pltpu.SemaphoreType.DMA
    f32, bf16 = jnp.float32, jnp.bfloat16
    shape = jax.ShapeDtypeStruct
    return pl.pallas_call(
        lambda *refs: back_kernel(n_dp, *refs),
        out_shape=(
            shape((tokens, width), bf16),
            shape((tokens, width), f32),
            shape((8, 128), f32),
            *[shape((small, width), f32)] * 4,
            shape((small, hidden_width), f32),
            shape((large, width), f32),
            shape((n_dp, 2, 2, 2, 8, width), bf16),
        ),
        in_specs=[IN_SMEM] + [IN_VMEM] * 12 + [IN_PLACE] * 6,
        out_specs=tuple([IN_VMEM] * 10),
        scratch_shapes=[
            pltpu.VMEM((tokens, width), bf16),
            pltpu.VMEM((frames, tokens, 128), bf16),
            pltpu.VMEM((3, tokens, width), bf16),
            pltpu.VMEM((slots, n_dp, 2, 2, small, width), bf16),
            pltpu.VMEM((slots, n_dp, 2, small, width), bf16),
            pltpu.VMEM((slots, n_dp, small, width), bf16),
            pltpu.VMEM((units, n_dp - 1, small, width), bf16),
            pltpu.VMEM((2, n_dp, 2, 2, small, width), bf16),
            pltpu.VMEM((tokens, width), bf16),
            pltpu.VMEM((first_up + 3, 2, width // 2, tokens), bf16),
            pltpu.VMEM((tokens, width), bf16),
            pltpu.VMEM((tokens, width), bf16),
            pltpu.VMEM((tokens, hidden_width), bf16),
            pltpu.VMEM((tokens, width), bf16),
            pltpu.VMEM((tokens, width), f32),
            pltpu.VMEM((tokens, width), f32),
            pltpu.VMEM((width, width), bf16),
            dma((1 + 2 * tiles + 3,)),
            dma((3, 8)),
            dma((3, 8)),
            *[dma((units,))] * 6,
            dma((units, n_dp - 1)),
            dma((units, n_dp - 1)),
            dma((3,)),
            dma((3,)),
            dma((n_dp - 1,)),
            dma((n_dp - 1,)),
        ],
        compiler_params=pltpu.CompilerParams(
            collective_id=0, has_side_effects=True, vmem_limit_bytes=67043328
        ),
        name="back_part",
    )(
        table,
        attended,
        *[array.reshape(frames, tokens, 128) for array in (queries, keys, values)],
        lse,
        bias.reshape(frames, tokens, 128),
        hidden,
        cotangent,
        normed,
        modulation,
        cond_act,
        valid,
        *weights,
    )


def slot_table(first, frames):
    pair = jnp.arange(4 * frames, dtype=jnp.int32)
    frame, back = pair // 4, pair % 4
    held = (frame - back) >= jnp.repeat(first, 4)
    rank = jnp.sum((held[None, :] & (pair[None, :] < pair[:, None])).astype(jnp.int32), axis=1)
    slot = jnp.where(held, rank, SLOTS)
    hit = slot[None, :] == jnp.arange(SLOTS, dtype=jnp.int32)[:, None]
    query = jnp.sum(jnp.where(hit, frame[None, :], 0), axis=1)
    key = jnp.sum(jnp.where(hit, (frame - back)[None, :], 0), axis=1)
    grid = slot.reshape(frames, 4)
    columns = [
        jnp.concatenate([grid[way:, way], jnp.full((way,), SLOTS, jnp.int32)]) for way in range(4)
    ]
    same = (query == key).astype(jnp.int32)
    return jnp.concatenate([query, key, slot, jnp.stack(columns, axis=1).reshape(-1), same])


def per_device(
    hidden_in,
    frame_cond,
    query_weight,
    key_weight,
    value_weight,
    output_weight,
    up_weight,
    down_weight,
    modulation_weight,
    clip_lengths,
    patch_valid,
    cotangent,
):
    tok_dev, model_width = hidden_in.shape
    frames_dev = frame_cond.shape[0]
    group_tokens = patch_valid.shape[0]
    head_index = lax.axis_index("head")
    clip_of, frame_of, position = group_layout(clip_lengths[0], group_tokens, PATCHES)
    local_start = head_index * tok_dev
    local_position = lax.dynamic_slice_in_dim(position, local_start, tok_dev)
    local_valid = (
        lax.dynamic_slice_in_dim(patch_valid, local_start, tok_dev)
        .astype(jnp.float32)
        .reshape(frames_dev, PATCHES)
    )
    angles = local_position.astype(jnp.float32)[:, None] * frequencies(HEAD_DIM // 2)[None, :]
    cond_value = frame_cond.astype(jnp.float32)
    cond_act = jax.nn.silu(cond_value).astype(jnp.bfloat16)
    modulation = jnp.dot(cond_act, modulation_weight, preferred_element_type=jnp.float32).reshape(
        frames_dev, 1, 6 * model_width
    )
    shift_one, scale_one, gate_one, shift_two, scale_two, gate_two = jnp.split(
        modulation, 6, axis=2
    )
    tokens = hidden_in.astype(jnp.float32).reshape(frames_dev, PATCHES, model_width)
    normed_one = (
        modulate(tokens, shift_one, scale_one).astype(jnp.bfloat16).reshape(tok_dev, model_width)
    )
    query_raw = jnp.dot(normed_one, query_weight, preferred_element_type=jnp.float32)
    key_raw = jnp.dot(normed_one, key_weight, preferred_element_type=jnp.float32)
    query_send = (
        rotate(query_raw.reshape(tok_dev, HEADS, HEAD_DIM), angles)
        .reshape(tok_dev, model_width)
        .astype(jnp.bfloat16)
    )
    key_send = (
        rotate(key_raw.reshape(tok_dev, HEADS, HEAD_DIM), angles)
        .reshape(tok_dev, model_width)
        .astype(jnp.bfloat16)
    )
    value_send = jnp.dot(normed_one, value_weight, preferred_element_type=jnp.float32).astype(
        jnp.bfloat16
    )
    head_query, head_key, head_value = (
        lax.all_to_all(query_send, "head", split_axis=1, concat_axis=0, tiled=True),
        lax.all_to_all(key_send, "head", split_axis=1, concat_axis=0, tiled=True),
        lax.all_to_all(value_send, "head", split_axis=1, concat_axis=0, tiled=True),
    )
    first_frames = (frame_of - position)[::PATCHES]
    bias = jnp.broadcast_to(
        jnp.where(patch_valid == 1, 0.0, MASKED).astype(jnp.float32)[:, None],
        (group_tokens, 128),
    )
    attended_send, logsum = attend_forward(first_frames, head_query, head_key, head_value, bias)
    n_dp = lax.axis_size("dp")
    row_angles = angles[0]
    cosine, sine = jnp.cos(row_angles), jnp.sin(row_angles)
    table_rows = jnp.concatenate(
        [
            modulation.reshape(6, model_width),
            jnp.tile(jnp.concatenate([cosine, cosine]), HEADS)[None],
            jnp.tile(jnp.concatenate([sine, -sine]), HEADS)[None],
        ],
        axis=0,
    )
    (
        block_out,
        grad_input,
        statistics,
        grad_query,
        grad_key,
        grad_value,
        grad_output,
        grad_up,
        grad_down,
        gathered,
    ) = back_part(
        n_dp,
        slot_table(first_frames, group_tokens // PATCHES),
        attended_send,
        head_query,
        head_key,
        head_value,
        logsum,
        bias,
        hidden_in,
        cotangent,
        normed_one,
        table_rows,
        cond_act,
        jnp.broadcast_to(local_valid.reshape(tok_dev, 1), (tok_dev, 128)),
        (output_weight, up_weight, down_weight, query_weight, key_weight, value_weight),
    )
    device = lax.axis_index("dp") * lax.axis_size("head") + head_index
    gathered = gathered.reshape(n_dp * 8, 8, model_width)
    share = model_width // (n_dp * 8)
    dmod_all = gathered[:, 1:7].reshape(n_dp * 8, 6 * model_width)
    grad_modulation = inner_rows(
        lax.dynamic_slice_in_dim(gathered[:, 0], device * share, share, 1), dmod_all
    )
    modulation_grad = lax.dynamic_slice_in_dim(dmod_all, device, 1, 0)
    cond_act_grad = times_transposed(modulation_grad, modulation_weight)
    grad_cond = jax.vjp(jax.nn.silu, cond_value)[1](cond_act_grad)[0]
    return (
        block_out,
        grad_input,
        grad_cond,
        grad_query,
        grad_key,
        grad_value,
        grad_output,
        grad_up,
        grad_down,
        grad_modulation,
        statistics[:1, :3],
    )


def solution(mesh):
    in_specs = (
        P(("dp", "head"), None),
        P(("dp", "head"), None),
        P(),
        P(),
        P(),
        P(),
        P(),
        P(),
        P(),
        P("dp", None),
        P("dp"),
        P(("dp", "head"), None),
    )
    out_specs = (
        P(("dp", "head"), None),
        P(("dp", "head"), None),
        P(("dp", "head"), None),
        P(("dp", "head"), None),
        P(("dp", "head"), None),
        P(("dp", "head"), None),
        P(("dp", "head"), None),
        P(("dp", "head"), None),
        P(("dp", "head"), None),
        P(("dp", "head"), None),
        P(("dp", "head"), None),
    )
    return jax.shard_map(
        per_device, mesh=mesh, in_specs=in_specs, out_specs=out_specs, check_vma=False
    )
```

```python
import math

import jax
import jax.numpy as jnp
from jax import lax
from jax.experimental import pallas as pl
from jax.experimental.pallas import tpu as pltpu
from jax.sharding import PartitionSpec as P

HEADS = 16
HEAD_DIM = 64
PATCHES = 256


EPSILON = 1e-06
MASKED = -1e30


def frequencies(half_dim):
    return jnp.exp(jnp.arange(half_dim, dtype=jnp.float32) * (-math.log(10000.0) / half_dim))


def dot_nt(left, right):
    return lax.dot_general(
        left, right, (((1,), (1,)), ((), ())), preferred_element_type=jnp.float32
    )


def dot_nn(left, right):
    return lax.dot_general(
        left, right, (((1,), (0,)), ((), ())), preferred_element_type=jnp.float32
    )


def head_parts(block):
    lane = lax.broadcasted_iota(jnp.int32, block.shape, 1)
    zero = jnp.zeros_like(block)
    return jnp.where(lane < HEAD_DIM, block, zero), jnp.where(lane < HEAD_DIM, zero, block)


def key_bias(bias_ref, key_frame, frame):
    half = bias_ref[pl.ds(key_frame * PATCHES, PATCHES), :]
    bias = jnp.concatenate([half, half], axis=1)
    row = lax.broadcasted_iota(jnp.int32, bias.shape, 0)
    column = lax.broadcasted_iota(jnp.int32, bias.shape, 1)
    own = (row == column) & (key_frame == frame)
    return jnp.where(own, 0.0, bias)


def attend_forward_kernel(first_ref, q_ref, k_ref, v_ref, bias_ref, o_ref, lse_ref, scores):
    frames = q_ref.shape[0] // PATCHES

    def one_frame(frame, _):
        rows = pl.ds(frame * PATCHES, PATCHES)
        parts = head_parts(q_ref[rows, :] * jnp.bfloat16(0.125))
        first = first_ref[frame]

        def score(key_frame, tops):
            keys = k_ref[pl.ds(key_frame * PATCHES, PATCHES), :]
            bias = key_bias(bias_ref, key_frame, frame)
            new = []
            for head in range(2):
                value = dot_nt(keys, parts[head]) + bias
                scores[head, key_frame - first] = value
                new.append(jnp.maximum(tops[head], jnp.max(value, axis=0, keepdims=True)))
            return tuple(new)

        low = jnp.full((1, PATCHES), MASKED, jnp.float32)
        tops = lax.fori_loop(first, frame + 1, score, (low, low))

        def exponent(key_frame, totals):
            new = []
            for head in range(2):
                value = jnp.exp(scores[head, key_frame - first] - tops[head])
                scores[head, key_frame - first] = value
                new.append(totals[head] + jnp.sum(value, axis=0, keepdims=True))
            return tuple(new)

        zero = jnp.zeros((1, PATCHES), jnp.float32)
        totals = lax.fori_loop(first, frame + 1, exponent, (zero, zero))
        inverse = [1.0 / total for total in totals]

        def weigh(key_frame, sums):
            turned = v_ref[pl.ds(key_frame * PATCHES, PATCHES), :].T
            new = []
            for head in range(2):
                probs = (scores[head, key_frame - first] * inverse[head]).astype(jnp.bfloat16)
                new.append(
                    sums[head]
                    + dot_nn(turned[head * HEAD_DIM : (head + 1) * HEAD_DIM, :], probs)
                )
            return tuple(new)

        empty = jnp.zeros((HEAD_DIM, PATCHES), jnp.float32)
        sums = lax.fori_loop(first, frame + 1, weigh, (empty, empty))
        o_ref[rows, :] = jnp.concatenate(sums, axis=0).T.astype(jnp.bfloat16)
        for head in range(2):
            lse_ref[frame, head : head + 1, :] = tops[head] + jnp.log(totals[head])
        return 0

    lax.fori_loop(0, frames, one_frame, 0)


IN_SMEM = pl.BlockSpec(memory_space=pltpu.SMEM)
IN_VMEM = pl.BlockSpec(memory_space=pltpu.VMEM)
IN_PLACE = pl.BlockSpec(memory_space=pl.ANY)
MESH_ID = pl.DeviceIdType.MESH


def attend_forward(first, queries, keys, values, bias):
    tokens, width = queries.shape
    frames = tokens // PATCHES
    return pl.pallas_call(
        attend_forward_kernel,
        out_shape=(
            jax.ShapeDtypeStruct((tokens, width), jnp.bfloat16),
            jax.ShapeDtypeStruct((frames, 2, PATCHES), jnp.float32),
        ),
        in_specs=[IN_SMEM] + [IN_VMEM] * 4,
        out_specs=(IN_VMEM, IN_VMEM),
        scratch_shapes=[pltpu.VMEM((2, 4, PATCHES, PATCHES), jnp.float32)],
        name="attend_forward",
    )(first, queries, keys, values, bias)


SLOTS = 17
BLOCK = 256


def peer_head(head, flips):
    core = lax.rem(head, 2)
    second = lax.rem(lax.div(head, 2), 2)
    third = lax.div(head, 4)
    if flips % 2:
        core = 1 - core
    if flips // 2 % 2:
        second = 1 - second
    if flips // 4:
        third = 1 - third
    return 4 * third + 2 * second + core


def remote(source, target, send, receive, where):
    return pltpu.make_async_remote_copy(
        src_ref=source,
        dst_ref=target,
        send_sem=send,
        recv_sem=receive,
        device_id=where,
        device_id_type=MESH_ID,
    )


def gelu_and_slope(value):
    square = value * value
    inner = 0.7978845608028654 * value * (1.0 + 0.044715 * square)
    bend = jnp.tanh(inner)
    half = 0.5 * (1.0 + bend)
    slope = half + 0.5 * value * (1.0 - bend * bend) * (
        0.7978845608028654 * (1.0 + 0.134145 * square)
    )
    return value * half, slope


def turn_pairs(values, _):
    lane = lax.rem(lax.broadcasted_iota(jnp.int32, values.shape, 1), HEAD_DIM)
    up = pltpu.roll(values, 128 - HEAD_DIM // 2, 1)
    down = pltpu.roll(values, HEAD_DIM // 2, 1)
    return jnp.where(lane < HEAD_DIM // 2, up, down)


def back_kernel(n_dp, *refs):
    (
        table,
        att_own,
        lse_ref,
        x_ref,
        cot_ref,
        mod_ref,
        rope_ref,
        cond_ref,
        valid_ref,
        q_hbm,
        k_hbm,
        v_hbm,
        bias_hbm,
        n1_hbm,
        wo_hbm,
        up_hbm,
        down_hbm,
        wq_hbm,
        wk_hbm,
        wv_hbm,
        wmod_hbm,
        block_hbm,
        gin_ref,
        stat_ref,
        gq_ref,
        gk_ref,
        gv_ref,
        go_ref,
        gup_ref,
        gdown_ref,
        gmod_hbm,
        gcond_ref,
        n1_all,
        att_fr,
        do_own,
        from_core,
        from_first,
        from_second,
        from_dp,
        core_out,
        da_send,
        lhs,
        dmlp,
        dhid,
        dattn,
        mid,
        rows_ref,
        z_send,
        z_recv,
        p_send,
        p_recv,
        load_sem,
        a2a_send,
        a2a_recv,
        core_send,
        core_recv,
        first_send,
        first_recv,
        second_send,
        second_recv,
        dp_send,
        dp_recv,
        row_send,
        row_recv,
        row_dp_send,
        row_dp_recv,
        gather_send,
        gather_recv,
        z_send_sem,
        z_recv_sem,
        mod_sem,
    ) = refs
    tokens, width = x_ref.shape
    frames = q_hbm.shape[0]
    hidden_width = up_hbm.shape[1]
    tiles = hidden_width // width
    chunks = width // BLOCK
    small = width // (n_dp * 8)
    large = hidden_width // (n_dp * 8)
    half_rows = n_dp * 4 * small
    group = lax.axis_index("dp")
    head = lax.axis_index("head")
    core = lax.rem(head, 2)
    xbit = lax.rem(lax.div(head, 2), 2)
    ybit = lax.div(head, 4)
    core_peer, x_peer, y_peer = peer_head(head, 1), peer_head(head, 2), peer_head(head, 4)
    dp_peers = [lax.rem(group + hop, n_dp) for hop in range(1, n_dp)]
    others = range(1, 8)

    barrier = pltpu.get_barrier_semaphore()
    for flips in others:
        pl.semaphore_signal(
            barrier, inc=1, device_id=(group, peer_head(head, flips)), device_id_type=MESH_ID
        )
    for peer in dp_peers:
        pl.semaphore_signal(barrier, inc=1, device_id=(peer, head), device_id_type=MESH_ID)

    pl.semaphore_wait(barrier, 7 + len(dp_peers))

    own_rows = pl.ds(head * tokens, tokens)
    own_lanes = pl.ds(head * 128, 128)

    def att_copy(flips):
        peer = peer_head(head, flips)
        return remote(
            att_own.at[pl.ds(peer * tokens, tokens), :],
            att_fr.at[:, own_lanes],
            a2a_send.at[0, flips],
            a2a_recv.at[0, flips],
            (group, peer),
        )

    def grad_copy(flips):
        peer = peer_head(head, flips)
        return remote(
            da_send.at[:, pl.ds(peer * 128, 128)],
            do_own.at[head],
            a2a_send.at[1, flips],
            a2a_recv.at[1, flips],
            (group, peer),
        )

    first_up = large // small
    first_out = first_up + tiles
    count = first_out + 3

    def slot_of(unit):
        return unit

    def lhs_of(unit):
        if unit < first_up:
            return unit
        return first_up if unit < first_out else first_up + 1

    def core_copy(unit):
        return remote(
            core_out.at[unit % 2],
            from_core.at[slot_of(unit)],
            core_send.at[unit],
            core_recv.at[unit],
            (group, core_peer),
        )

    def x_leads(unit):
        return unit % 2 == 0

    def first_copy(unit):
        slot = slot_of(unit)
        if x_leads(unit):
            source, peer = from_core.at[slot, :, :, 1 - xbit], x_peer
        else:
            source, peer = from_core.at[slot, :, 1 - ybit], y_peer
        return remote(
            source, from_first.at[slot], first_send.at[unit], first_recv.at[unit], (group, peer)
        )

    def second_copy(unit):
        slot = slot_of(unit)
        if x_leads(unit):
            source, peer = from_core.at[slot, :, 1 - ybit, xbit], y_peer
        else:
            source, peer = from_core.at[slot, :, ybit, 1 - xbit], x_peer
        return remote(
            source, from_second.at[slot], second_send.at[unit], second_recv.at[unit], (group, peer)
        )

    def dp_copy(unit, hop):
        peer = dp_peers[hop]
        return remote(
            from_core.at[slot_of(unit), peer, ybit, xbit],
            from_dp.at[unit, hop],
            dp_send.at[unit, hop],
            dp_recv.at[unit, hop],
            (peer, head),
        )

    def added(left, right):
        return (left.astype(jnp.float32) + right.astype(jnp.float32)).astype(jnp.bfloat16)

    def put(target, lanes, value, unit):
        value = value.astype(jnp.bfloat16)
        if unit <= first_out:
            target[:, :, :, :, lanes] = value.reshape(n_dp, 2, 2, small, BLOCK)
        else:
            value = value.reshape(4, n_dp, small, BLOCK)
            for chip in range(4):
                target[:, chip // 2, chip % 2, :, lanes] = value[chip]

    def got(source, lanes, unit):
        if unit <= first_out:
            return source[:, :, :, :, lanes].reshape(half_rows, BLOCK)
        return jnp.concatenate(
            [
                source[:, chip // 2, chip % 2, :, lanes].reshape(half_rows // 4, BLOCK)
                for chip in range(4)
            ],
            axis=0,
        )

    def produce(unit, product):
        if unit >= 2:
            core_copy(unit - 2).wait_send()

        def body(chunk, _):
            lanes = pl.ds(pl.multiple_of(chunk * BLOCK, BLOCK), BLOCK)
            put(core_out.at[unit % 2], lanes, product(unit, 1 - core, chunk), unit)
            return 0

        lax.fori_loop(0, chunks, body, 0)
        core_copy(unit).start()

    def take_core(unit, product):
        core_copy(unit).wait_recv()
        place = from_core.at[slot_of(unit)]

        def body(chunk, _):
            lanes = pl.ds(pl.multiple_of(chunk * BLOCK, BLOCK), BLOCK)
            value = product(unit, core, chunk) + got(place, lanes, unit).astype(jnp.float32)
            put(place, lanes, value, unit)
            return 0

        lax.fori_loop(0, chunks, body, 0)
        first_copy(unit).start()

    def take_first(unit):
        first_copy(unit).wait()
        slot = slot_of(unit)

        def body(index, _):
            at_dp = lax.div(index, 2)
            other = lax.rem(index, 2)
            at_y, at_x = (other, xbit) if x_leads(unit) else (ybit, other)
            from_core[slot, at_dp, at_y, at_x] = added(
                from_core[slot, at_dp, at_y, at_x], from_first[slot, at_dp, other]
            )
            return 0

        lax.fori_loop(0, n_dp * 2, body, 0)
        second_copy(unit).start()

    def take_second(unit):
        second_copy(unit).wait()
        slot = slot_of(unit)

        def body(at_dp, _):
            from_core[slot, at_dp, ybit, xbit] = added(
                from_core[slot, at_dp, ybit, xbit], from_second[slot, at_dp]
            )
            return 0

        lax.fori_loop(0, n_dp, body, 0)
        for hop in range(n_dp - 1):
            dp_copy(unit, hop).start()

    def take_dp(unit):
        for hop in range(n_dp - 1):
            dp_copy(unit, hop).wait()
        total = from_core[slot_of(unit), group, ybit, xbit].astype(jnp.float32)
        for hop in range(n_dp - 1):
            total = total + from_dp[unit, hop].astype(jnp.float32)
        if unit < first_up:
            gdown_ref[unit * small : (unit + 1) * small, :] = total
        elif unit < first_out:
            place = (unit - first_up) * width
            gup_ref[:, place : place + width] = total
        else:
            go_ref[...] = total

    def turned_rows(index, source):
        for chunk in range(chunks):
            value = source[:, chunk * BLOCK : (chunk + 1) * BLOCK].T
            value = value.reshape(BLOCK // (2 * small), 2, small, tokens)
            for side in range(2):
                lhs[index, side, chunk * BLOCK // 2 : (chunk + 1) * BLOCK // 2, :] = value[
                    :, side
                ].reshape(BLOCK // 2, tokens)

    shift_one, scale_one, gate_one = (mod_ref[row : row + 1, :] for row in range(3))
    shift_two, scale_two, gate_two = (mod_ref[row : row + 1, :] for row in range(3, 6))
    step_rows = 32
    steps = tokens // step_rows

    def row_block(index):
        return pl.ds(pl.multiple_of(index * step_rows, step_rows), step_rows)

    def lane_block(chunk):
        return pl.ds(pl.multiple_of(chunk * BLOCK, BLOCK), BLOCK)

    def masked_square(values, rows):
        sums = jnp.sum(values * values, axis=1, keepdims=True) * valid_ref[rows, :1]
        return jnp.sum(sums, axis=0, keepdims=True)

    one = jnp.zeros((1, 1), jnp.float32)
    row_zero = jnp.zeros((1, width), jnp.float32)

    for flips in others:
        att_copy(flips).start()
    att_fr[:, own_lanes] = att_own[own_rows, :]

    def weight_product(unit, side, chunk):
        if unit < first_up:
            right = dmlp[:, lane_block(chunk)]
        elif unit < first_out:
            start = (unit - first_up) * width + chunk * BLOCK
            right = dhid[:, pl.ds(pl.multiple_of(start, BLOCK), BLOCK)]
        else:
            right = dattn[:, lane_block(chunk)]
        return dot_nn(lhs[lhs_of(unit), side], right)

    def run_plan(point, product=weight_product):
        for kind, unit in PLAN.get(point, ()):
            if kind == "P":
                produce(unit, product)
            elif kind == "C":
                take_core(unit, product)
            elif kind == "F":
                take_first(unit)
            elif kind == "S":
                take_second(unit)
            else:
                take_dp(unit)

    half = tokens // 2
    low, high = pl.ds(0, half), pl.ds(half, half)

    def gather_copy(index):
        if index == 0:
            source, target, peer = n1_hbm.at[low], n1_all.at[head, low], x_peer
        elif index == 1:
            source, target, peer = n1_hbm.at[high], n1_all.at[head, high], y_peer
        elif index == 2:
            source, target, peer = n1_hbm.at[low], n1_all.at[head, low], y_peer
        elif index == 3:
            source, target, peer = n1_all.at[x_peer, low], n1_all.at[x_peer, low], y_peer
        elif index == 4:
            source, target, peer = n1_hbm.at[high], n1_all.at[head, high], x_peer
        elif index == 5:
            source, target, peer = n1_all.at[y_peer, high], n1_all.at[y_peer, high], x_peer
        elif index == 6:
            source, target, peer = n1_hbm, n1_all.at[head], core_peer
        else:
            block = peer_head(head, 2 * (index - 6))
            source, target, peer = n1_all.at[block], n1_all.at[block], core_peer
        return remote(
            source, target, gather_send.at[index], gather_recv.at[index], (group, peer)
        )

    def mlp_part(up, down, act, dn2, wo, ba, n2):
        wo_load = pltpu.make_async_copy(wo_hbm, wo, load_sem.at[0])
        wo_load.start()
        up_loads = [
            pltpu.make_async_copy(
                up_hbm.at[:, pl.ds(tile * width, width)],
                up.at[:, pl.ds(tile * width, width)],
                load_sem.at[1 + tile],
            )
            for tile in range(tiles)
        ]
        down_loads = [
            pltpu.make_async_copy(
                down_hbm.at[pl.ds(tile * width, width), :],
                down.at[pl.ds(tile * width, width), :],
                load_sem.at[1 + tiles + tile],
            )
            for tile in range(tiles)
        ]
        for tile in range(tiles):
            up_loads[tile].start()
            down_loads[tile].start()

        wo_load.wait()
        for flips in others:
            att_copy(flips).wait()
        for index in (0, 1, 6):
            gather_copy(index).start()
        turned_rows(first_up + 1, att_fr)

        def project(chunk, _):
            lanes = lane_block(chunk)
            ba[:, lanes] = dot_nn(att_fr[...], wo[:, lanes])
            return 0

        lax.fori_loop(0, chunks, project, 0)

        def second_norm(index, total):
            rows = row_block(index)
            branch = gate_one * ba[rows, :]
            value = x_ref[rows, :].astype(jnp.float32) + branch
            mid[rows, :] = value
            scale = lax.rsqrt(jnp.mean(value * value, axis=1, keepdims=True) + EPSILON)
            n2[rows, :] = (value * scale * (1.0 + scale_two) + shift_two).astype(jnp.bfloat16)
            dmlp[rows, :] = (gate_two * cot_ref[rows, :].astype(jnp.float32)).astype(jnp.bfloat16)
            return total + masked_square(branch, rows)

        stat_attn = lax.fori_loop(0, steps, second_norm, one)
        turned_rows(first_up, n2)

        pairs = BLOCK // (2 * large)

        def feed(index, _):
            @pl.when(lax.rem(index, chunks) == 0)
            def _():
                tile = lax.div(index, chunks)
                pltpu.make_async_copy(
                    up_hbm.at[:, pl.ds(0, width)],
                    up.at[:, pl.ds(0, width)],
                    load_sem.at[1 + tile],
                ).wait()
                pltpu.make_async_copy(
                    down_hbm.at[pl.ds(0, width), :],
                    down.at[pl.ds(0, width), :],
                    load_sem.at[1 + tiles + tile],
                ).wait()

            @pl.when(index == GATHER_AT)
            def _():
                for step in (0, 1):
                    gather_copy(step).wait()
                for step in (2, 3, 4, 5):
                    gather_copy(step).start()

            lanes = lane_block(index)
            active, slope = gelu_and_slope(dot_nn(n2[...], up[:, lanes]))
            active = active.astype(jnp.bfloat16)
            act[:, lanes] = active
            grad = dot_nt(dmlp[...], down[lanes, :])
            dhid[:, lanes] = (grad * slope).astype(jnp.bfloat16)
            turned = active.T.reshape(pairs, 2, first_up, small, tokens)
            where = pl.ds(pl.multiple_of(index * pairs * small, pairs * small), pairs * small)
            for unit in range(first_up):
                for side in range(2):
                    lhs[unit, side, where, :] = turned[:, side, unit].reshape(
                        pairs * small, tokens
                    )
            return 0

        lax.fori_loop(0, hidden_width // BLOCK, feed, 0)

        run_plan("fed")

        def to_normed(chunk, _):
            lanes = lane_block(chunk)
            dn2[:, lanes] = dot_nt(dhid[...], up[lanes, :])
            return 0

        lax.fori_loop(0, chunks, to_normed, 0)
        run_plan("normed")

        def second_norm_back(index, sums):
            shift_sum, scale_sum, gate_sum = sums
            rows = row_block(index)
            value = mid[rows, :]
            scale = lax.rsqrt(jnp.mean(value * value, axis=1, keepdims=True) + EPSILON)
            normed = value * scale
            grad = dn2[rows, :]
            shift_sum = shift_sum + jnp.sum(grad, axis=0, keepdims=True)
            scale_sum = scale_sum + jnp.sum(grad * normed, axis=0, keepdims=True)
            inner = grad * (1.0 + scale_two)
            mean = jnp.mean(inner * normed, axis=1, keepdims=True)
            total = cot_ref[rows, :].astype(jnp.float32) + scale * (inner - normed * mean)
            dn2[rows, :] = total
            gate_sum = gate_sum + jnp.sum(total * ba[rows, :], axis=0, keepdims=True)
            dattn[rows, :] = (gate_one * total).astype(jnp.bfloat16)
            return shift_sum, scale_sum, gate_sum

        shift_two_grad, scale_two_grad, gate_one_grad = lax.fori_loop(
            0, steps, second_norm_back, (row_zero, row_zero, row_zero)
        )

        def to_attended(chunk, _):
            lanes = lane_block(chunk)
            da_send[:, lanes] = dot_nt(dattn[...], wo[lanes, :]).astype(jnp.bfloat16)
            return 0

        lax.fori_loop(0, chunks, to_attended, 0)
        for flips in others:
            grad_copy(flips).start()
        do_own[head] = da_send[:, own_lanes]

        run_plan("attended")

        def branch_out(chunk, _):
            lanes = lane_block(chunk)
            ba[:, lanes] = dot_nn(act[...], down[:, lanes])
            return 0

        lax.fori_loop(0, chunks, branch_out, 0)
        run_plan("branch")

        def outputs(index, sums):
            gate_sum, stat_mlp, stat_out = sums
            rows = row_block(index)
            raw = ba[rows, :]
            branch = gate_two * raw
            value = mid[rows, :] + branch
            n2[rows, :] = value.astype(jnp.bfloat16)
            gate_sum = gate_sum + jnp.sum(
                cot_ref[rows, :].astype(jnp.float32) * raw, axis=0, keepdims=True
            )
            stat_mlp = stat_mlp + masked_square(branch, rows)
            stat_out = stat_out + masked_square(value, rows)
            mid[rows, :] = dn2[rows, :]
            return gate_sum, stat_mlp, stat_out

        gate_two_grad, stat_mlp, stat_out = lax.fori_loop(0, steps, outputs, (row_zero, one, one))
        lane = lax.broadcasted_iota(jnp.int32, stat_ref.shape, 1)
        stats = jnp.where(lane == 0, stat_attn, jnp.where(lane == 1, stat_mlp, stat_out))
        stat_ref[...] = jnp.sqrt(stats / (tokens * width) + EPSILON)
        for row, vector in (
            (3, gate_one_grad),
            (4, shift_two_grad),
            (5, scale_two_grad),
            (6, gate_two_grad),
        ):
            gin_ref[row : row + 1, :] = vector
        block_copy = pltpu.make_async_copy(n2, block_hbm, load_sem.at[0])
        block_copy.start()
        run_plan("outputs")
        block_copy.wait()

    pl.run_scoped(
        mlp_part,
        pltpu.VMEM((width, hidden_width), jnp.bfloat16),
        pltpu.VMEM((hidden_width, width), jnp.bfloat16),
        pltpu.VMEM((tokens, hidden_width), jnp.bfloat16),
        pltpu.VMEM((tokens, width), jnp.float32),
        pltpu.VMEM((width, width), jnp.bfloat16),
        pltpu.VMEM((tokens, width), jnp.float32),
        pltpu.VMEM((tokens, width), jnp.bfloat16),
    )
    saved_rows = [gin_ref[row : row + 1, :] for row in range(3, 7)]

    def attention_part(
        q_ref,
        k_ref,
        v_ref,
        bias_ref,
        n1_group,
        w_own,
        dq_slots,
        dk_slots,
        dv_slots,
        deltas,
        d_all,
        d_turned,
        dn1,
        cond_sum,
    ):
        pieces = [
            (q_hbm, q_ref),
            (k_hbm, k_ref),
            (v_hbm, v_ref),
            (bias_hbm, bias_ref),
            (wq_hbm.at[:, own_lanes], w_own.at[:, pl.ds(0, 128)]),
            (wk_hbm.at[:, own_lanes], w_own.at[:, pl.ds(128, 128)]),
            (wv_hbm.at[:, own_lanes], w_own.at[:, pl.ds(256, 128)]),
        ]
        loads = [
            pltpu.make_async_copy(source, target, load_sem.at[1 + place])
            for place, (source, target) in enumerate(pieces)
        ]
        for copy in loads:
            copy.start()

        pages = frames // 2

        class mod_load:
            def __init__(self, block):
                self.copies = [
                    pltpu.make_async_copy(
                        wmod_hbm.at[pl.ds(page * tokens, tokens), pl.ds(block * width, width)],
                        n1_group.at[block % 2 * pages + page],
                        mod_sem.at[block, page],
                    )
                    for page in range(pages)
                ]

            def start(self):
                for copy in self.copies:
                    copy.start()

            def wait(self):
                for copy in self.copies:
                    copy.wait()

        run_plan("scope")
        for step in (2, 3, 4, 5):
            gather_copy(step).wait()
        for step in (7, 8, 9):
            gather_copy(step).start()
        for flips in others:
            grad_copy(flips).wait()
        for copy in loads:
            copy.wait()
        for slots in (dq_slots, dk_slots, dv_slots):
            slots[SLOTS] = jnp.zeros(slots.shape[1:], jnp.float32)

        def frame_delta(frame, _):
            rows = pl.ds(pl.multiple_of(frame * tokens, tokens), tokens)
            product = (
                do_own[frame].astype(jnp.float32) * att_own[rows, :].astype(jnp.float32)
            ).T
            for part in range(2):
                deltas[frame, part : part + 1, :] = jnp.sum(
                    product[part * HEAD_DIM : (part + 1) * HEAD_DIM, :], axis=0, keepdims=True
                )
            return 0

        lax.fori_loop(0, frames, frame_delta, 0)

        def one_slot(index, _):
            frame = table[index]
            key_frame = table[SLOTS + index]
            q_parts = head_parts(q_ref[frame] * jnp.bfloat16(0.125))
            do_parts = head_parts(do_own[frame])
            keys = k_ref[key_frame]
            values = v_ref[key_frame]
            turned = keys.T
            half = bias_ref[key_frame]
            row = lax.broadcasted_iota(jnp.int32, (tokens, tokens), 0)
            column = lax.broadcasted_iota(jnp.int32, (tokens, tokens), 1)
            same = table[2 * SLOTS + 8 * frames + index].astype(jnp.float32)
            keep = 1.0 - jnp.where(row == column, 1.0, 0.0) * same
            bias = jnp.concatenate([half, half], axis=1) * keep
            dv = dk = None
            dq = []
            for part in range(2):
                lse = lse_ref[frame, part : part + 1, :]
                delta = deltas[frame, part : part + 1, :]
                probs = jnp.exp(dot_nt(keys, q_parts[part]) + bias - lse)
                prob_grad = dot_nt(values, do_parts[part])
                score_grad = (probs * (prob_grad - delta)).astype(jnp.bfloat16)
                dv_part = dot_nn(probs.astype(jnp.bfloat16), do_parts[part])
                dk_part = dot_nn(score_grad, q_parts[part])
                dv = dv_part if dv is None else dv + dv_part
                dk = dk_part if dk is None else dk + dk_part
                dq.append(
                    dot_nn(turned[part * HEAD_DIM : (part + 1) * HEAD_DIM, :], score_grad)
                )
            dv_slots[index] = dv
            dk_slots[index] = dk
            dq_slots[index] = jnp.concatenate(dq, axis=0)
            for place in range(SLOTS):
                if PLAN.get(place):
                    pl.when(index == place)(lambda place=place: run_plan(place))
            return 0

        lax.fori_loop(0, SLOTS, one_slot, 0)

        def summed(slots, start, frame):
            total = slots[table[start + 4 * frame]]
            for way in range(1, 4):
                total = total + slots[table[start + 4 * frame + way]]
            return total

        def combine(frame, _):
            side, chip = lax.rem(frame, 2), lax.div(frame, 2)
            cosine = rope_ref[frame, 0:1, :]
            sine = rope_ref[frame, 1:2, :]

            def turned_back(value):
                value = value.astype(jnp.bfloat16).astype(jnp.float32)
                return (value * cosine + turn_pairs(value, None) * sine).astype(jnp.bfloat16)

            start = 2 * SLOTS + 4 * frames
            parts = (
                turned_back(summed(dq_slots, 2 * SLOTS, frame).T * 0.125),
                turned_back(summed(dk_slots, start, frame)),
                summed(dv_slots, start, frame).astype(jnp.bfloat16),
            )
            where = pl.ds(pl.multiple_of(frame * tokens, tokens), tokens)
            for place, part in enumerate(parts):
                d_all[side, chip, :, place * 128 : (place + 1) * 128] = part
                d_turned[place * 128 : (place + 1) * 128, where] = part.T
            return 0

        lax.fori_loop(0, frames, combine, 0)

        def normed_product(unit, side, chunk):
            first = (unit - first_out - 1) * half
            left = d_all[side, :, first : first + half, :].reshape(half_rows, 384)
            return dot_nt(left, w_own[lane_block(chunk), :])

        def normed_plan(point):
            run_plan(point, normed_product)

        for step in (6, 7, 8, 9):
            gather_copy(step).wait()
        group_loads = [
            pltpu.make_async_copy(n1_hbm, n1_group.at[head], load_sem.at[0])
        ] + [
            pltpu.make_async_copy(
                n1_all.at[peer_head(head, flips)],
                n1_group.at[peer_head(head, flips)],
                load_sem.at[flips],
            )
            for flips in others
        ]
        for copy in group_loads:
            copy.start()
        normed_plan("combined")
        for copy in group_loads:
            copy.wait()

        piece = width // n_dp

        def own_columns(chunk, _):
            right = n1_group[:, :, lane_block(chunk)].reshape(frames * tokens, BLOCK)
            value = dot_nn(d_turned[...], right).astype(jnp.bfloat16)
            for part in range(BLOCK // piece):
                z_send[chunk * (BLOCK // piece) + part] = value[
                    :, part * piece : (part + 1) * piece
                ]
            return 0

        lax.fori_loop(0, chunks, own_columns, 0)
        mod_load(2).start()
        mod_load(3).start()
        z_copies = [
            remote(
                z_send.at[dp_peers[hop]],
                z_recv.at[hop],
                z_send_sem.at[hop],
                z_recv_sem.at[hop],
                (dp_peers[hop], head),
            )
            for hop in range(n_dp - 1)
        ]
        for copy in z_copies:
            copy.start()
        normed_plan("columns")

        def cond_block(block, vector, first):
            vector = vector.astype(jnp.bfloat16).astype(jnp.float32)

            def body(index, _):
                rows = pl.ds(pl.multiple_of(index * 64, 64), 64)
                page = block % 2 * pages + lax.div(index, tokens // 64)
                inside = pl.ds(pl.multiple_of(lax.rem(index, tokens // 64) * 64, 64), 64)
                total = jnp.zeros((64, 128), jnp.float32) if first else cond_sum[rows, :]
                for lanes in range(0, width, 128):
                    total = total + n1_group[page, inside, lanes : lanes + 128].astype(
                        jnp.float32
                    ) * vector[:, lanes : lanes + 128]
                cond_sum[rows, :] = total
                return 0

            lax.fori_loop(0, width // 64, body, 0)

        mod_load(2).wait()
        cond_block(2, saved_rows[0], True)
        mod_load(4).start()
        mod_load(3).wait()
        cond_block(3, saved_rows[1], False)
        mod_load(5).start()
        normed_plan("cond1")
        mod_load(4).wait()
        cond_block(4, saved_rows[2], False)
        mod_load(0).start()
        mod_load(5).wait()
        cond_block(5, saved_rows[3], False)
        mod_load(1).start()
        normed_plan("cond2")

        for copy in z_copies:
            copy.wait()
        total = z_send[group].astype(jnp.float32)
        for hop in range(n_dp - 1):
            total = total + z_recv[hop].astype(jnp.float32)
        p_send[...] = total.T.reshape(8, small, 384)

        def part_copy(flips):
            peer = peer_head(head, flips)
            return remote(
                p_send.at[peer],
                p_recv.at[head],
                a2a_send.at[2, flips],
                a2a_recv.at[2, flips],
                (group, peer),
            )

        for flips in others:
            part_copy(flips).start()
        p_recv[head] = p_send[head]

        for unit in (first_out + 1, first_out + 2):
            second_copy(unit).wait()
            value = from_core[slot_of(unit), :, ybit, xbit].astype(jnp.float32)
            value = value + from_second[slot_of(unit)].astype(jnp.float32)
            first = (unit - first_out - 1) * half
            dn1[first : first + half, :] = value.reshape(half, width)

        def first_norm_back(index, sums):
            shift_sum, scale_sum = sums
            rows = row_block(index)
            value = x_ref[rows, :].astype(jnp.float32)
            scale = lax.rsqrt(jnp.mean(value * value, axis=1, keepdims=True) + EPSILON)
            normed = value * scale
            grad = dn1[rows, :]
            shift_sum = shift_sum + jnp.sum(grad, axis=0, keepdims=True)
            scale_sum = scale_sum + jnp.sum(grad * normed, axis=0, keepdims=True)
            inner = grad * (1.0 + scale_one)
            mean = jnp.mean(inner * normed, axis=1, keepdims=True)
            gin_ref[rows, :] = mid[rows, :] + scale * (inner - normed * mean)
            return shift_sum, scale_sum

        shift_one_grad, scale_one_grad = lax.fori_loop(
            0, steps, first_norm_back, (row_zero, row_zero)
        )
        vectors = jnp.concatenate(
            [
                cond_ref[0:1, :],
                shift_one_grad,
                scale_one_grad,
                *saved_rows,
                row_zero,
            ],
            axis=0,
        )
        rows_ref[group, ybit, xbit, core] = vectors.astype(jnp.bfloat16)

        mine = rows_ref.at[group, ybit, xbit, core]
        row_dp = [
            remote(mine, mine, row_dp_send.at[hop], row_dp_recv.at[hop], (dp_peers[hop], head))
            for hop in range(n_dp - 1)
        ]
        y_part = rows_ref.at[:, ybit, xbit, core]
        x_part = rows_ref.at[:, :, xbit, core]
        core_part = rows_ref.at[:, :, :, core]
        row_y = remote(y_part, y_part, row_send.at[0], row_recv.at[0], (group, y_peer))
        row_x = remote(x_part, x_part, row_send.at[1], row_recv.at[1], (group, x_peer))
        row_core = remote(core_part, core_part, row_send.at[2], row_recv.at[2], (group, core_peer))
        for copy in row_dp:
            copy.start()
        run_plan("rows")
        mod_load(0).wait()
        cond_block(0, shift_one_grad, False)
        mod_load(1).wait()
        cond_block(1, scale_one_grad, False)
        cond = cond_ref[1:2, :]
        gate = 1.0 / (1.0 + jnp.exp(-cond))
        gcond_ref[...] = jnp.sum(cond_sum[...].T, axis=0, keepdims=True) * (
            gate * (1.0 + cond * (1.0 - gate))
        )
        for copy in row_dp:
            copy.wait()
        row_y.start()
        run_plan("row_y")
        row_y.wait()
        row_x.start()
        run_plan("row_x")
        row_x.wait()
        row_core.start()
        for flips in others:
            part_copy(flips).wait()
        for block in range(8):
            for place, target in enumerate((gq_ref, gk_ref, gv_ref)):
                target[:, block * 128 : (block + 1) * 128] = p_recv[
                    block, :, place * 128 : (place + 1) * 128
                ]
        run_plan("row_core")
        row_core.wait()
        everyone = rows_ref[...].reshape(n_dp * 64, width)
        device = group * 8 + head
        wanted = lax.broadcasted_iota(jnp.int32, (small, width), 0) + device * small
        column = lax.broadcasted_iota(jnp.int32, (small, width), 1)
        picked = dot_nt(jnp.where(wanted == column, 1.0, 0.0).astype(jnp.bfloat16), everyone)
        place = lax.rem(lax.broadcasted_iota(jnp.int32, picked.shape, 1), 8)
        picked = jnp.where(place == 0, picked, 0.0)
        mod_out = []
        for block in range(6):
            left = pltpu.roll(picked, 1 + block, 1).astype(jnp.bfloat16)
            dn1[block * small : (block + 1) * small, :] = dot_nn(left, everyone)
            mod_out.append(
                pltpu.make_async_copy(
                    dn1.at[pl.ds(block * small, small), :],
                    gmod_hbm.at[:, pl.ds(block * width, width)],
                    load_sem.at[block],
                )
            )
            mod_out[-1].start()
        run_plan("end")
        for copy in mod_out:
            copy.wait()
        for unit in (count - 2, count - 1):
            core_copy(unit).wait_send()

    pl.run_scoped(
        attention_part,
        pltpu.VMEM((frames, tokens, 128), jnp.bfloat16),
        pltpu.VMEM((frames, tokens, 128), jnp.bfloat16),
        pltpu.VMEM((frames, tokens, 128), jnp.bfloat16),
        pltpu.VMEM((frames, tokens, 128), jnp.float32),
        pltpu.VMEM((frames, tokens, width), jnp.bfloat16),
        pltpu.VMEM((width, 384), jnp.bfloat16),
        pltpu.VMEM((SLOTS + 1, 128, tokens), jnp.float32),
        pltpu.VMEM((SLOTS + 1, tokens, 128), jnp.float32),
        pltpu.VMEM((SLOTS + 1, tokens, 128), jnp.float32),
        pltpu.VMEM((frames, 2, tokens), jnp.float32),
        pltpu.VMEM((2, frames // 2, tokens, 384), jnp.bfloat16),
        pltpu.VMEM((384, frames * tokens), jnp.bfloat16),
        pltpu.VMEM((tokens, width), jnp.float32),
        pltpu.VMEM((width, 128), jnp.float32),
    )


PLAN = {
    "fed": [("P", 0), ("P", 1)],
    "normed": [("C", 0), ("C", 1)],
    "attended": [("P", 2), ("P", 3)],
    "branch": [("C", 2), ("C", 3)],
    "outputs": [("P", 4), ("P", 5)],
    "scope": [("F", 0), ("F", 1)],
    2: [("C", 4), ("P", 6)],
    4: [("C", 5), ("P", 7)],
    8: [("F", 2)],
    9: [("F", 3)],
    10: [("C", 6)],
    12: [("S", 0)],
    13: [("S", 1)],
    14: [("C", 7)],
    15: [("P", 8)],
    "combined": [("P", 9), ("P", 10), ("C", 9), ("C", 10)],
    "columns": [("F", 4), ("F", 5)],
    "cond1": [("F", 9), ("F", 10)],
    "cond2": [],
    "rows": [("C", 8), ("S", 2), ("S", 3), ("D", 0), ("D", 1)],
    "row_y": [("F", 6), ("F", 7), ("D", 2)],
    "row_x": [("S", 4), ("D", 3)],
    "row_core": [("S", 5), ("F", 8), ("S", 6), ("S", 7)],
    "end": [("D", 4), ("D", 5), ("D", 6), ("D", 7), ("S", 8), ("D", 8)],
}
GATHER_AT = 8


def back_part(n_dp, vmem_operands, hbm_operands):
    table, attended, lse, hidden = vmem_operands[:4]
    hbm_up = hbm_operands[6]
    tokens, width = hidden.shape
    group_tokens = attended.shape[0]
    frames = group_tokens // tokens
    hidden_width = hbm_up.shape[1]
    devices = n_dp * 8
    small, large = width // devices, hidden_width // devices
    first_up = large // small
    tiles = hidden_width // width
    units = first_up + tiles + 3
    dma = pltpu.SemaphoreType.DMA
    f32, bf16 = jnp.float32, jnp.bfloat16
    shape = jax.ShapeDtypeStruct
    return pl.pallas_call(
        lambda *refs: back_kernel(n_dp, *refs),
        out_shape=(
            shape((tokens, width), bf16),
            shape((tokens, width), f32),
            shape((8, 128), f32),
            *[shape((small, width), f32)] * 4,
            shape((small, hidden_width), f32),
            shape((large, width), f32),
            shape((small, 6 * width), f32),
            shape((1, width), f32),
            shape((frames, tokens, width), bf16),
        ),
        in_specs=[IN_SMEM]
        + [IN_VMEM] * (len(vmem_operands) - 1)
        + [IN_PLACE] * len(hbm_operands),
        out_specs=(IN_PLACE, *[IN_VMEM] * 8, IN_PLACE, IN_VMEM, IN_PLACE),
        scratch_shapes=[
            pltpu.VMEM((tokens, width), bf16),
            pltpu.VMEM((frames, tokens, 128), bf16),
            pltpu.VMEM((units, n_dp, 2, 2, small, width), bf16),
            pltpu.VMEM((units, n_dp, 2, small, width), bf16),
            pltpu.VMEM((units, n_dp, small, width), bf16),
            pltpu.VMEM((units - 2, n_dp - 1, small, width), bf16),
            pltpu.VMEM((2, n_dp, 2, 2, small, width), bf16),
            pltpu.VMEM((tokens, width), bf16),
            pltpu.VMEM((first_up + 2, 2, width // 2, tokens), bf16),
            pltpu.VMEM((tokens, width), bf16),
            pltpu.VMEM((tokens, hidden_width), bf16),
            pltpu.VMEM((tokens, width), bf16),
            pltpu.VMEM((tokens, width), f32),
            pltpu.VMEM((n_dp, 2, 2, 2, 8, width), bf16),
            pltpu.VMEM((n_dp, 384, width // n_dp), bf16),
            pltpu.VMEM((n_dp - 1, 384, width // n_dp), bf16),
            pltpu.VMEM((8, small, 384), f32),
            pltpu.VMEM((8, small, 384), f32),
            dma((16,)),
            dma((3, 8)),
            dma((3, 8)),
            *[dma((units,))] * 6,
            dma((units, n_dp - 1)),
            dma((units, n_dp - 1)),
            dma((3,)),
            dma((3,)),
            dma((n_dp - 1,)),
            dma((n_dp - 1,)),
            dma((10,)),
            dma((10,)),
            dma((n_dp - 1,)),
            dma((n_dp - 1,)),
            dma((6, frames // 2)),
        ],
        compiler_params=pltpu.CompilerParams(
            collective_id=0, has_side_effects=True, vmem_limit_bytes=67043328
        ),
        name="back_part",
    )(*vmem_operands, *hbm_operands)


def front_kernel(*refs):
    (
        x_ref,
        mod_ref,
        rope_ref,
        wq_hbm,
        wk_hbm,
        wv_hbm,
        n1_ref,
        q_ref,
        k_ref,
        v_ref,
        weights,
        sent,
        load_sem,
        send_sem,
        recv_sem,
    ) = refs
    tokens, width = x_ref.shape
    group = lax.axis_index("dp")
    head = lax.axis_index("head")
    core = lax.rem(head, 2)
    barrier = pltpu.get_barrier_semaphore()
    for flips in range(1, 8):
        pl.semaphore_signal(
            barrier, inc=1, device_id=(group, peer_head(head, flips)), device_id_type=MESH_ID
        )
    loads = [
        pltpu.make_async_copy(source, weights.at[place], load_sem.at[place])
        for place, source in enumerate((wq_hbm, wk_hbm, wv_hbm))
    ]
    for copy in loads:
        copy.start()
    shift, scaling = mod_ref[0:1, :], mod_ref[1:2, :]

    def norm(index, _):
        rows = pl.ds(pl.multiple_of(index * 32, 32), 32)
        value = x_ref[rows, :].astype(jnp.float32)
        scale = lax.rsqrt(jnp.mean(value * value, axis=1, keepdims=True) + EPSILON)
        n1_ref[rows, :] = (value * scale * (1.0 + scaling) + shift).astype(jnp.bfloat16)
        return 0

    lax.fori_loop(0, tokens // 32, norm, 0)
    pl.semaphore_wait(barrier, 7)
    cosine, sine = rope_ref[0:1, :], rope_ref[1:2, :]
    outs = (q_ref, k_ref, v_ref)

    def copy_to(place, flips):
        peer = peer_head(head, flips)
        return remote(
            sent.at[place, :, pl.ds(peer * 128, 128)],
            outs[place].at[head],
            send_sem.at[place, flips],
            recv_sem.at[place, flips],
            (group, peer),
        )

    for place in range(3):
        loads[place].wait()
        for chip_flips in (6, 2, 4, 0):
            chip = lax.div(peer_head(head, chip_flips), 2)
            lanes = pl.ds(pl.multiple_of(chip * BLOCK, BLOCK), BLOCK)
            value = dot_nn(n1_ref[...], weights[place, :, lanes])
            for side in range(2):
                part = value[:, side * 128 : (side + 1) * 128]
                if place < 2:
                    part = part * cosine + turn_pairs(part, None) * sine
                where = pl.ds(pl.multiple_of(chip * BLOCK + side * 128, 128), 128)
                sent[place, :, where] = part.astype(jnp.bfloat16)
            for flips in (chip_flips, chip_flips + 1):
                if flips:
                    copy_to(place, flips).start()
        outs[place][head] = sent[place, :, pl.ds(pl.multiple_of(head * 128, 128), 128)]
    for place in range(3):
        for flips in range(1, 8):
            copy_to(place, flips).wait()


def front_part(hidden, modulation, rope, query_weight, key_weight, value_weight):
    tokens, width = hidden.shape
    dma = pltpu.SemaphoreType.DMA
    block = jax.ShapeDtypeStruct((8, tokens, 128), jnp.bfloat16)
    return pl.pallas_call(
        front_kernel,
        out_shape=(jax.ShapeDtypeStruct((tokens, width), jnp.bfloat16), block, block, block),
        in_specs=[IN_VMEM] * 3 + [IN_PLACE] * 3,
        out_specs=(IN_VMEM,) * 4,
        scratch_shapes=[
            pltpu.VMEM((3, width, width), jnp.bfloat16),
            pltpu.VMEM((3, tokens, width), jnp.bfloat16),
            dma((3,)),
            dma((3, 8)),
            dma((3, 8)),
        ],
        compiler_params=pltpu.CompilerParams(
            collective_id=1, has_side_effects=True, vmem_limit_bytes=32 * 1024 * 1024
        ),
        name="front_part",
    )(hidden, modulation, rope, query_weight, key_weight, value_weight)


def slot_table(first, frames):
    pair = jnp.arange(4 * frames, dtype=jnp.int32)
    frame, back = pair // 4, pair % 4
    held = (frame - back) >= jnp.repeat(first, 4)
    rank = jnp.sum((held[None, :] & (pair[None, :] < pair[:, None])).astype(jnp.int32), axis=1)
    slot = jnp.where(held, rank, SLOTS)
    hit = slot[None, :] == jnp.arange(SLOTS, dtype=jnp.int32)[:, None]
    query = jnp.sum(jnp.where(hit, frame[None, :], 0), axis=1)
    key = jnp.sum(jnp.where(hit, (frame - back)[None, :], 0), axis=1)
    grid = slot.reshape(frames, 4)
    columns = [
        jnp.concatenate([grid[way:, way], jnp.full((way,), SLOTS, jnp.int32)]) for way in range(4)
    ]
    same = (query == key).astype(jnp.int32)
    return jnp.concatenate([query, key, slot, jnp.stack(columns, axis=1).reshape(-1), same])


def per_device(
    hidden_in,
    frame_cond,
    query_weight,
    key_weight,
    value_weight,
    output_weight,
    up_weight,
    down_weight,
    modulation_weight,
    clip_lengths,
    patch_valid,
    cotangent,
):
    tok_dev, model_width = hidden_in.shape
    group_tokens = patch_valid.shape[0]
    frames = group_tokens // PATCHES
    head_index = lax.axis_index("head")
    n_dp = lax.axis_size("dp")
    frame = jnp.arange(frames, dtype=jnp.int32)
    ends = jnp.cumsum(clip_lengths[0])
    first_frames = jnp.max(
        jnp.where(ends[None, :] <= frame[:, None], ends[None, :], 0), axis=1
    ).astype(jnp.int32)
    angles = (frame - first_frames).astype(jnp.float32)[:, None] * frequencies(HEAD_DIM // 2)[None]
    cosine, sine = jnp.cos(angles), jnp.sin(angles)
    cosines = jnp.concatenate([cosine] * 4, axis=1)
    sines = jnp.concatenate([-sine, sine] * 2, axis=1)
    rope = jnp.stack([cosines, sines], axis=1)
    rope_back = jnp.stack([cosines, -sines], axis=1)
    local_valid = lax.dynamic_slice_in_dim(patch_valid, head_index * tok_dev, tok_dev)
    cond_value = frame_cond.astype(jnp.float32)
    cond_act = jax.nn.silu(cond_value).astype(jnp.bfloat16)
    modulation = jnp.dot(cond_act, modulation_weight, preferred_element_type=jnp.float32).reshape(
        6, model_width
    )
    normed_one, head_query, head_key, head_value = front_part(
        hidden_in,
        modulation[:2],
        lax.dynamic_index_in_dim(rope, head_index, 0, keepdims=False),
        query_weight,
        key_weight,
        value_weight,
    )
    bias = jnp.broadcast_to(
        jnp.where(patch_valid == 1, 0.0, MASKED).astype(jnp.float32)[:, None],
        (group_tokens, 128),
    )
    attended, logsum = attend_forward(
        first_frames,
        *[array.reshape(group_tokens, 128) for array in (head_query, head_key, head_value)],
        bias,
    )
    results = back_part(
        n_dp,
        (
            slot_table(first_frames, frames),
            attended,
            logsum,
            hidden_in,
            cotangent,
            modulation,
            rope_back,
            jnp.concatenate([cond_act.astype(jnp.float32), cond_value], axis=0),
            jnp.broadcast_to(local_valid.astype(jnp.float32)[:, None], (tok_dev, 128)),
        ),
        (
            head_query,
            head_key,
            head_value,
            bias.reshape(frames, PATCHES, 128),
            normed_one,
            output_weight,
            up_weight,
            down_weight,
            query_weight,
            key_weight,
            value_weight,
            modulation_weight,
        ),
    )
    (block_out, grad_input, statistics, gq, gk, gv, go, gup, gdown, gmod, gcond, _) = results
    return (
        block_out,
        grad_input,
        gcond,
        gq,
        gk,
        gv,
        go,
        gup,
        gdown,
        gmod,
        statistics[:1, :3],
    )


def solution(mesh):
    in_specs = (
        P(("dp", "head"), None),
        P(("dp", "head"), None),
        P(),
        P(),
        P(),
        P(),
        P(),
        P(),
        P(),
        P("dp", None),
        P("dp"),
        P(("dp", "head"), None),
    )
    out_specs = (
        P(("dp", "head"), None),
        P(("dp", "head"), None),
        P(("dp", "head"), None),
        P(("dp", "head"), None),
        P(("dp", "head"), None),
        P(("dp", "head"), None),
        P(("dp", "head"), None),
        P(("dp", "head"), None),
        P(("dp", "head"), None),
        P(("dp", "head"), None),
        P(("dp", "head"), None),
    )
    return jax.shard_map(
        per_device, mesh=mesh, in_specs=in_specs, out_specs=out_specs, check_vma=False
    )
```

```python
import math

import jax
import jax.numpy as jnp
from jax import lax
from jax.experimental import pallas as pl
from jax.experimental.pallas import tpu as pltpu
from jax.sharding import PartitionSpec as P

HEADS = 16
HEAD_DIM = 64
PATCHES = 256


EPSILON = 1e-06
MASKED = -1e30


def frequencies(half_dim):
    return jnp.exp(jnp.arange(half_dim, dtype=jnp.float32) * (-math.log(10000.0) / half_dim))


def dot_nt(left, right):
    return lax.dot_general(
        left, right, (((1,), (1,)), ((), ())), preferred_element_type=jnp.float32
    )


def dot_nn(left, right):
    return lax.dot_general(
        left, right, (((1,), (0,)), ((), ())), preferred_element_type=jnp.float32
    )


def head_parts(block):
    lane = lax.broadcasted_iota(jnp.int32, block.shape, 1)
    zero = jnp.zeros_like(block)
    return jnp.where(lane < HEAD_DIM, block, zero), jnp.where(lane < HEAD_DIM, zero, block)


def key_bias(bias_ref, key_frame, frame):
    half = bias_ref[pl.ds(key_frame * PATCHES, PATCHES), :]
    bias = jnp.concatenate([half, half], axis=1)
    row = lax.broadcasted_iota(jnp.int32, bias.shape, 0)
    column = lax.broadcasted_iota(jnp.int32, bias.shape, 1)
    own = (row == column) & (key_frame == frame)
    return jnp.where(own, 0.0, bias)


def attend_forward_kernel(first_ref, q_ref, k_ref, v_ref, bias_ref, o_ref, lse_ref, scores):
    frames = q_ref.shape[0] // PATCHES

    def one_frame(frame, _):
        rows = pl.ds(frame * PATCHES, PATCHES)
        parts = head_parts(q_ref[rows, :] * jnp.bfloat16(0.125))
        first = first_ref[frame]

        def score(key_frame, tops):
            keys = k_ref[pl.ds(key_frame * PATCHES, PATCHES), :]
            bias = key_bias(bias_ref, key_frame, frame)
            new = []
            for head in range(2):
                value = dot_nt(keys, parts[head]) + bias
                scores[head, key_frame - first] = value
                new.append(jnp.maximum(tops[head], jnp.max(value, axis=0, keepdims=True)))
            return tuple(new)

        low = jnp.full((1, PATCHES), MASKED, jnp.float32)
        tops = lax.fori_loop(first, frame + 1, score, (low, low))

        def exponent(key_frame, totals):
            new = []
            for head in range(2):
                value = jnp.exp(scores[head, key_frame - first] - tops[head])
                scores[head, key_frame - first] = value
                new.append(totals[head] + jnp.sum(value, axis=0, keepdims=True))
            return tuple(new)

        zero = jnp.zeros((1, PATCHES), jnp.float32)
        totals = lax.fori_loop(first, frame + 1, exponent, (zero, zero))
        inverse = [1.0 / total for total in totals]

        def weigh(key_frame, sums):
            turned = v_ref[pl.ds(key_frame * PATCHES, PATCHES), :].T
            new = []
            for head in range(2):
                probs = (scores[head, key_frame - first] * inverse[head]).astype(jnp.bfloat16)
                new.append(
                    sums[head]
                    + dot_nn(turned[head * HEAD_DIM : (head + 1) * HEAD_DIM, :], probs)
                )
            return tuple(new)

        empty = jnp.zeros((HEAD_DIM, PATCHES), jnp.float32)
        sums = lax.fori_loop(first, frame + 1, weigh, (empty, empty))
        o_ref[rows, :] = jnp.concatenate(sums, axis=0).T.astype(jnp.bfloat16)
        for head in range(2):
            lse_ref[frame, head : head + 1, :] = tops[head] + jnp.log(totals[head])
        return 0

    lax.fori_loop(0, frames, one_frame, 0)


IN_SMEM = pl.BlockSpec(memory_space=pltpu.SMEM)
IN_VMEM = pl.BlockSpec(memory_space=pltpu.VMEM)
IN_PLACE = pl.BlockSpec(memory_space=pl.ANY)
MESH_ID = pl.DeviceIdType.MESH


def attend_forward(first, queries, keys, values, bias):
    tokens, width = queries.shape
    frames = tokens // PATCHES
    return pl.pallas_call(
        attend_forward_kernel,
        out_shape=(
            jax.ShapeDtypeStruct((tokens, width), jnp.bfloat16),
            jax.ShapeDtypeStruct((frames, 2, PATCHES), jnp.float32),
        ),
        in_specs=[IN_SMEM] + [IN_VMEM] * 4,
        out_specs=(IN_VMEM, IN_VMEM),
        scratch_shapes=[pltpu.VMEM((2, 4, PATCHES, PATCHES), jnp.float32)],
        name="attend_forward",
    )(first, queries, keys, values, bias)


SLOTS = 17
BLOCK = 256


def peer_head(head, flips):
    core = lax.rem(head, 2)
    second = lax.rem(lax.div(head, 2), 2)
    third = lax.div(head, 4)
    if flips % 2:
        core = 1 - core
    if flips // 2 % 2:
        second = 1 - second
    if flips // 4:
        third = 1 - third
    return 4 * third + 2 * second + core


def remote(source, target, send, receive, where):
    return pltpu.make_async_remote_copy(
        src_ref=source,
        dst_ref=target,
        send_sem=send,
        recv_sem=receive,
        device_id=where,
        device_id_type=MESH_ID,
    )


def gelu_and_slope(value):
    square = value * value
    inner = 0.7978845608028654 * value * (1.0 + 0.044715 * square)
    bend = jnp.tanh(inner)
    half = 0.5 * (1.0 + bend)
    slope = half + 0.5 * value * (1.0 - bend * bend) * (
        0.7978845608028654 * (1.0 + 0.134145 * square)
    )
    return value * half, slope


def turn_pairs(values, _):
    lane = lax.rem(lax.broadcasted_iota(jnp.int32, values.shape, 1), HEAD_DIM)
    up = pltpu.roll(values, 128 - HEAD_DIM // 2, 1)
    down = pltpu.roll(values, HEAD_DIM // 2, 1)
    return jnp.where(lane < HEAD_DIM // 2, up, down)


def back_kernel(n_dp, *refs):
    (
        table,
        att_own,
        lse_ref,
        x_ref,
        cot_ref,
        mod_ref,
        rope_ref,
        cond_ref,
        valid_ref,
        q_hbm,
        k_hbm,
        v_hbm,
        bias_hbm,
        n1_hbm,
        wo_hbm,
        up_hbm,
        down_hbm,
        wq_hbm,
        wk_hbm,
        wv_hbm,
        wmod_hbm,
        block_hbm,
        gin_ref,
        stat_ref,
        gq_ref,
        gk_ref,
        gv_ref,
        go_ref,
        gup_ref,
        gdown_ref,
        gmod_hbm,
        gcond_ref,
        n1_all,
        att_fr,
        do_own,
        from_core,
        from_first,
        from_second,
        from_dp,
        core_out,
        da_send,
        lhs,
        dmlp,
        dhid,
        dattn,
        mid,
        rows_ref,
        z_send,
        z_recv,
        p_send,
        p_recv,
        load_sem,
        a2a_send,
        a2a_recv,
        core_send,
        core_recv,
        first_send,
        first_recv,
        second_send,
        second_recv,
        dp_send,
        dp_recv,
        row_send,
        row_recv,
        row_dp_send,
        row_dp_recv,
        gather_send,
        gather_recv,
        z_send_sem,
        z_recv_sem,
        mod_sem,
    ) = refs
    tokens, width = x_ref.shape
    frames = q_hbm.shape[0]
    hidden_width = up_hbm.shape[1]
    tiles = hidden_width // width
    chunks = width // BLOCK
    small = width // (n_dp * 8)
    large = hidden_width // (n_dp * 8)
    half_rows = n_dp * 4 * small
    group = lax.axis_index("dp")
    head = lax.axis_index("head")
    core = lax.rem(head, 2)
    xbit = lax.rem(lax.div(head, 2), 2)
    ybit = lax.div(head, 4)
    core_peer, x_peer, y_peer = peer_head(head, 1), peer_head(head, 2), peer_head(head, 4)
    dp_peers = [lax.rem(group + hop, n_dp) for hop in range(1, n_dp)]
    others = range(1, 8)

    barrier = pltpu.get_barrier_semaphore()
    for flips in others:
        pl.semaphore_signal(
            barrier, inc=1, device_id=(group, peer_head(head, flips)), device_id_type=MESH_ID
        )
    for peer in dp_peers:
        pl.semaphore_signal(barrier, inc=1, device_id=(peer, head), device_id_type=MESH_ID)

    pl.semaphore_wait(barrier, 7 + len(dp_peers))

    own_rows = pl.ds(head * tokens, tokens)
    own_lanes = pl.ds(head * 128, 128)

    def att_copy(flips):
        peer = peer_head(head, flips)
        return remote(
            att_own.at[pl.ds(peer * tokens, tokens), :],
            att_fr.at[:, own_lanes],
            a2a_send.at[0, flips],
            a2a_recv.at[0, flips],
            (group, peer),
        )

    def grad_copy(flips):
        peer = peer_head(head, flips)
        return remote(
            da_send.at[:, pl.ds(peer * 128, 128)],
            do_own.at[head],
            a2a_send.at[1, flips],
            a2a_recv.at[1, flips],
            (group, peer),
        )

    first_up = large // small
    first_out = first_up + tiles
    count = first_out + 3

    def slot_of(unit):
        return unit

    def lhs_of(unit):
        if unit < first_up:
            return unit
        return first_up if unit < first_out else first_up + 1

    def core_copy(unit):
        return remote(
            core_out.at[unit % 2],
            from_core.at[slot_of(unit)],
            core_send.at[unit],
            core_recv.at[unit],
            (group, core_peer),
        )

    def x_leads(unit):
        return unit % 2 == 0

    def first_copy(unit):
        slot = slot_of(unit)
        if x_leads(unit):
            source, peer = from_core.at[slot, :, :, 1 - xbit], x_peer
        else:
            source, peer = from_core.at[slot, :, 1 - ybit], y_peer
        return remote(
            source, from_first.at[slot], first_send.at[unit], first_recv.at[unit], (group, peer)
        )

    def second_copy(unit):
        slot = slot_of(unit)
        if x_leads(unit):
            source, peer = from_core.at[slot, :, 1 - ybit, xbit], y_peer
        else:
            source, peer = from_core.at[slot, :, ybit, 1 - xbit], x_peer
        return remote(
            source, from_second.at[slot], second_send.at[unit], second_recv.at[unit], (group, peer)
        )

    def dp_copy(unit, hop):
        peer = dp_peers[hop]
        return remote(
            from_core.at[slot_of(unit), peer, ybit, xbit],
            from_dp.at[unit, hop],
            dp_send.at[unit, hop],
            dp_recv.at[unit, hop],
            (peer, head),
        )

    def added(left, right):
        return (left.astype(jnp.float32) + right.astype(jnp.float32)).astype(jnp.bfloat16)

    def put(target, lanes, value, unit):
        value = value.astype(jnp.bfloat16)
        if unit <= first_out:
            target[:, :, :, :, lanes] = value.reshape(n_dp, 2, 2, small, BLOCK)
        else:
            value = value.reshape(4, n_dp, small, BLOCK)
            for chip in range(4):
                target[:, chip // 2, chip % 2, :, lanes] = value[chip]

    def got(source, lanes, unit):
        if unit <= first_out:
            return source[:, :, :, :, lanes].reshape(half_rows, BLOCK)
        return jnp.concatenate(
            [
                source[:, chip // 2, chip % 2, :, lanes].reshape(half_rows // 4, BLOCK)
                for chip in range(4)
            ],
            axis=0,
        )

    def produce(unit, product):
        if unit >= 2:
            core_copy(unit - 2).wait_send()

        def body(chunk, _):
            lanes = pl.ds(pl.multiple_of(chunk * BLOCK, BLOCK), BLOCK)
            put(core_out.at[unit % 2], lanes, product(unit, 1 - core, chunk), unit)
            return 0

        lax.fori_loop(0, chunks, body, 0)
        core_copy(unit).start()

    def take_core(unit, product):
        core_copy(unit).wait_recv()
        place = from_core.at[slot_of(unit)]

        def body(chunk, _):
            lanes = pl.ds(pl.multiple_of(chunk * BLOCK, BLOCK), BLOCK)
            value = product(unit, core, chunk) + got(place, lanes, unit).astype(jnp.float32)
            put(place, lanes, value, unit)
            return 0

        lax.fori_loop(0, chunks, body, 0)
        first_copy(unit).start()

    def take_first(unit):
        first_copy(unit).wait()
        slot = slot_of(unit)

        def body(index, _):
            at_dp = lax.div(index, 2)
            other = lax.rem(index, 2)
            at_y, at_x = (other, xbit) if x_leads(unit) else (ybit, other)
            from_core[slot, at_dp, at_y, at_x] = added(
                from_core[slot, at_dp, at_y, at_x], from_first[slot, at_dp, other]
            )
            return 0

        lax.fori_loop(0, n_dp * 2, body, 0)
        second_copy(unit).start()

    def take_second(unit):
        second_copy(unit).wait()
        slot = slot_of(unit)

        def body(at_dp, _):
            from_core[slot, at_dp, ybit, xbit] = added(
                from_core[slot, at_dp, ybit, xbit], from_second[slot, at_dp]
            )
            return 0

        lax.fori_loop(0, n_dp, body, 0)
        for hop in range(n_dp - 1):
            dp_copy(unit, hop).start()

    def take_dp(unit):
        for hop in range(n_dp - 1):
            dp_copy(unit, hop).wait()
        total = from_core[slot_of(unit), group, ybit, xbit].astype(jnp.float32)
        for hop in range(n_dp - 1):
            total = total + from_dp[unit, hop].astype(jnp.float32)
        if unit < first_up:
            gdown_ref[unit * small : (unit + 1) * small, :] = total
        elif unit < first_out:
            place = (unit - first_up) * width
            gup_ref[:, place : place + width] = total
        else:
            go_ref[...] = total

    def turned_rows(index, source):
        for chunk in range(chunks):
            value = source[:, chunk * BLOCK : (chunk + 1) * BLOCK].T
            value = value.reshape(BLOCK // (2 * small), 2, small, tokens)
            for side in range(2):
                lhs[index, side, chunk * BLOCK // 2 : (chunk + 1) * BLOCK // 2, :] = value[
                    :, side
                ].reshape(BLOCK // 2, tokens)

    shift_one, scale_one, gate_one = (mod_ref[row : row + 1, :] for row in range(3))
    shift_two, scale_two, gate_two = (mod_ref[row : row + 1, :] for row in range(3, 6))
    step_rows = 32
    steps = tokens // step_rows

    def row_block(index):
        return pl.ds(pl.multiple_of(index * step_rows, step_rows), step_rows)

    def lane_block(chunk):
        return pl.ds(pl.multiple_of(chunk * BLOCK, BLOCK), BLOCK)

    def masked_square(values, rows):
        sums = jnp.sum(values * values, axis=1, keepdims=True) * valid_ref[rows, :1]
        return jnp.sum(sums, axis=0, keepdims=True)

    one = jnp.zeros((1, 1), jnp.float32)
    row_zero = jnp.zeros((1, width), jnp.float32)

    for flips in others:
        att_copy(flips).start()
    att_fr[:, own_lanes] = att_own[own_rows, :]

    def weight_product(unit, side, chunk):
        if unit < first_up:
            right = dmlp[:, lane_block(chunk)]
        elif unit < first_out:
            start = (unit - first_up) * width + chunk * BLOCK
            right = dhid[:, pl.ds(pl.multiple_of(start, BLOCK), BLOCK)]
        else:
            right = dattn[:, lane_block(chunk)]
        return dot_nn(lhs[lhs_of(unit), side], right)

    def run_plan(point, product=weight_product):
        for kind, unit in PLAN.get(point, ()):
            if kind == "P":
                produce(unit, product)
            elif kind == "C":
                take_core(unit, product)
            elif kind == "F":
                take_first(unit)
            elif kind == "S":
                take_second(unit)
            else:
                take_dp(unit)

    half = tokens // 2
    low, high = pl.ds(0, half), pl.ds(half, half)

    def gather_copy(index):
        if index == 0:
            source, target, peer = n1_hbm.at[low], n1_all.at[head, low], x_peer
        elif index == 1:
            source, target, peer = n1_hbm.at[high], n1_all.at[head, high], y_peer
        elif index == 2:
            source, target, peer = n1_hbm.at[low], n1_all.at[head, low], y_peer
        elif index == 3:
            source, target, peer = n1_all.at[x_peer, low], n1_all.at[x_peer, low], y_peer
        elif index == 4:
            source, target, peer = n1_hbm.at[high], n1_all.at[head, high], x_peer
        elif index == 5:
            source, target, peer = n1_all.at[y_peer, high], n1_all.at[y_peer, high], x_peer
        elif index == 6:
            source, target, peer = n1_hbm, n1_all.at[head], core_peer
        else:
            block = peer_head(head, 2 * (index - 6))
            source, target, peer = n1_all.at[block], n1_all.at[block], core_peer
        return remote(
            source, target, gather_send.at[index], gather_recv.at[index], (group, peer)
        )

    def mlp_part(up, down, act, dn2, wo, ba, n2):
        wo_load = pltpu.make_async_copy(wo_hbm, wo, load_sem.at[0])
        wo_load.start()
        up_loads = [
            pltpu.make_async_copy(
                up_hbm.at[:, pl.ds(tile * width, width)],
                up.at[:, pl.ds(tile * width, width)],
                load_sem.at[1 + tile],
            )
            for tile in range(tiles)
        ]
        down_loads = [
            pltpu.make_async_copy(
                down_hbm.at[pl.ds(tile * width, width), :],
                down.at[pl.ds(tile * width, width), :],
                load_sem.at[1 + tiles + tile],
            )
            for tile in range(tiles)
        ]
        for tile in range(tiles):
            up_loads[tile].start()
            down_loads[tile].start()

        wo_load.wait()
        for flips in others:
            att_copy(flips).wait()
        for index in (0, 1, 6):
            gather_copy(index).start()
        turned_rows(first_up + 1, att_fr)

        def project(chunk, _):
            lanes = lane_block(chunk)
            ba[:, lanes] = dot_nn(att_fr[...], wo[:, lanes])
            return 0

        lax.fori_loop(0, chunks, project, 0)

        def second_norm(index, total):
            rows = row_block(index)
            branch = gate_one * ba[rows, :]
            value = x_ref[rows, :].astype(jnp.float32) + branch
            mid[rows, :] = value
            scale = lax.rsqrt(jnp.mean(value * value, axis=1, keepdims=True) + EPSILON)
            n2[rows, :] = (value * scale * (1.0 + scale_two) + shift_two).astype(jnp.bfloat16)
            dmlp[rows, :] = (gate_two * cot_ref[rows, :].astype(jnp.float32)).astype(jnp.bfloat16)
            return total + masked_square(branch, rows)

        stat_attn = lax.fori_loop(0, steps, second_norm, one)
        turned_rows(first_up, n2)

        pairs = BLOCK // (2 * large)

        def feed(index, _):
            @pl.when(lax.rem(index, chunks) == 0)
            def _():
                tile = lax.div(index, chunks)
                pltpu.make_async_copy(
                    up_hbm.at[:, pl.ds(0, width)],
                    up.at[:, pl.ds(0, width)],
                    load_sem.at[1 + tile],
                ).wait()
                pltpu.make_async_copy(
                    down_hbm.at[pl.ds(0, width), :],
                    down.at[pl.ds(0, width), :],
                    load_sem.at[1 + tiles + tile],
                ).wait()

            @pl.when(index == GATHER_AT)
            def _():
                for step in (0, 1):
                    gather_copy(step).wait()
                for step in (2, 3, 4, 5):
                    gather_copy(step).start()

            lanes = lane_block(index)
            active, slope = gelu_and_slope(dot_nn(n2[...], up[:, lanes]))
            active = active.astype(jnp.bfloat16)
            act[:, lanes] = active
            grad = dot_nt(dmlp[...], down[lanes, :])
            dhid[:, lanes] = (grad * slope).astype(jnp.bfloat16)
            turned = active.T.reshape(pairs, 2, first_up, small, tokens)
            where = pl.ds(pl.multiple_of(index * pairs * small, pairs * small), pairs * small)
            for unit in range(first_up):
                for side in range(2):
                    lhs[unit, side, where, :] = turned[:, side, unit].reshape(
                        pairs * small, tokens
                    )
            return 0

        lax.fori_loop(0, hidden_width // BLOCK, feed, 0)

        run_plan("fed")

        def to_normed(chunk, _):
            lanes = lane_block(chunk)
            dn2[:, lanes] = dot_nt(dhid[...], up[lanes, :])
            return 0

        lax.fori_loop(0, chunks, to_normed, 0)
        run_plan("normed")

        def second_norm_back(index, sums):
            shift_sum, scale_sum, gate_sum = sums
            rows = row_block(index)
            value = mid[rows, :]
            scale = lax.rsqrt(jnp.mean(value * value, axis=1, keepdims=True) + EPSILON)
            normed = value * scale
            grad = dn2[rows, :]
            shift_sum = shift_sum + jnp.sum(grad, axis=0, keepdims=True)
            scale_sum = scale_sum + jnp.sum(grad * normed, axis=0, keepdims=True)
            inner = grad * (1.0 + scale_two)
            mean = jnp.mean(inner * normed, axis=1, keepdims=True)
            total = cot_ref[rows, :].astype(jnp.float32) + scale * (inner - normed * mean)
            dn2[rows, :] = total
            gate_sum = gate_sum + jnp.sum(total * ba[rows, :], axis=0, keepdims=True)
            dattn[rows, :] = (gate_one * total).astype(jnp.bfloat16)
            return shift_sum, scale_sum, gate_sum

        shift_two_grad, scale_two_grad, gate_one_grad = lax.fori_loop(
            0, steps, second_norm_back, (row_zero, row_zero, row_zero)
        )

        def to_attended(chunk, _):
            lanes = lane_block(chunk)
            da_send[:, lanes] = dot_nt(dattn[...], wo[lanes, :]).astype(jnp.bfloat16)
            return 0

        lax.fori_loop(0, chunks, to_attended, 0)
        for flips in others:
            grad_copy(flips).start()
        do_own[head] = da_send[:, own_lanes]

        run_plan("attended")

        def branch_out(chunk, _):
            lanes = lane_block(chunk)
            ba[:, lanes] = dot_nn(act[...], down[:, lanes])
            return 0

        lax.fori_loop(0, chunks, branch_out, 0)
        run_plan("branch")

        def outputs(index, sums):
            gate_sum, stat_mlp, stat_out = sums
            rows = row_block(index)
            raw = ba[rows, :]
            branch = gate_two * raw
            value = mid[rows, :] + branch
            n2[rows, :] = value.astype(jnp.bfloat16)
            gate_sum = gate_sum + jnp.sum(
                cot_ref[rows, :].astype(jnp.float32) * raw, axis=0, keepdims=True
            )
            stat_mlp = stat_mlp + masked_square(branch, rows)
            stat_out = stat_out + masked_square(value, rows)
            mid[rows, :] = dn2[rows, :]
            return gate_sum, stat_mlp, stat_out

        gate_two_grad, stat_mlp, stat_out = lax.fori_loop(0, steps, outputs, (row_zero, one, one))
        lane = lax.broadcasted_iota(jnp.int32, stat_ref.shape, 1)
        stats = jnp.where(lane == 0, stat_attn, jnp.where(lane == 1, stat_mlp, stat_out))
        stat_ref[...] = jnp.sqrt(stats / (tokens * width) + EPSILON)
        for row, vector in (
            (3, gate_one_grad),
            (4, shift_two_grad),
            (5, scale_two_grad),
            (6, gate_two_grad),
        ):
            gin_ref[row : row + 1, :] = vector
        block_copy = pltpu.make_async_copy(n2, block_hbm, load_sem.at[0])
        block_copy.start()
        run_plan("outputs")
        block_copy.wait()

    pl.run_scoped(
        mlp_part,
        pltpu.VMEM((width, hidden_width), jnp.bfloat16),
        pltpu.VMEM((hidden_width, width), jnp.bfloat16),
        pltpu.VMEM((tokens, hidden_width), jnp.bfloat16),
        pltpu.VMEM((tokens, width), jnp.float32),
        pltpu.VMEM((width, width), jnp.bfloat16),
        pltpu.VMEM((tokens, width), jnp.float32),
        pltpu.VMEM((tokens, width), jnp.bfloat16),
    )
    saved_rows = [gin_ref[row : row + 1, :] for row in range(3, 7)]

    def attention_part(
        q_ref,
        k_ref,
        v_ref,
        bias_ref,
        n1_group,
        w_own,
        dq_slots,
        dk_slots,
        dv_slots,
        deltas,
        d_all,
        d_turned,
        dn1,
        cond_sum,
    ):
        pieces = [
            (q_hbm, q_ref),
            (k_hbm, k_ref),
            (v_hbm, v_ref),
            (bias_hbm, bias_ref),
            (wq_hbm.at[:, own_lanes], w_own.at[:, pl.ds(0, 128)]),
            (wk_hbm.at[:, own_lanes], w_own.at[:, pl.ds(128, 128)]),
            (wv_hbm.at[:, own_lanes], w_own.at[:, pl.ds(256, 128)]),
        ]
        loads = [
            pltpu.make_async_copy(source, target, load_sem.at[1 + place])
            for place, (source, target) in enumerate(pieces)
        ]
        for copy in loads:
            copy.start()

        pages = frames // 2

        class mod_load:
            def __init__(self, block):
                self.copies = [
                    pltpu.make_async_copy(
                        wmod_hbm.at[pl.ds(page * tokens, tokens), pl.ds(block * width, width)],
                        n1_group.at[block % 2 * pages + page],
                        mod_sem.at[block, page],
                    )
                    for page in range(pages)
                ]

            def start(self):
                for copy in self.copies:
                    copy.start()

            def wait(self):
                for copy in self.copies:
                    copy.wait()

        run_plan("scope")
        for step in (2, 3, 4, 5):
            gather_copy(step).wait()
        for step in (7, 8, 9):
            gather_copy(step).start()
        for flips in others:
            grad_copy(flips).wait()
        for copy in loads:
            copy.wait()
        for slots in (dq_slots, dk_slots, dv_slots):
            slots[SLOTS] = jnp.zeros(slots.shape[1:], jnp.float32)

        def frame_delta(frame, _):
            rows = pl.ds(pl.multiple_of(frame * tokens, tokens), tokens)
            product = (
                do_own[frame].astype(jnp.float32) * att_own[rows, :].astype(jnp.float32)
            ).T
            for part in range(2):
                deltas[frame, part : part + 1, :] = jnp.sum(
                    product[part * HEAD_DIM : (part + 1) * HEAD_DIM, :], axis=0, keepdims=True
                )
            return 0

        lax.fori_loop(0, frames, frame_delta, 0)

        def one_slot(index, _):
            frame = table[index]
            key_frame = table[SLOTS + index]
            q_parts = head_parts(q_ref[frame] * jnp.bfloat16(0.125))
            do_parts = head_parts(do_own[frame])
            keys = k_ref[key_frame]
            values = v_ref[key_frame]
            turned = keys.T
            half = bias_ref[key_frame]
            row = lax.broadcasted_iota(jnp.int32, (tokens, tokens), 0)
            column = lax.broadcasted_iota(jnp.int32, (tokens, tokens), 1)
            same = table[2 * SLOTS + 8 * frames + index].astype(jnp.float32)
            keep = 1.0 - jnp.where(row == column, 1.0, 0.0) * same
            bias = jnp.concatenate([half, half], axis=1) * keep
            dv = dk = None
            dq = []
            for part in range(2):
                lse = lse_ref[frame, part : part + 1, :]
                delta = deltas[frame, part : part + 1, :]
                probs = jnp.exp(dot_nt(keys, q_parts[part]) + bias - lse)
                prob_grad = dot_nt(values, do_parts[part])
                score_grad = (probs * (prob_grad - delta)).astype(jnp.bfloat16)
                dv_part = dot_nn(probs.astype(jnp.bfloat16), do_parts[part])
                dk_part = dot_nn(score_grad, q_parts[part])
                dv = dv_part if dv is None else dv + dv_part
                dk = dk_part if dk is None else dk + dk_part
                dq.append(
                    dot_nn(turned[part * HEAD_DIM : (part + 1) * HEAD_DIM, :], score_grad)
                )
            dv_slots[index] = dv
            dk_slots[index] = dk
            dq_slots[index] = jnp.concatenate(dq, axis=0)
            for place in range(SLOTS):
                if PLAN.get(place):
                    pl.when(index == place)(lambda place=place: run_plan(place))
            return 0

        lax.fori_loop(0, SLOTS, one_slot, 0)

        def summed(slots, start, frame):
            total = slots[table[start + 4 * frame]]
            for way in range(1, 4):
                total = total + slots[table[start + 4 * frame + way]]
            return total

        def combine(frame, _):
            side, chip = lax.rem(frame, 2), lax.div(frame, 2)
            cosine = rope_ref[frame, 0:1, :]
            sine = rope_ref[frame, 1:2, :]

            def turned_back(value):
                value = value.astype(jnp.bfloat16).astype(jnp.float32)
                return (value * cosine + turn_pairs(value, None) * sine).astype(jnp.bfloat16)

            start = 2 * SLOTS + 4 * frames
            parts = (
                turned_back(summed(dq_slots, 2 * SLOTS, frame).T * 0.125),
                turned_back(summed(dk_slots, start, frame)),
                summed(dv_slots, start, frame).astype(jnp.bfloat16),
            )
            where = pl.ds(pl.multiple_of(frame * tokens, tokens), tokens)
            for place, part in enumerate(parts):
                d_all[side, chip, :, place * 128 : (place + 1) * 128] = part
                d_turned[place * 128 : (place + 1) * 128, where] = part.T
            return 0

        lax.fori_loop(0, frames, combine, 0)

        def normed_product(unit, side, chunk):
            first = (unit - first_out - 1) * half
            left = d_all[side, :, first : first + half, :].reshape(half_rows, 384)
            return dot_nt(left, w_own[lane_block(chunk), :])

        def normed_plan(point):
            run_plan(
                point,
                lambda unit, *where: (normed_product if unit > first_out else weight_product)(
                    unit, *where
                ),
            )

        for step in (6, 7, 8, 9):
            gather_copy(step).wait()
        group_loads = [
            pltpu.make_async_copy(n1_hbm, n1_group.at[head], load_sem.at[0])
        ] + [
            pltpu.make_async_copy(
                n1_all.at[peer_head(head, flips)],
                n1_group.at[peer_head(head, flips)],
                load_sem.at[flips],
            )
            for flips in others
        ]
        for copy in group_loads:
            copy.start()
        normed_plan("combined")
        for copy in group_loads:
            copy.wait()

        piece = width // n_dp

        def own_columns(chunk, _):
            right = n1_group[:, :, lane_block(chunk)].reshape(frames * tokens, BLOCK)
            value = dot_nn(d_turned[...], right).astype(jnp.bfloat16)
            for part in range(BLOCK // piece):
                z_send[chunk * (BLOCK // piece) + part] = value[
                    :, part * piece : (part + 1) * piece
                ]
            return 0

        lax.fori_loop(0, chunks, own_columns, 0)
        mod_load(2).start()
        mod_load(3).start()
        z_copies = [
            remote(
                z_send.at[dp_peers[hop]],
                z_recv.at[hop],
                z_send_sem.at[hop],
                z_recv_sem.at[hop],
                (dp_peers[hop], head),
            )
            for hop in range(n_dp - 1)
        ]
        for copy in z_copies:
            copy.start()
        normed_plan("columns")

        def cond_block(block, vector, first):
            vector = vector.astype(jnp.bfloat16).astype(jnp.float32)

            def body(index, _):
                rows = pl.ds(pl.multiple_of(index * 64, 64), 64)
                page = block % 2 * pages + lax.div(index, tokens // 64)
                inside = pl.ds(pl.multiple_of(lax.rem(index, tokens // 64) * 64, 64), 64)
                total = jnp.zeros((64, 128), jnp.float32) if first else cond_sum[rows, :]
                for lanes in range(0, width, 128):
                    total = total + n1_group[page, inside, lanes : lanes + 128].astype(
                        jnp.float32
                    ) * vector[:, lanes : lanes + 128]
                cond_sum[rows, :] = total
                return 0

            lax.fori_loop(0, width // 64, body, 0)

        mod_load(2).wait()
        cond_block(2, saved_rows[0], True)
        mod_load(4).start()
        mod_load(3).wait()
        cond_block(3, saved_rows[1], False)
        mod_load(5).start()
        normed_plan("cond1")
        mod_load(4).wait()
        cond_block(4, saved_rows[2], False)
        mod_load(0).start()
        mod_load(5).wait()
        cond_block(5, saved_rows[3], False)
        mod_load(1).start()
        normed_plan("cond2")

        for copy in z_copies:
            copy.wait()
        total = z_send[group].astype(jnp.float32)
        for hop in range(n_dp - 1):
            total = total + z_recv[hop].astype(jnp.float32)
        p_send[...] = total.T.reshape(8, small, 384)

        def part_copy(flips):
            peer = peer_head(head, flips)
            return remote(
                p_send.at[peer],
                p_recv.at[head],
                a2a_send.at[2, flips],
                a2a_recv.at[2, flips],
                (group, peer),
            )

        for flips in others:
            part_copy(flips).start()
        p_recv[head] = p_send[head]

        for unit in (first_out + 1, first_out + 2):
            second_copy(unit).wait()
            value = from_core[slot_of(unit), :, ybit, xbit].astype(jnp.float32)
            value = value + from_second[slot_of(unit)].astype(jnp.float32)
            first = (unit - first_out - 1) * half
            dn1[first : first + half, :] = value.reshape(half, width)

        def first_norm_back(index, sums):
            shift_sum, scale_sum = sums
            rows = row_block(index)
            value = x_ref[rows, :].astype(jnp.float32)
            scale = lax.rsqrt(jnp.mean(value * value, axis=1, keepdims=True) + EPSILON)
            normed = value * scale
            grad = dn1[rows, :]
            shift_sum = shift_sum + jnp.sum(grad, axis=0, keepdims=True)
            scale_sum = scale_sum + jnp.sum(grad * normed, axis=0, keepdims=True)
            inner = grad * (1.0 + scale_one)
            mean = jnp.mean(inner * normed, axis=1, keepdims=True)
            gin_ref[rows, :] = mid[rows, :] + scale * (inner - normed * mean)
            return shift_sum, scale_sum

        shift_one_grad, scale_one_grad = lax.fori_loop(
            0, steps, first_norm_back, (row_zero, row_zero)
        )
        vectors = jnp.concatenate(
            [
                cond_ref[0:1, :],
                shift_one_grad,
                scale_one_grad,
                *saved_rows,
                row_zero,
            ],
            axis=0,
        )
        rows_ref[group, ybit, xbit, core] = vectors.astype(jnp.bfloat16)

        mine = rows_ref.at[group, ybit, xbit, core]
        row_dp = [
            remote(mine, mine, row_dp_send.at[hop], row_dp_recv.at[hop], (dp_peers[hop], head))
            for hop in range(n_dp - 1)
        ]
        y_part = rows_ref.at[:, ybit, xbit, core]
        x_part = rows_ref.at[:, :, xbit, core]
        core_part = rows_ref.at[:, :, :, core]
        row_y = remote(y_part, y_part, row_send.at[0], row_recv.at[0], (group, y_peer))
        row_x = remote(x_part, x_part, row_send.at[1], row_recv.at[1], (group, x_peer))
        row_core = remote(core_part, core_part, row_send.at[2], row_recv.at[2], (group, core_peer))
        for copy in row_dp:
            copy.start()
        run_plan("rows")
        mod_load(0).wait()
        cond_block(0, shift_one_grad, False)
        mod_load(1).wait()
        cond_block(1, scale_one_grad, False)
        cond = cond_ref[1:2, :]
        gate = 1.0 / (1.0 + jnp.exp(-cond))
        gcond_ref[...] = jnp.sum(cond_sum[...].T, axis=0, keepdims=True) * (
            gate * (1.0 + cond * (1.0 - gate))
        )
        for copy in row_dp:
            copy.wait()
        row_y.start()
        run_plan("row_y")
        row_y.wait()
        row_x.start()
        run_plan("row_x")
        row_x.wait()
        row_core.start()
        for flips in others:
            part_copy(flips).wait()
        for block in range(8):
            for place, target in enumerate((gq_ref, gk_ref, gv_ref)):
                target[:, block * 128 : (block + 1) * 128] = p_recv[
                    block, :, place * 128 : (place + 1) * 128
                ]
        run_plan("row_core")
        row_core.wait()
        everyone = rows_ref[...].reshape(n_dp * 64, width)
        device = group * 8 + head
        wanted = lax.broadcasted_iota(jnp.int32, (small, width), 0) + device * small
        column = lax.broadcasted_iota(jnp.int32, (small, width), 1)
        picked = dot_nt(jnp.where(wanted == column, 1.0, 0.0).astype(jnp.bfloat16), everyone)
        place = lax.rem(lax.broadcasted_iota(jnp.int32, picked.shape, 1), 8)
        picked = jnp.where(place == 0, picked, 0.0)
        mod_out = []
        for block in range(6):
            left = pltpu.roll(picked, 1 + block, 1).astype(jnp.bfloat16)
            dn1[block * small : (block + 1) * small, :] = dot_nn(left, everyone)
            mod_out.append(
                pltpu.make_async_copy(
                    dn1.at[pl.ds(block * small, small), :],
                    gmod_hbm.at[:, pl.ds(block * width, width)],
                    load_sem.at[block],
                )
            )
            mod_out[-1].start()
        run_plan("end")
        for copy in mod_out:
            copy.wait()
        for unit in (count - 2, count - 1):
            core_copy(unit).wait_send()

    pl.run_scoped(
        attention_part,
        pltpu.VMEM((frames, tokens, 128), jnp.bfloat16),
        pltpu.VMEM((frames, tokens, 128), jnp.bfloat16),
        pltpu.VMEM((frames, tokens, 128), jnp.bfloat16),
        pltpu.VMEM((frames, tokens, 128), jnp.float32),
        pltpu.VMEM((frames, tokens, width), jnp.bfloat16),
        pltpu.VMEM((width, 384), jnp.bfloat16),
        pltpu.VMEM((SLOTS + 1, 128, tokens), jnp.float32),
        pltpu.VMEM((SLOTS + 1, tokens, 128), jnp.float32),
        pltpu.VMEM((SLOTS + 1, tokens, 128), jnp.float32),
        pltpu.VMEM((frames, 2, tokens), jnp.float32),
        pltpu.VMEM((2, frames // 2, tokens, 384), jnp.bfloat16),
        pltpu.VMEM((384, frames * tokens), jnp.bfloat16),
        pltpu.VMEM((tokens, width), jnp.float32),
        pltpu.VMEM((width, 128), jnp.float32),
    )


PLAN = {
    "fed": [("P", 0), ("P", 1)],
    "normed": [("C", 0), ("C", 1)],
    "attended": [("P", 2), ("P", 3)],
    "branch": [("C", 2), ("C", 3)],
    "outputs": [("P", 4), ("P", 5)],
    "scope": [("F", 0), ("F", 1)],
    2: [("P", 6)],
    4: [("P", 7)],
    6: [("P", 8)],
    12: [("C", 4)],
    13: [("C", 5)],
    "combined": [("P", 9), ("P", 10), ("S", 0), ("S", 1), ("F", 2), ("F", 3), ("C", 9), ("C", 10)],
    "columns": [("C", 8)],
    "cond2": [("F", 4), ("F", 5), ("S", 2), ("S", 3), ("F", 9), ("F", 10), ("C", 6), ("C", 7), ("S", 4), ("S", 5), ("F", 8), ("D", 0), ("D", 1)],
    "rows": [("D", 2), ("D", 3)],
    "row_y": [("D", 4), ("D", 5)],
    "row_x": [("F", 6), ("F", 7), ("S", 8)],
    "end": [("S", 6), ("S", 7), ("D", 8), ("D", 6), ("D", 7)],
}
GATHER_AT = 8


def back_part(n_dp, vmem_operands, hbm_operands):
    table, attended, lse, hidden = vmem_operands[:4]
    hbm_up = hbm_operands[6]
    tokens, width = hidden.shape
    group_tokens = attended.shape[0]
    frames = group_tokens // tokens
    hidden_width = hbm_up.shape[1]
    devices = n_dp * 8
    small, large = width // devices, hidden_width // devices
    first_up = large // small
    tiles = hidden_width // width
    units = first_up + tiles + 3
    dma = pltpu.SemaphoreType.DMA
    f32, bf16 = jnp.float32, jnp.bfloat16
    shape = jax.ShapeDtypeStruct
    return pl.pallas_call(
        lambda *refs: back_kernel(n_dp, *refs),
        out_shape=(
            shape((tokens, width), bf16),
            shape((tokens, width), f32),
            shape((8, 128), f32),
            *[shape((small, width), f32)] * 4,
            shape((small, hidden_width), f32),
            shape((large, width), f32),
            shape((small, 6 * width), f32),
            shape((1, width), f32),
            shape((frames, tokens, width), bf16),
        ),
        in_specs=[IN_SMEM]
        + [IN_VMEM] * (len(vmem_operands) - 1)
        + [IN_PLACE] * len(hbm_operands),
        out_specs=(IN_PLACE, *[IN_VMEM] * 8, IN_PLACE, IN_VMEM, IN_PLACE),
        scratch_shapes=[
            pltpu.VMEM((tokens, width), bf16),
            pltpu.VMEM((frames, tokens, 128), bf16),
            pltpu.VMEM((units, n_dp, 2, 2, small, width), bf16),
            pltpu.VMEM((units, n_dp, 2, small, width), bf16),
            pltpu.VMEM((units, n_dp, small, width), bf16),
            pltpu.VMEM((units - 2, n_dp - 1, small, width), bf16),
            pltpu.VMEM((2, n_dp, 2, 2, small, width), bf16),
            pltpu.VMEM((tokens, width), bf16),
            pltpu.VMEM((first_up + 2, 2, width // 2, tokens), bf16),
            pltpu.VMEM((tokens, width), bf16),
            pltpu.VMEM((tokens, hidden_width), bf16),
            pltpu.VMEM((tokens, width), bf16),
            pltpu.VMEM((tokens, width), f32),
            pltpu.VMEM((n_dp, 2, 2, 2, 8, width), bf16),
            pltpu.VMEM((n_dp, 384, width // n_dp), bf16),
            pltpu.VMEM((n_dp - 1, 384, width // n_dp), bf16),
            pltpu.VMEM((8, small, 384), f32),
            pltpu.VMEM((8, small, 384), f32),
            dma((16,)),
            dma((3, 8)),
            dma((3, 8)),
            *[dma((units,))] * 6,
            dma((units, n_dp - 1)),
            dma((units, n_dp - 1)),
            dma((3,)),
            dma((3,)),
            dma((n_dp - 1,)),
            dma((n_dp - 1,)),
            dma((10,)),
            dma((10,)),
            dma((n_dp - 1,)),
            dma((n_dp - 1,)),
            dma((6, frames // 2)),
        ],
        compiler_params=pltpu.CompilerParams(
            collective_id=0, has_side_effects=True, vmem_limit_bytes=67043328
        ),
        name="back_part",
    )(*vmem_operands, *hbm_operands)


def finish_kernel(*refs):
    count = len(refs) // 3
    sources, targets = refs[:count], refs[count : 2 * count]
    held, (load_sem, store_sem) = refs[2 * count : 3 * count], refs[3 * count :]
    loads = [
        pltpu.make_async_copy(source, room, load_sem.at[place])
        for place, (source, room) in enumerate(zip(sources, held))
    ]
    stores = [
        pltpu.make_async_copy(room, target, store_sem.at[place])
        for place, (room, target) in enumerate(zip(held, targets))
    ]
    for copy in loads:
        copy.start()
    for place in range(count - 1):
        loads[place].wait()
        stores[place].start()
    loads[-1].wait()
    targets[-1][...] = held[-1][0:1, 0:3]
    for copy in stores[:-1]:
        copy.wait()


def finish(arrays):
    shapes = [jax.ShapeDtypeStruct(array.shape, array.dtype) for array in arrays]
    held = [pltpu.VMEM(array.shape, array.dtype) for array in arrays]
    shapes[-1] = jax.ShapeDtypeStruct((1, 3), jnp.float32)
    return pl.pallas_call(
        finish_kernel,
        out_shape=tuple(shapes),
        in_specs=[IN_PLACE] * len(arrays),
        out_specs=(*[IN_PLACE] * (len(arrays) - 1), IN_VMEM),
        scratch_shapes=[
            *held,
            pltpu.SemaphoreType.DMA((len(arrays),)),
            pltpu.SemaphoreType.DMA((len(arrays),)),
        ],
        name="finish",
    )(*arrays)


def front_kernel(*refs):
    (
        x_ref,
        mod_ref,
        rope_ref,
        wq_hbm,
        wk_hbm,
        wv_hbm,
        n1_ref,
        q_ref,
        k_ref,
        v_ref,
        weights,
        sent,
        load_sem,
        send_sem,
        recv_sem,
    ) = refs
    tokens, width = x_ref.shape
    group = lax.axis_index("dp")
    head = lax.axis_index("head")
    core = lax.rem(head, 2)
    barrier = pltpu.get_barrier_semaphore()
    for flips in range(1, 8):
        pl.semaphore_signal(
            barrier, inc=1, device_id=(group, peer_head(head, flips)), device_id_type=MESH_ID
        )
    loads = [
        pltpu.make_async_copy(source, weights.at[place], load_sem.at[place])
        for place, source in enumerate((wq_hbm, wk_hbm, wv_hbm))
    ]
    for copy in loads:
        copy.start()
    shift, scaling = mod_ref[0:1, :], mod_ref[1:2, :]

    def norm(index, _):
        rows = pl.ds(pl.multiple_of(index * 32, 32), 32)
        value = x_ref[rows, :].astype(jnp.float32)
        scale = lax.rsqrt(jnp.mean(value * value, axis=1, keepdims=True) + EPSILON)
        n1_ref[rows, :] = (value * scale * (1.0 + scaling) + shift).astype(jnp.bfloat16)
        return 0

    lax.fori_loop(0, tokens // 32, norm, 0)
    pl.semaphore_wait(barrier, 7)
    cosine, sine = rope_ref[0:1, :], rope_ref[1:2, :]
    outs = (q_ref, k_ref, v_ref)

    def copy_to(place, flips):
        peer = peer_head(head, flips)
        return remote(
            sent.at[place, :, pl.ds(peer * 128, 128)],
            outs[place].at[head],
            send_sem.at[place, flips],
            recv_sem.at[place, flips],
            (group, peer),
        )

    for place in range(3):
        loads[place].wait()
        for chip_flips in (6, 2, 4, 0):
            chip = lax.div(peer_head(head, chip_flips), 2)
            lanes = pl.ds(pl.multiple_of(chip * BLOCK, BLOCK), BLOCK)
            value = dot_nn(n1_ref[...], weights[place, :, lanes])
            for side in range(2):
                part = value[:, side * 128 : (side + 1) * 128]
                if place < 2:
                    part = part * cosine + turn_pairs(part, None) * sine
                where = pl.ds(pl.multiple_of(chip * BLOCK + side * 128, 128), 128)
                sent[place, :, where] = part.astype(jnp.bfloat16)
            for flips in (chip_flips, chip_flips + 1):
                if flips:
                    copy_to(place, flips).start()
        outs[place][head] = sent[place, :, pl.ds(pl.multiple_of(head * 128, 128), 128)]
    for place in range(3):
        for flips in range(1, 8):
            copy_to(place, flips).wait()


def front_part(hidden, modulation, rope, query_weight, key_weight, value_weight):
    tokens, width = hidden.shape
    dma = pltpu.SemaphoreType.DMA
    block = jax.ShapeDtypeStruct((8, tokens, 128), jnp.bfloat16)
    return pl.pallas_call(
        front_kernel,
        out_shape=(jax.ShapeDtypeStruct((tokens, width), jnp.bfloat16), block, block, block),
        in_specs=[IN_VMEM] * 3 + [IN_PLACE] * 3,
        out_specs=(IN_VMEM,) * 4,
        scratch_shapes=[
            pltpu.VMEM((3, width, width), jnp.bfloat16),
            pltpu.VMEM((3, tokens, width), jnp.bfloat16),
            dma((3,)),
            dma((3, 8)),
            dma((3, 8)),
        ],
        compiler_params=pltpu.CompilerParams(
            collective_id=1, has_side_effects=True, vmem_limit_bytes=32 * 1024 * 1024
        ),
        name="front_part",
    )(hidden, modulation, rope, query_weight, key_weight, value_weight)


def slot_table(first, frames):
    pair = jnp.arange(4 * frames, dtype=jnp.int32)
    frame, back = pair // 4, pair % 4
    held = (frame - back) >= jnp.repeat(first, 4)
    rank = jnp.sum((held[None, :] & (pair[None, :] < pair[:, None])).astype(jnp.int32), axis=1)
    slot = jnp.where(held, rank, SLOTS)
    hit = slot[None, :] == jnp.arange(SLOTS, dtype=jnp.int32)[:, None]
    query = jnp.sum(jnp.where(hit, frame[None, :], 0), axis=1)
    key = jnp.sum(jnp.where(hit, (frame - back)[None, :], 0), axis=1)
    grid = slot.reshape(frames, 4)
    columns = [
        jnp.concatenate([grid[way:, way], jnp.full((way,), SLOTS, jnp.int32)]) for way in range(4)
    ]
    same = (query == key).astype(jnp.int32)
    return jnp.concatenate([query, key, slot, jnp.stack(columns, axis=1).reshape(-1), same])


def per_device(
    hidden_in,
    frame_cond,
    query_weight,
    key_weight,
    value_weight,
    output_weight,
    up_weight,
    down_weight,
    modulation_weight,
    clip_lengths,
    patch_valid,
    cotangent,
):
    tok_dev, model_width = hidden_in.shape
    group_tokens = patch_valid.shape[0]
    frames = group_tokens // PATCHES
    head_index = lax.axis_index("head")
    n_dp = lax.axis_size("dp")
    frame = jnp.arange(frames, dtype=jnp.int32)
    ends = jnp.cumsum(clip_lengths[0])
    first_frames = jnp.max(
        jnp.where(ends[None, :] <= frame[:, None], ends[None, :], 0), axis=1
    ).astype(jnp.int32)
    angles = (frame - first_frames).astype(jnp.float32)[:, None] * frequencies(HEAD_DIM // 2)[None]
    cosine, sine = jnp.cos(angles), jnp.sin(angles)
    cosines = jnp.concatenate([cosine] * 4, axis=1)
    sines = jnp.concatenate([-sine, sine] * 2, axis=1)
    rope = jnp.stack([cosines, sines], axis=1)
    rope_back = jnp.stack([cosines, -sines], axis=1)
    local_valid = lax.dynamic_slice_in_dim(patch_valid, head_index * tok_dev, tok_dev)
    cond_value = frame_cond.astype(jnp.float32)
    cond_act = jax.nn.silu(cond_value).astype(jnp.bfloat16)
    modulation = jnp.dot(cond_act, modulation_weight, preferred_element_type=jnp.float32).reshape(
        6, model_width
    )
    normed_one, head_query, head_key, head_value = front_part(
        hidden_in,
        modulation[:2],
        lax.dynamic_index_in_dim(rope, head_index, 0, keepdims=False),
        query_weight,
        key_weight,
        value_weight,
    )
    bias = jnp.broadcast_to(
        jnp.where(patch_valid == 1, 0.0, MASKED).astype(jnp.float32)[:, None],
        (group_tokens, 128),
    )
    attended, logsum = attend_forward(
        first_frames,
        *[array.reshape(group_tokens, 128) for array in (head_query, head_key, head_value)],
        bias,
    )
    results = back_part(
        n_dp,
        (
            slot_table(first_frames, frames),
            attended,
            logsum,
            hidden_in,
            cotangent,
            modulation,
            rope_back,
            jnp.concatenate([cond_act.astype(jnp.float32), cond_value], axis=0),
            jnp.broadcast_to(local_valid.astype(jnp.float32)[:, None], (tok_dev, 128)),
        ),
        (
            head_query,
            head_key,
            head_value,
            bias.reshape(frames, PATCHES, 128),
            normed_one,
            output_weight,
            up_weight,
            down_weight,
            query_weight,
            key_weight,
            value_weight,
            modulation_weight,
        ),
    )
    (block_out, grad_input, statistics, gq, gk, gv, go, gup, gdown, gmod, gcond, _) = results
    (grad_input, gmod, block_out, gup, gdown, gq, gk, gv, go, gcond, statistics) = finish(
        (grad_input, gmod, block_out, gup, gdown, gq, gk, gv, go, gcond, statistics)
    )
    return (
        block_out,
        grad_input,
        gcond,
        gq,
        gk,
        gv,
        go,
        gup,
        gdown,
        gmod,
        statistics,
    )


def solution(mesh):
    in_specs = (
        P(("dp", "head"), None),
        P(("dp", "head"), None),
        P(),
        P(),
        P(),
        P(),
        P(),
        P(),
        P(),
        P("dp", None),
        P("dp"),
        P(("dp", "head"), None),
    )
    out_specs = (
        P(("dp", "head"), None),
        P(("dp", "head"), None),
        P(("dp", "head"), None),
        P(("dp", "head"), None),
        P(("dp", "head"), None),
        P(("dp", "head"), None),
        P(("dp", "head"), None),
        P(("dp", "head"), None),
        P(("dp", "head"), None),
        P(("dp", "head"), None),
        P(("dp", "head"), None),
    )
    return jax.shard_map(
        per_device, mesh=mesh, in_specs=in_specs, out_specs=out_specs, check_vma=False
    )
```

```python
import math

import jax
import jax.numpy as jnp
import numpy as np
from jax import lax
from jax.experimental import pallas as pl
from jax.experimental.pallas import tpu as pltpu
from jax.sharding import PartitionSpec as P

HEADS = 16
HEAD_DIM = 64
PATCHES = 256


EPSILON = 1e-06
MASKED = -1e30


def dot_nt(left, right):
    return lax.dot_general(
        left, right, (((1,), (1,)), ((), ())), preferred_element_type=jnp.float32
    )


def dot_nn(left, right):
    return lax.dot_general(
        left, right, (((1,), (0,)), ((), ())), preferred_element_type=jnp.float32
    )


def head_parts(block):
    lane = lax.broadcasted_iota(jnp.int32, block.shape, 1)
    zero = jnp.zeros_like(block)
    return jnp.where(lane < HEAD_DIM, block, zero), jnp.where(lane < HEAD_DIM, zero, block)


def key_bias(bias_ref, key_frame, frame):
    half = bias_ref[pl.ds(key_frame * PATCHES, PATCHES), :]
    bias = jnp.concatenate([half, half], axis=1)
    row = lax.broadcasted_iota(jnp.int32, bias.shape, 0)
    column = lax.broadcasted_iota(jnp.int32, bias.shape, 1)
    own = (row == column) & (key_frame == frame)
    return jnp.where(own, 0.0, bias)


def attend_forward_kernel(first_ref, q_ref, k_ref, v_ref, bias_ref, o_ref, lse_ref, scores):
    frames = q_ref.shape[0] // PATCHES

    def one_frame(frame, _):
        rows = pl.ds(frame * PATCHES, PATCHES)
        parts = head_parts(q_ref[rows, :] * jnp.bfloat16(0.125))
        first = first_ref[frame]

        def score(key_frame, tops):
            keys = k_ref[pl.ds(key_frame * PATCHES, PATCHES), :]
            bias = key_bias(bias_ref, key_frame, frame)
            new = []
            for head in range(2):
                value = dot_nt(keys, parts[head]) + bias
                scores[head, key_frame - first] = value
                new.append(jnp.maximum(tops[head], jnp.max(value, axis=0, keepdims=True)))
            return tuple(new)

        low = jnp.full((1, PATCHES), MASKED, jnp.float32)
        tops = lax.fori_loop(first, frame + 1, score, (low, low))

        def exponent(key_frame, totals):
            new = []
            for head in range(2):
                value = jnp.exp(scores[head, key_frame - first] - tops[head])
                scores[head, key_frame - first] = value
                new.append(totals[head] + jnp.sum(value, axis=0, keepdims=True))
            return tuple(new)

        zero = jnp.zeros((1, PATCHES), jnp.float32)
        totals = lax.fori_loop(first, frame + 1, exponent, (zero, zero))
        inverse = [1.0 / total for total in totals]

        def weigh(key_frame, sums):
            turned = v_ref[pl.ds(key_frame * PATCHES, PATCHES), :].T
            new = []
            for head in range(2):
                probs = (scores[head, key_frame - first] * inverse[head]).astype(jnp.bfloat16)
                new.append(
                    sums[head]
                    + dot_nn(turned[head * HEAD_DIM : (head + 1) * HEAD_DIM, :], probs)
                )
            return tuple(new)

        empty = jnp.zeros((HEAD_DIM, PATCHES), jnp.float32)
        sums = lax.fori_loop(first, frame + 1, weigh, (empty, empty))
        o_ref[rows, :] = jnp.concatenate(sums, axis=0).T.astype(jnp.bfloat16)
        for head in range(2):
            lse_ref[frame, head : head + 1, :] = tops[head] + jnp.log(totals[head])
        return 0

    lax.fori_loop(0, frames, one_frame, 0)


IN_SMEM = pl.BlockSpec(memory_space=pltpu.SMEM)
IN_VMEM = pl.BlockSpec(memory_space=pltpu.VMEM)
IN_PLACE = pl.BlockSpec(memory_space=pl.ANY)
MESH_ID = pl.DeviceIdType.MESH


def attend_forward(first, queries, keys, values, bias):
    tokens, width = queries.shape
    frames = tokens // PATCHES
    return pl.pallas_call(
        attend_forward_kernel,
        out_shape=(
            jax.ShapeDtypeStruct((tokens, width), jnp.bfloat16),
            jax.ShapeDtypeStruct((frames, 2, PATCHES), jnp.float32),
        ),
        in_specs=[IN_SMEM] + [IN_VMEM] * 4,
        out_specs=(IN_VMEM, IN_VMEM),
        scratch_shapes=[pltpu.VMEM((2, 4, PATCHES, PATCHES), jnp.float32)],
        name="attend_forward",
    )(first, queries, keys, values, bias)


SLOTS = 17
BLOCK = 256


def peer_head(head, flips):
    core = lax.rem(head, 2)
    second = lax.rem(lax.div(head, 2), 2)
    third = lax.div(head, 4)
    if flips % 2:
        core = 1 - core
    if flips // 2 % 2:
        second = 1 - second
    if flips // 4:
        third = 1 - third
    return 4 * third + 2 * second + core


def remote(source, target, send, receive, where):
    return pltpu.make_async_remote_copy(
        src_ref=source,
        dst_ref=target,
        send_sem=send,
        recv_sem=receive,
        device_id=where,
        device_id_type=MESH_ID,
    )


def gelu_and_slope(value):
    square = value * value
    inner = 0.7978845608028654 * value * (1.0 + 0.044715 * square)
    bend = jnp.tanh(inner)
    half = 0.5 * (1.0 + bend)
    slope = half + 0.5 * value * (1.0 - bend * bend) * (
        0.7978845608028654 * (1.0 + 0.134145 * square)
    )
    return value * half, slope


def turn_pairs(values):
    lane = lax.rem(lax.broadcasted_iota(jnp.int32, values.shape, 1), HEAD_DIM)
    up = pltpu.roll(values, 128 - HEAD_DIM // 2, 1)
    down = pltpu.roll(values, HEAD_DIM // 2, 1)
    return jnp.where(lane < HEAD_DIM // 2, up, down)


def back_kernel(n_dp, *refs):
    (
        table,
        att_own,
        lse_ref,
        x_ref,
        cot_ref,
        mod_ref,
        rope_ref,
        cond_ref,
        q_hbm,
        k_hbm,
        v_hbm,
        bias_hbm,
        n1_hbm,
        wo_hbm,
        up_hbm,
        down_hbm,
        wq_hbm,
        wk_hbm,
        wv_hbm,
        wmod_hbm,
        block_hbm,
        gin_ref,
        stat_ref,
        gq_ref,
        gk_ref,
        gv_ref,
        go_ref,
        gup_ref,
        gdown_ref,
        gmod_hbm,
        gcond_ref,
        valid_ref,
        att_fr,
        do_own,
        from_core,
        from_first,
        from_second,
        from_dp,
        core_out,
        da_send,
        lhs,
        dmlp,
        dhid,
        dattn,
        mid,
        rows_ref,
        z_send,
        z_recv,
        p_send,
        p_recv,
        load_sem,
        a2a_send,
        a2a_recv,
        core_send,
        core_recv,
        first_send,
        first_recv,
        second_send,
        second_recv,
        dp_send,
        dp_recv,
        row_send,
        row_recv,
        row_dp_send,
        row_dp_recv,
        z_send_sem,
        z_recv_sem,
        mod_sem,
    ) = refs
    tokens, width = x_ref.shape
    frames = q_hbm.shape[0]
    hidden_width = up_hbm.shape[1]
    tiles = hidden_width // width
    chunks = width // BLOCK
    small = width // (n_dp * 8)
    large = hidden_width // (n_dp * 8)
    half_rows = n_dp * 4 * small
    group = lax.axis_index("dp")
    head = lax.axis_index("head")
    core = lax.rem(head, 2)
    xbit = lax.rem(lax.div(head, 2), 2)
    ybit = lax.div(head, 4)
    core_peer, x_peer, y_peer = peer_head(head, 1), peer_head(head, 2), peer_head(head, 4)
    dp_peers = [lax.rem(group + hop, n_dp) for hop in range(1, n_dp)]
    others = range(1, 8)

    barrier = pltpu.get_barrier_semaphore()
    for flips in others:
        pl.semaphore_signal(
            barrier, inc=1, device_id=(group, peer_head(head, flips)), device_id_type=MESH_ID
        )
    for peer in dp_peers:
        pl.semaphore_signal(barrier, inc=1, device_id=(peer, head), device_id_type=MESH_ID)

    pl.semaphore_wait(barrier, 7 + len(dp_peers))

    own_rows = pl.ds(head * tokens, tokens)
    own_lanes = pl.ds(head * 128, 128)

    def att_copy(flips):
        peer = peer_head(head, flips)
        return remote(
            att_own.at[pl.ds(peer * tokens, tokens), :],
            att_fr.at[:, own_lanes],
            a2a_send.at[0, flips],
            a2a_recv.at[0, flips],
            (group, peer),
        )

    def grad_copy(flips):
        peer = peer_head(head, flips)
        return remote(
            da_send.at[:, pl.ds(peer * 128, 128)],
            do_own.at[head],
            a2a_send.at[1, flips],
            a2a_recv.at[1, flips],
            (group, peer),
        )

    first_up = large // small
    first_out = first_up + tiles
    count = first_out + 3

    def slot_of(unit):
        return unit

    def lhs_of(unit):
        if unit < first_up:
            return unit
        return first_up if unit < first_out else first_up + 1

    def core_copy(unit):
        return remote(
            core_out.at[unit % 2],
            from_core.at[slot_of(unit)],
            core_send.at[unit],
            core_recv.at[unit],
            (group, core_peer),
        )

    def x_leads(unit):
        return unit % 2 == 0

    def first_copy(unit):
        slot = slot_of(unit)
        if x_leads(unit):
            source, peer = from_core.at[slot, :, :, 1 - xbit], x_peer
        else:
            source, peer = from_core.at[slot, :, 1 - ybit], y_peer
        return remote(
            source, from_first.at[slot], first_send.at[unit], first_recv.at[unit], (group, peer)
        )

    def second_copy(unit):
        slot = slot_of(unit)
        if x_leads(unit):
            source, peer = from_core.at[slot, :, 1 - ybit, xbit], y_peer
        else:
            source, peer = from_core.at[slot, :, ybit, 1 - xbit], x_peer
        return remote(
            source, from_second.at[slot], second_send.at[unit], second_recv.at[unit], (group, peer)
        )

    def dp_copy(unit, hop):
        peer = dp_peers[hop]
        return remote(
            from_core.at[slot_of(unit), peer, ybit, xbit],
            from_dp.at[unit, hop],
            dp_send.at[unit, hop],
            dp_recv.at[unit, hop],
            (peer, head),
        )

    def added(left, right):
        return (left.astype(jnp.float32) + right.astype(jnp.float32)).astype(jnp.bfloat16)

    def put(target, lanes, value, unit):
        value = value.astype(jnp.bfloat16)
        if unit <= first_out:
            target[:, :, :, :, lanes] = value.reshape(n_dp, 2, 2, small, BLOCK)
        else:
            value = value.reshape(4, n_dp, small, BLOCK)
            for chip in range(4):
                target[:, chip // 2, chip % 2, :, lanes] = value[chip]

    def got(source, lanes, unit):
        if unit <= first_out:
            return source[:, :, :, :, lanes].reshape(half_rows, BLOCK)
        return jnp.concatenate(
            [
                source[:, chip // 2, chip % 2, :, lanes].reshape(half_rows // 4, BLOCK)
                for chip in range(4)
            ],
            axis=0,
        )

    def produce(unit, product):
        if unit >= 2:
            core_copy(unit - 2).wait_send()

        def body(chunk, _):
            lanes = pl.ds(pl.multiple_of(chunk * BLOCK, BLOCK), BLOCK)
            put(core_out.at[unit % 2], lanes, product(unit, 1 - core, chunk), unit)
            return 0

        lax.fori_loop(0, chunks, body, 0)
        core_copy(unit).start()

    def take_core(unit, product):
        core_copy(unit).wait_recv()
        place = from_core.at[slot_of(unit)]

        def body(chunk, _):
            lanes = pl.ds(pl.multiple_of(chunk * BLOCK, BLOCK), BLOCK)
            value = product(unit, core, chunk) + got(place, lanes, unit).astype(jnp.float32)
            put(place, lanes, value, unit)
            return 0

        lax.fori_loop(0, chunks, body, 0)
        first_copy(unit).start()

    def take_first(unit):
        first_copy(unit).wait()
        slot = slot_of(unit)

        def body(index, _):
            at_dp = lax.div(index, 2)
            other = lax.rem(index, 2)
            at_y, at_x = (other, xbit) if x_leads(unit) else (ybit, other)
            from_core[slot, at_dp, at_y, at_x] = added(
                from_core[slot, at_dp, at_y, at_x], from_first[slot, at_dp, other]
            )
            return 0

        lax.fori_loop(0, n_dp * 2, body, 0)
        second_copy(unit).start()

    def take_second(unit):
        second_copy(unit).wait()
        slot = slot_of(unit)

        def body(at_dp, _):
            from_core[slot, at_dp, ybit, xbit] = added(
                from_core[slot, at_dp, ybit, xbit], from_second[slot, at_dp]
            )
            return 0

        lax.fori_loop(0, n_dp, body, 0)
        for hop in range(n_dp - 1):
            dp_copy(unit, hop).start()

    def take_dp(unit):
        for hop in range(n_dp - 1):
            dp_copy(unit, hop).wait()
        total = from_core[slot_of(unit), group, ybit, xbit].astype(jnp.float32)
        for hop in range(n_dp - 1):
            total = total + from_dp[unit, hop].astype(jnp.float32)
        if unit < first_up:
            gdown_ref[unit * small : (unit + 1) * small, :] = total
        elif unit < first_out:
            place = (unit - first_up) * width
            gup_ref[:, place : place + width] = total
        else:
            go_ref[...] = total

    def turned_rows(index, source):
        for chunk in range(chunks):
            value = source[:, chunk * BLOCK : (chunk + 1) * BLOCK].T
            value = value.reshape(BLOCK // (2 * small), 2, small, tokens)
            for side in range(2):
                lhs[index, side, chunk * BLOCK // 2 : (chunk + 1) * BLOCK // 2, :] = value[
                    :, side
                ].reshape(BLOCK // 2, tokens)

    shift_one, scale_one, gate_one = (mod_ref[row : row + 1, :] for row in range(3))
    shift_two, scale_two, gate_two = (mod_ref[row : row + 1, :] for row in range(3, 6))
    step_rows = 32
    steps = tokens // step_rows

    def row_block(index):
        return pl.ds(pl.multiple_of(index * step_rows, step_rows), step_rows)

    def lane_block(chunk):
        return pl.ds(pl.multiple_of(chunk * BLOCK, BLOCK), BLOCK)

    def masked_square(values, rows):
        counted = jnp.where(valid_ref[rows, :1] < -1.0, 0.0, 1.0)
        sums = jnp.sum(values * values, axis=1, keepdims=True) * counted
        return jnp.sum(sums, axis=0, keepdims=True)

    one = jnp.zeros((1, 1), jnp.float32)
    row_zero = jnp.zeros((1, width), jnp.float32)

    valid_load = pltpu.make_async_copy(bias_hbm.at[head], valid_ref, load_sem.at[15])
    valid_load.start()
    for flips in others:
        att_copy(flips).start()
    att_fr[:, own_lanes] = att_own[own_rows, :]

    def weight_product(unit, side, chunk):
        if unit < first_up:
            right = dmlp[:, lane_block(chunk)]
        elif unit < first_out:
            start = (unit - first_up) * width + chunk * BLOCK
            right = dhid[:, pl.ds(pl.multiple_of(start, BLOCK), BLOCK)]
        else:
            right = dattn[:, lane_block(chunk)]
        return dot_nn(lhs[lhs_of(unit), side], right)

    def run_plan(point, product=weight_product):
        for kind, unit in PLAN.get(point, ()):
            if kind == "P":
                produce(unit, product)
            elif kind == "C":
                take_core(unit, product)
            elif kind == "F":
                take_first(unit)
            elif kind == "S":
                take_second(unit)
            else:
                take_dp(unit)

    half = tokens // 2

    def mlp_part(up, down, act, dn2, wo, ba, n2):
        wo_load = pltpu.make_async_copy(wo_hbm, wo, load_sem.at[0])
        wo_load.start()
        up_loads = [
            pltpu.make_async_copy(
                up_hbm.at[:, pl.ds(tile * width, width)],
                up.at[:, pl.ds(tile * width, width)],
                load_sem.at[1 + tile],
            )
            for tile in range(tiles)
        ]
        down_loads = [
            pltpu.make_async_copy(
                down_hbm.at[pl.ds(tile * width, width), :],
                down.at[pl.ds(tile * width, width), :],
                load_sem.at[1 + tiles + tile],
            )
            for tile in range(tiles)
        ]
        for tile in range(tiles):
            up_loads[tile].start()
            down_loads[tile].start()

        valid_load.wait()
        wo_load.wait()
        for flips in others:
            att_copy(flips).wait()
        turned_rows(first_up + 1, att_fr)

        def project(chunk, _):
            lanes = lane_block(chunk)
            ba[:, lanes] = dot_nn(att_fr[...], wo[:, lanes])
            return 0

        lax.fori_loop(0, chunks, project, 0)

        def second_norm(index, total):
            rows = row_block(index)
            branch = gate_one * ba[rows, :]
            value = x_ref[rows, :].astype(jnp.float32) + branch
            mid[rows, :] = value
            scale = lax.rsqrt(jnp.mean(value * value, axis=1, keepdims=True) + EPSILON)
            n2[rows, :] = (value * scale * (1.0 + scale_two) + shift_two).astype(jnp.bfloat16)
            dmlp[rows, :] = (gate_two * cot_ref[rows, :].astype(jnp.float32)).astype(jnp.bfloat16)
            return total + masked_square(branch, rows)

        stat_attn = lax.fori_loop(0, steps, second_norm, one)
        turned_rows(first_up, n2)

        pairs = BLOCK // (2 * large)

        def feed(index, _):
            @pl.when(lax.rem(index, chunks) == 0)
            def _():
                tile = lax.div(index, chunks)
                pltpu.make_async_copy(
                    up_hbm.at[:, pl.ds(0, width)],
                    up.at[:, pl.ds(0, width)],
                    load_sem.at[1 + tile],
                ).wait()
                pltpu.make_async_copy(
                    down_hbm.at[pl.ds(0, width), :],
                    down.at[pl.ds(0, width), :],
                    load_sem.at[1 + tiles + tile],
                ).wait()

            lanes = lane_block(index)
            active, slope = gelu_and_slope(dot_nn(n2[...], up[:, lanes]))
            active = active.astype(jnp.bfloat16)
            act[:, lanes] = active
            grad = dot_nt(dmlp[...], down[lanes, :])
            dhid[:, lanes] = (grad * slope).astype(jnp.bfloat16)
            turned = active.T.reshape(pairs, 2, first_up, small, tokens)
            where = pl.ds(pl.multiple_of(index * pairs * small, pairs * small), pairs * small)
            for unit in range(first_up):
                for side in range(2):
                    lhs[unit, side, where, :] = turned[:, side, unit].reshape(
                        pairs * small, tokens
                    )
            return 0

        lax.fori_loop(0, hidden_width // BLOCK, feed, 0)

        run_plan("fed")

        def to_normed(chunk, _):
            lanes = lane_block(chunk)
            dn2[:, lanes] = dot_nt(dhid[...], up[lanes, :])
            return 0

        lax.fori_loop(0, chunks, to_normed, 0)
        run_plan("normed")

        def second_norm_back(index, sums):
            shift_sum, scale_sum, gate_sum = sums
            rows = row_block(index)
            value = mid[rows, :]
            scale = lax.rsqrt(jnp.mean(value * value, axis=1, keepdims=True) + EPSILON)
            normed = value * scale
            grad = dn2[rows, :]
            shift_sum = shift_sum + jnp.sum(grad, axis=0, keepdims=True)
            scale_sum = scale_sum + jnp.sum(grad * normed, axis=0, keepdims=True)
            inner = grad * (1.0 + scale_two)
            mean = jnp.mean(inner * normed, axis=1, keepdims=True)
            total = cot_ref[rows, :].astype(jnp.float32) + scale * (inner - normed * mean)
            dn2[rows, :] = total
            gate_sum = gate_sum + jnp.sum(total * ba[rows, :], axis=0, keepdims=True)
            dattn[rows, :] = (gate_one * total).astype(jnp.bfloat16)
            return shift_sum, scale_sum, gate_sum

        shift_two_grad, scale_two_grad, gate_one_grad = lax.fori_loop(
            0, steps, second_norm_back, (row_zero, row_zero, row_zero)
        )

        def to_attended(chunk, _):
            lanes = lane_block(chunk)
            da_send[:, lanes] = dot_nt(dattn[...], wo[lanes, :]).astype(jnp.bfloat16)
            return 0

        lax.fori_loop(0, chunks, to_attended, 0)
        for flips in others:
            grad_copy(flips).start()
        do_own[head] = da_send[:, own_lanes]

        run_plan("attended")

        def branch_out(chunk, _):
            lanes = lane_block(chunk)
            ba[:, lanes] = dot_nn(act[...], down[:, lanes])
            return 0

        lax.fori_loop(0, chunks, branch_out, 0)
        run_plan("branch")

        def outputs(index, sums):
            gate_sum, stat_mlp, stat_out = sums
            rows = row_block(index)
            raw = ba[rows, :]
            branch = gate_two * raw
            value = mid[rows, :] + branch
            n2[rows, :] = value.astype(jnp.bfloat16)
            gate_sum = gate_sum + jnp.sum(
                cot_ref[rows, :].astype(jnp.float32) * raw, axis=0, keepdims=True
            )
            stat_mlp = stat_mlp + masked_square(branch, rows)
            stat_out = stat_out + masked_square(value, rows)
            mid[rows, :] = dn2[rows, :]
            return gate_sum, stat_mlp, stat_out

        gate_two_grad, stat_mlp, stat_out = lax.fori_loop(0, steps, outputs, (row_zero, one, one))
        lane = lax.broadcasted_iota(jnp.int32, stat_ref.shape, 1)
        stats = jnp.where(lane == 0, stat_attn, jnp.where(lane == 1, stat_mlp, stat_out))
        stat_ref[...] = jnp.sqrt(stats / (tokens * width) + EPSILON)
        for row, vector in (
            (3, gate_one_grad),
            (4, shift_two_grad),
            (5, scale_two_grad),
            (6, gate_two_grad),
        ):
            gin_ref[row : row + 1, :] = vector
        block_copy = pltpu.make_async_copy(n2, block_hbm, load_sem.at[0])
        block_copy.start()
        run_plan("outputs")
        block_copy.wait()

    pl.run_scoped(
        mlp_part,
        pltpu.VMEM((width, hidden_width), jnp.bfloat16),
        pltpu.VMEM((hidden_width, width), jnp.bfloat16),
        pltpu.VMEM((tokens, hidden_width), jnp.bfloat16),
        pltpu.VMEM((tokens, width), jnp.float32),
        pltpu.VMEM((width, width), jnp.bfloat16),
        pltpu.VMEM((tokens, width), jnp.float32),
        pltpu.VMEM((tokens, width), jnp.bfloat16),
    )
    saved_rows = [gin_ref[row : row + 1, :] for row in range(3, 7)]

    def attention_part(
        q_ref,
        k_ref,
        v_ref,
        bias_ref,
        n1_group,
        w_own,
        dq_slots,
        dk_slots,
        dv_slots,
        deltas,
        d_all,
        d_turned,
        dn1,
        cond_sum,
    ):
        pieces = [
            (q_hbm, q_ref),
            (k_hbm, k_ref),
            (v_hbm, v_ref),
            (bias_hbm, bias_ref),
            (wq_hbm.at[:, own_lanes], w_own.at[:, pl.ds(0, 128)]),
            (wk_hbm.at[:, own_lanes], w_own.at[:, pl.ds(128, 128)]),
            (wv_hbm.at[:, own_lanes], w_own.at[:, pl.ds(256, 128)]),
        ]
        loads = [
            pltpu.make_async_copy(source, target, load_sem.at[1 + place])
            for place, (source, target) in enumerate(pieces)
        ]
        for copy in loads:
            copy.start()

        pages = frames // 2

        class mod_load:
            def __init__(self, block):
                self.copies = [
                    pltpu.make_async_copy(
                        wmod_hbm.at[pl.ds(page * tokens, tokens), pl.ds(block * width, width)],
                        n1_group.at[block % 2 * pages + page],
                        mod_sem.at[block, page],
                    )
                    for page in range(pages)
                ]

            def start(self):
                for copy in self.copies:
                    copy.start()

            def wait(self):
                for copy in self.copies:
                    copy.wait()

        group_load = pltpu.make_async_copy(n1_hbm, n1_group, load_sem.at[0])
        group_load.start()
        run_plan("scope")
        for flips in others:
            grad_copy(flips).wait()
        for copy in loads:
            copy.wait()
        for slots in (dq_slots, dk_slots, dv_slots):
            slots[SLOTS] = jnp.zeros(slots.shape[1:], jnp.float32)

        def frame_delta(frame, _):
            rows = pl.ds(pl.multiple_of(frame * tokens, tokens), tokens)
            product = (
                do_own[frame].astype(jnp.float32) * att_own[rows, :].astype(jnp.float32)
            ).T
            for part in range(2):
                deltas[frame, part : part + 1, :] = jnp.sum(
                    product[part * HEAD_DIM : (part + 1) * HEAD_DIM, :], axis=0, keepdims=True
                )
            return 0

        lax.fori_loop(0, frames, frame_delta, 0)

        def one_slot(index, _):
            frame = table[index]
            key_frame = table[SLOTS + index]
            q_parts = head_parts(q_ref[frame] * jnp.bfloat16(0.125))
            do_parts = head_parts(do_own[frame])
            keys = k_ref[key_frame]
            values = v_ref[key_frame]
            turned = keys.T
            half = bias_ref[key_frame]
            row = lax.broadcasted_iota(jnp.int32, (tokens, tokens), 0)
            column = lax.broadcasted_iota(jnp.int32, (tokens, tokens), 1)
            same = table[2 * SLOTS + 8 * frames + index].astype(jnp.float32)
            keep = 1.0 - jnp.where(row == column, 1.0, 0.0) * same
            bias = jnp.concatenate([half, half], axis=1) * keep
            dv = dk = None
            dq = []
            for part in range(2):
                lse = lse_ref[frame, part : part + 1, :]
                delta = deltas[frame, part : part + 1, :]
                probs = jnp.exp(dot_nt(keys, q_parts[part]) + bias - lse)
                prob_grad = dot_nt(values, do_parts[part])
                score_grad = (probs * (prob_grad - delta)).astype(jnp.bfloat16)
                dv_part = dot_nn(probs.astype(jnp.bfloat16), do_parts[part])
                dk_part = dot_nn(score_grad, q_parts[part])
                dv = dv_part if dv is None else dv + dv_part
                dk = dk_part if dk is None else dk + dk_part
                dq.append(
                    dot_nn(turned[part * HEAD_DIM : (part + 1) * HEAD_DIM, :], score_grad)
                )
            dv_slots[index] = dv
            dk_slots[index] = dk
            dq_slots[index] = jnp.concatenate(dq, axis=0)
            for place in range(SLOTS):
                if PLAN.get(place):
                    pl.when(index == place)(lambda place=place: run_plan(place))
            return 0

        lax.fori_loop(0, SLOTS, one_slot, 0)

        def summed(slots, start, frame):
            total = slots[table[start + 4 * frame]]
            for way in range(1, 4):
                total = total + slots[table[start + 4 * frame + way]]
            return total

        def combine(frame, _):
            side, chip = lax.rem(frame, 2), lax.div(frame, 2)
            cosine = rope_ref[frame, 0:1, :]
            sine = rope_ref[frame, 1:2, :]

            def turned_back(value):
                value = value.astype(jnp.bfloat16).astype(jnp.float32)
                return (value * cosine - turn_pairs(value) * sine).astype(jnp.bfloat16)

            start = 2 * SLOTS + 4 * frames
            parts = (
                turned_back(summed(dq_slots, 2 * SLOTS, frame).T * 0.125),
                turned_back(summed(dk_slots, start, frame)),
                summed(dv_slots, start, frame).astype(jnp.bfloat16),
            )
            where = pl.ds(pl.multiple_of(frame * tokens, tokens), tokens)
            for place, part in enumerate(parts):
                d_all[side, chip, :, place * 128 : (place + 1) * 128] = part
                d_turned[place * 128 : (place + 1) * 128, where] = part.T
            return 0

        lax.fori_loop(0, frames, combine, 0)

        def normed_product(unit, side, chunk):
            first = (unit - first_out - 1) * half
            left = d_all[side, :, first : first + half, :].reshape(half_rows, 384)
            return dot_nt(left, w_own[lane_block(chunk), :])

        def normed_plan(point):
            run_plan(
                point,
                lambda unit, *where: (normed_product if unit > first_out else weight_product)(
                    unit, *where
                ),
            )

        normed_plan("combined")
        group_load.wait()

        piece = width // n_dp

        def own_columns(chunk, _):
            right = n1_group[:, :, lane_block(chunk)].reshape(frames * tokens, BLOCK)
            value = dot_nn(d_turned[...], right).astype(jnp.bfloat16)
            for part in range(BLOCK // piece):
                z_send[chunk * (BLOCK // piece) + part] = value[
                    :, part * piece : (part + 1) * piece
                ]
            return 0

        lax.fori_loop(0, chunks, own_columns, 0)
        mod_load(2).start()
        mod_load(3).start()
        z_copies = [
            remote(
                z_send.at[dp_peers[hop]],
                z_recv.at[hop],
                z_send_sem.at[hop],
                z_recv_sem.at[hop],
                (dp_peers[hop], head),
            )
            for hop in range(n_dp - 1)
        ]
        for copy in z_copies:
            copy.start()
        normed_plan("columns")

        def cond_block(block, vector, first):
            vector = vector.astype(jnp.bfloat16).astype(jnp.float32)

            def body(index, _):
                rows = pl.ds(pl.multiple_of(index * 64, 64), 64)
                page = block % 2 * pages + lax.div(index, tokens // 64)
                inside = pl.ds(pl.multiple_of(lax.rem(index, tokens // 64) * 64, 64), 64)
                total = jnp.zeros((64, 128), jnp.float32) if first else cond_sum[rows, :]
                for lanes in range(0, width, 128):
                    total = total + n1_group[page, inside, lanes : lanes + 128].astype(
                        jnp.float32
                    ) * vector[:, lanes : lanes + 128]
                cond_sum[rows, :] = total
                return 0

            lax.fori_loop(0, width // 64, body, 0)

        mod_load(2).wait()
        cond_block(2, saved_rows[0], True)
        mod_load(4).start()
        mod_load(3).wait()
        cond_block(3, saved_rows[1], False)
        mod_load(5).start()
        normed_plan("cond1")
        mod_load(4).wait()
        cond_block(4, saved_rows[2], False)
        mod_load(0).start()
        mod_load(5).wait()
        cond_block(5, saved_rows[3], False)
        mod_load(1).start()
        normed_plan("cond2")

        for copy in z_copies:
            copy.wait()
        total = z_send[group].astype(jnp.float32)
        for hop in range(n_dp - 1):
            total = total + z_recv[hop].astype(jnp.float32)
        p_send[...] = total.T.reshape(8, small, 384)

        def part_copy(flips):
            peer = peer_head(head, flips)
            return remote(
                p_send.at[peer],
                p_recv.at[head],
                a2a_send.at[2, flips],
                a2a_recv.at[2, flips],
                (group, peer),
            )

        for flips in others:
            part_copy(flips).start()
        p_recv[head] = p_send[head]

        for unit in (first_out + 1, first_out + 2):
            second_copy(unit).wait()
            value = from_core[slot_of(unit), :, ybit, xbit].astype(jnp.float32)
            value = value + from_second[slot_of(unit)].astype(jnp.float32)
            first = (unit - first_out - 1) * half
            dn1[first : first + half, :] = value.reshape(half, width)

        def first_norm_back(index, sums):
            shift_sum, scale_sum = sums
            rows = row_block(index)
            value = x_ref[rows, :].astype(jnp.float32)
            scale = lax.rsqrt(jnp.mean(value * value, axis=1, keepdims=True) + EPSILON)
            normed = value * scale
            grad = dn1[rows, :]
            shift_sum = shift_sum + jnp.sum(grad, axis=0, keepdims=True)
            scale_sum = scale_sum + jnp.sum(grad * normed, axis=0, keepdims=True)
            inner = grad * (1.0 + scale_one)
            mean = jnp.mean(inner * normed, axis=1, keepdims=True)
            gin_ref[rows, :] = mid[rows, :] + scale * (inner - normed * mean)
            return shift_sum, scale_sum

        shift_one_grad, scale_one_grad = lax.fori_loop(
            0, steps, first_norm_back, (row_zero, row_zero)
        )
        cond = cond_ref[...].astype(jnp.float32)
        gate = 1.0 / (1.0 + jnp.exp(-cond))
        vectors = jnp.concatenate(
            [
                cond * gate,
                shift_one_grad,
                scale_one_grad,
                *saved_rows,
                row_zero,
            ],
            axis=0,
        )
        rows_ref[group, ybit, xbit, core] = vectors.astype(jnp.bfloat16)

        mine = rows_ref.at[group, ybit, xbit, core]
        row_dp = [
            remote(mine, mine, row_dp_send.at[hop], row_dp_recv.at[hop], (dp_peers[hop], head))
            for hop in range(n_dp - 1)
        ]
        y_part = rows_ref.at[:, ybit, xbit, core]
        x_part = rows_ref.at[:, :, xbit, core]
        core_part = rows_ref.at[:, :, :, core]
        row_y = remote(y_part, y_part, row_send.at[0], row_recv.at[0], (group, y_peer))
        row_x = remote(x_part, x_part, row_send.at[1], row_recv.at[1], (group, x_peer))
        row_core = remote(core_part, core_part, row_send.at[2], row_recv.at[2], (group, core_peer))
        for copy in row_dp:
            copy.start()
        run_plan("rows")
        mod_load(0).wait()
        cond_block(0, shift_one_grad, False)
        mod_load(1).wait()
        cond_block(1, scale_one_grad, False)
        gcond_ref[...] = jnp.sum(cond_sum[...].T, axis=0, keepdims=True) * (
            gate * (1.0 + cond * (1.0 - gate))
        )
        for copy in row_dp:
            copy.wait()
        row_y.start()
        run_plan("row_y")
        row_y.wait()
        row_x.start()
        run_plan("row_x")
        row_x.wait()
        row_core.start()
        for flips in others:
            part_copy(flips).wait()
        for block in range(8):
            for place, target in enumerate((gq_ref, gk_ref, gv_ref)):
                target[:, block * 128 : (block + 1) * 128] = p_recv[
                    block, :, place * 128 : (place + 1) * 128
                ]
        run_plan("row_core")
        row_core.wait()
        everyone = rows_ref[...].reshape(n_dp * 64, width)
        device = group * 8 + head
        wanted = lax.broadcasted_iota(jnp.int32, (small, width), 0) + device * small
        column = lax.broadcasted_iota(jnp.int32, (small, width), 1)
        picked = dot_nt(jnp.where(wanted == column, 1.0, 0.0).astype(jnp.bfloat16), everyone)
        place = lax.rem(lax.broadcasted_iota(jnp.int32, picked.shape, 1), 8)
        picked = jnp.where(place == 0, picked, 0.0)
        mod_out = []
        for block in range(6):
            left = pltpu.roll(picked, 1 + block, 1).astype(jnp.bfloat16)
            dn1[block * small : (block + 1) * small, :] = dot_nn(left, everyone)
            mod_out.append(
                pltpu.make_async_copy(
                    dn1.at[pl.ds(block * small, small), :],
                    gmod_hbm.at[:, pl.ds(block * width, width)],
                    load_sem.at[block],
                )
            )
            mod_out[-1].start()
        run_plan("end")
        for copy in mod_out:
            copy.wait()
        for unit in (count - 2, count - 1):
            core_copy(unit).wait_send()

    pl.run_scoped(
        attention_part,
        pltpu.VMEM((frames, tokens, 128), jnp.bfloat16),
        pltpu.VMEM((frames, tokens, 128), jnp.bfloat16),
        pltpu.VMEM((frames, tokens, 128), jnp.bfloat16),
        pltpu.VMEM((frames, tokens, 128), jnp.float32),
        pltpu.VMEM((frames, tokens, width), jnp.bfloat16),
        pltpu.VMEM((width, 384), jnp.bfloat16),
        pltpu.VMEM((SLOTS + 1, 128, tokens), jnp.float32),
        pltpu.VMEM((SLOTS + 1, tokens, 128), jnp.float32),
        pltpu.VMEM((SLOTS + 1, tokens, 128), jnp.float32),
        pltpu.VMEM((frames, 2, tokens), jnp.float32),
        pltpu.VMEM((2, frames // 2, tokens, 384), jnp.bfloat16),
        pltpu.VMEM((384, frames * tokens), jnp.bfloat16),
        pltpu.VMEM((tokens, width), jnp.float32),
        pltpu.VMEM((width, 128), jnp.float32),
    )


PLAN = {
    "fed": [("P", 0), ("P", 1)],
    "normed": [("C", 0), ("C", 1)],
    "attended": [("P", 2), ("P", 3)],
    "branch": [("C", 2), ("C", 3)],
    "outputs": [("P", 4), ("P", 5)],
    "scope": [("F", 0), ("F", 1)],
    2: [("P", 6)],
    4: [("P", 7)],
    6: [("P", 8)],
    12: [("C", 4)],
    13: [("C", 5)],
    "combined": [("P", 9), ("P", 10), ("S", 0), ("S", 1), ("F", 2), ("F", 3), ("C", 9), ("C", 10)],
    "columns": [("C", 8)],
    "cond2": [("F", 4), ("F", 5), ("S", 2), ("S", 3), ("F", 9), ("F", 10), ("C", 6), ("C", 7), ("S", 4), ("S", 5), ("F", 8), ("D", 0), ("D", 1)],
    "rows": [("D", 2), ("D", 3)],
    "row_y": [("D", 4), ("D", 5)],
    "row_x": [("F", 6), ("F", 7), ("S", 8)],
    "end": [("S", 6), ("S", 7), ("D", 8), ("D", 6), ("D", 7)],
}


def back_part(n_dp, vmem_operands, hbm_operands):
    table, attended, lse, hidden = vmem_operands[:4]
    hbm_up = hbm_operands[6]
    tokens, width = hidden.shape
    group_tokens = attended.shape[0]
    frames = group_tokens // tokens
    hidden_width = hbm_up.shape[1]
    devices = n_dp * 8
    small, large = width // devices, hidden_width // devices
    first_up = large // small
    tiles = hidden_width // width
    units = first_up + tiles + 3
    dma = pltpu.SemaphoreType.DMA
    f32, bf16 = jnp.float32, jnp.bfloat16
    shape = jax.ShapeDtypeStruct
    return pl.pallas_call(
        lambda *refs: back_kernel(n_dp, *refs),
        out_shape=(
            shape((tokens, width), bf16),
            shape((tokens, width), f32),
            shape((8, 128), f32),
            *[shape((small, width), f32)] * 4,
            shape((small, hidden_width), f32),
            shape((large, width), f32),
            shape((small, 6 * width), f32),
            shape((1, width), f32),
        ),
        in_specs=[IN_SMEM]
        + [IN_VMEM] * (len(vmem_operands) - 1)
        + [IN_PLACE] * len(hbm_operands),
        out_specs=(IN_PLACE, *[IN_VMEM] * 8, IN_PLACE, IN_VMEM),
        scratch_shapes=[
            pltpu.VMEM((tokens, 128), f32),
            pltpu.VMEM((tokens, width), bf16),
            pltpu.VMEM((frames, tokens, 128), bf16),
            pltpu.VMEM((units, n_dp, 2, 2, small, width), bf16),
            pltpu.VMEM((units, n_dp, 2, small, width), bf16),
            pltpu.VMEM((units, n_dp, small, width), bf16),
            pltpu.VMEM((units - 2, n_dp - 1, small, width), bf16),
            pltpu.VMEM((2, n_dp, 2, 2, small, width), bf16),
            pltpu.VMEM((tokens, width), bf16),
            pltpu.VMEM((first_up + 2, 2, width // 2, tokens), bf16),
            pltpu.VMEM((tokens, width), bf16),
            pltpu.VMEM((tokens, hidden_width), bf16),
            pltpu.VMEM((tokens, width), bf16),
            pltpu.VMEM((tokens, width), f32),
            pltpu.VMEM((n_dp, 2, 2, 2, 8, width), bf16),
            pltpu.VMEM((n_dp, 384, width // n_dp), bf16),
            pltpu.VMEM((n_dp - 1, 384, width // n_dp), bf16),
            pltpu.VMEM((8, small, 384), f32),
            pltpu.VMEM((8, small, 384), f32),
            dma((16,)),
            dma((3, 8)),
            dma((3, 8)),
            *[dma((units,))] * 6,
            dma((units, n_dp - 1)),
            dma((units, n_dp - 1)),
            dma((3,)),
            dma((3,)),
            dma((n_dp - 1,)),
            dma((n_dp - 1,)),
            dma((n_dp - 1,)),
            dma((n_dp - 1,)),
            dma((6, frames // 2)),
        ],
        compiler_params=pltpu.CompilerParams(
            collective_id=0, has_side_effects=True, vmem_limit_bytes=67043328
        ),
        name="back_part",
    )(*vmem_operands, *hbm_operands)


def finish_kernel(*refs):
    count = len(refs) // 3
    sources, targets = refs[:count], refs[count : 2 * count]
    held, (load_sem, store_sem) = refs[2 * count : 3 * count], refs[3 * count :]
    loads = [
        pltpu.make_async_copy(source, room, load_sem.at[place])
        for place, (source, room) in enumerate(zip(sources, held))
    ]
    stores = [
        pltpu.make_async_copy(room, target, store_sem.at[place])
        for place, (room, target) in enumerate(zip(held, targets))
    ]
    for copy in loads:
        copy.start()
    for place in range(count - 1):
        loads[place].wait()
        stores[place].start()
    loads[-1].wait()
    targets[-1][...] = held[-1][0:1, 0:3]
    for copy in stores[:-1]:
        copy.wait()


def finish(arrays):
    shapes = [jax.ShapeDtypeStruct(array.shape, array.dtype) for array in arrays]
    held = [pltpu.VMEM(array.shape, array.dtype) for array in arrays]
    shapes[-1] = jax.ShapeDtypeStruct((1, 3), jnp.float32)
    return pl.pallas_call(
        finish_kernel,
        out_shape=tuple(shapes),
        in_specs=[IN_PLACE] * len(arrays),
        out_specs=(*[IN_PLACE] * (len(arrays) - 1), IN_VMEM),
        scratch_shapes=[
            *held,
            pltpu.SemaphoreType.DMA((len(arrays),)),
            pltpu.SemaphoreType.DMA((len(arrays),)),
        ],
        name="finish",
    )(*arrays)


def tables_kernel(lengths, valid_ref, wave_ref, table, first_ref, rope_ref, bias_ref):
    frames = rope_ref.shape[0]
    ends = [lengths[0, 0]]
    for clip in range(1, lengths.shape[1] - 1):
        ends.append(ends[-1] + lengths[0, clip])
    columns = 2 * SLOTS + 4 * frames
    for slot in range(SLOTS):
        table[slot] = 0
        table[SLOTS + slot] = 0
    for frame in range(frames):
        for way in range(1, 4):
            table[columns + 4 * frame + way] = SLOTS
    used = jnp.int32(0)
    for frame in range(frames):
        first = jnp.int32(0)
        for end in ends:
            first = jnp.where(end <= frame, end, first)
        first_ref[frame] = first
        cosine, sine = wave_ref[0, 0:1, :], wave_ref[0, 1:2, :]
        for place in range(1, wave_ref.shape[0]):
            here = frame - first == place
            cosine = jnp.where(here, wave_ref[place, 0:1, :], cosine)
            sine = jnp.where(here, wave_ref[place, 1:2, :], sine)
        rope_ref[frame, 0:1, :] = cosine
        rope_ref[frame, 1:2, :] = sine
        for back in range(4):
            if back > frame:
                table[2 * SLOTS + 4 * frame + back] = SLOTS
                continue
            held = frame - back >= first
            slot = jnp.where(held, used, SLOTS)
            table[2 * SLOTS + 4 * frame + back] = slot
            table[columns + 4 * (frame - back) + back] = slot

            @pl.when(held)
            def _(slot=slot, frame=frame, back=back):
                table[slot] = frame
                table[SLOTS + slot] = frame - back

            used = used + jnp.where(held, 1, 0)
    for slot in range(SLOTS):
        table[columns + 4 * frames + slot] = jnp.where(table[slot] == table[SLOTS + slot], 1, 0)
    for row in range(valid_ref.shape[0]):
        keep = jnp.broadcast_to(valid_ref[row : row + 1, :], (128, 128)).astype(jnp.float32)
        bias_ref[row * 128 : (row + 1) * 128, :] = jnp.where(keep.T > 0.5, 0.0, MASKED)


def tables_part(lengths, valid):
    group_tokens = valid.shape[0]
    frames = group_tokens // PATCHES
    powers = 10000.0 ** (-np.arange(HEAD_DIM // 2, dtype=np.float64) / (HEAD_DIM // 2))
    angles = np.arange(4, dtype=np.float32)[:, None] * powers.astype(np.float32)[None]
    cosine, sine = np.cos(angles), np.sin(angles)
    wave = np.stack(
        [np.concatenate([cosine] * 4, axis=1), np.concatenate([-sine, sine] * 2, axis=1)], axis=1
    ).astype(np.float32)
    return pl.pallas_call(
        tables_kernel,
        out_shape=(
            jax.ShapeDtypeStruct((3 * SLOTS + 8 * frames,), jnp.int32),
            jax.ShapeDtypeStruct((frames,), jnp.int32),
            jax.ShapeDtypeStruct((frames, 2, 128), jnp.float32),
            jax.ShapeDtypeStruct((group_tokens, 128), jnp.float32),
        ),
        in_specs=[IN_SMEM, IN_VMEM, IN_VMEM],
        out_specs=(IN_SMEM, IN_SMEM, IN_VMEM, IN_VMEM),
        name="tables",
    )(lengths, valid.reshape(group_tokens // 128, 128), jnp.asarray(wave))


def front_kernel(*refs):
    (
        x_hbm,
        cond_ref,
        rope_ref,
        wq_hbm,
        wk_hbm,
        wv_hbm,
        wmod_hbm,
        n1_hbm,
        q_hbm,
        k_hbm,
        v_hbm,
        mod_ref,
        x_all,
        n1_all,
        q_all,
        k_all,
        v_all,
        w_own,
        wmod,
        cond_own,
        cond_all,
        steer,
        load_sem,
        mod_sem,
        out_sem,
        cond_send,
        cond_recv,
        gather_send,
        gather_recv,
    ) = refs
    tokens, width = x_hbm.shape
    frames = x_all.shape[0]
    half = tokens // 2
    group = lax.axis_index("dp")
    head = lax.axis_index("head")
    core = lax.rem(head, 2)
    xbit = lax.rem(lax.div(head, 2), 2)
    ybit = lax.div(head, 4)
    core_peer, x_peer, y_peer = peer_head(head, 1), peer_head(head, 2), peer_head(head, 4)
    diagonal = peer_head(head, 6)
    others = range(1, 8)
    barrier = pltpu.get_barrier_semaphore()
    for flips in others:
        pl.semaphore_signal(
            barrier, inc=1, device_id=(group, peer_head(head, flips)), device_id_type=MESH_ID
        )
    own_lanes = pl.ds(head * 128, 128)
    mod_loads = [
        pltpu.make_async_copy(
            wmod_hbm.at[:, pl.ds(block * width, width)], wmod.at[block], mod_sem.at[block]
        )
        for block in range(6)
    ]
    loads = [pltpu.make_async_copy(x_hbm, x_all.at[head], load_sem.at[0])] + [
        pltpu.make_async_copy(
            source.at[:, own_lanes], w_own.at[:, pl.ds(place * 128, 128)], load_sem.at[1 + place]
        )
        for place, source in enumerate((wq_hbm, wk_hbm, wv_hbm))
    ]
    for copy in mod_loads[:2] + loads + mod_loads[2:]:
        copy.start()
    value = cond_ref[...].astype(jnp.float32)
    act = jnp.broadcast_to(value / (1.0 + jnp.exp(-value)), (8, width)).astype(jnp.bfloat16)
    cond_own[...] = act
    cond_all[head] = act

    low, high = pl.ds(0, half), pl.ds(half, half)

    def gather_copy(index):
        if index == 0:
            source, target, peer = x_hbm.at[low], x_all.at[head, low], x_peer
        elif index == 1:
            source, target, peer = x_hbm.at[high], x_all.at[head, high], y_peer
        elif index == 2:
            source, target, peer = x_hbm.at[low], x_all.at[head, low], y_peer
        elif index == 3:
            source, target, peer = x_hbm.at[high], x_all.at[head, high], x_peer
        elif index == 4:
            source, target, peer = x_all.at[x_peer, low], x_all.at[x_peer, low], y_peer
        elif index == 5:
            source, target, peer = x_all.at[y_peer, high], x_all.at[y_peer, high], x_peer
        elif index == 6:
            source, target, peer = x_hbm, x_all.at[head], core_peer
        else:
            block = (x_peer, y_peer, y_peer, x_peer, diagonal, diagonal)[index - 7]
            rows = (low, high, low, high, low, high)[index - 7]
            source, target, peer = x_all.at[block, rows], x_all.at[block, rows], core_peer
        return remote(
            source, target, gather_send.at[index], gather_recv.at[index], (group, peer)
        )

    def cond_copy(flips):
        peer = peer_head(head, flips)
        return remote(
            cond_own, cond_all.at[head], cond_send.at[flips], cond_recv.at[flips], (group, peer)
        )

    pl.semaphore_wait(barrier, 7)
    for flips in others:
        cond_copy(flips).start()
    for index in (0, 1, 6, 2, 3):
        gather_copy(index).start()

    for flips in others:
        cond_copy(flips).wait()
    everyone = cond_all[...].reshape(frames * 8, width)

    def modulate(block):
        mod_loads[block].wait()

        def body(chunk, _):
            lanes = pl.ds(pl.multiple_of(chunk * BLOCK, BLOCK), BLOCK)
            steer[block, :, lanes] = dot_nn(everyone, wmod[block, :, lanes])
            return 0

        lax.fori_loop(0, width // BLOCK, body, 0)
        mod_ref[block : block + 1, :] = steer[block, pl.ds(pl.multiple_of(head * 8, 8), 8), :][0:1]

    modulate(0)
    modulate(1)
    for copy in loads:
        copy.wait()

    def out_copy(frame, rows, item):
        return pltpu.make_async_copy(
            n1_all.at[frame, rows], n1_hbm.at[frame, rows], out_sem.at[item]
        )

    def project(frame, side, item):
        steer_rows = pl.ds(pl.multiple_of(frame * 8, 8), 8)
        shift, scaling = steer[0, steer_rows, :][0:1], steer[1, steer_rows, :][0:1]

        def norm(index, _):
            rows = pl.ds(pl.multiple_of(side * half + index * 32, 32), 32)
            value = x_all[frame, rows, :].astype(jnp.float32)
            scale = lax.rsqrt(jnp.mean(value * value, axis=1, keepdims=True) + EPSILON)
            n1_all[frame, rows, :] = (value * scale * (1.0 + scaling) + shift).astype(
                jnp.bfloat16
            )
            return 0

        lax.fori_loop(0, half // 32, norm, 0)
        rows = pl.ds(pl.multiple_of(side * half, half), half)
        out_copy(frame, rows, item).start()
        value = dot_nn(n1_all[frame, rows, :], w_own[...])
        cosine, sine = rope_ref[frame, 0:1, :], rope_ref[frame, 1:2, :]
        for place, target in enumerate((q_all, k_all, v_all)):
            part = value[:, place * 128 : (place + 1) * 128]
            if place < 2:
                part = part * cosine + turn_pairs(part) * sine
            target[frame, rows, :] = part.astype(jnp.bfloat16)

    def stage(number, other_core):
        at_core = 1 - core if other_core else core

        def body(index, _):
            if number == 0:
                at_x, at_y, side = xbit, ybit, index
            elif number == 3:
                at_x, at_y, side = 1 - xbit, 1 - ybit, index
            else:
                at_x = xbit + (1 - index) * (1 - 2 * xbit)
                at_y = ybit + index * (1 - 2 * ybit)
                side = index if number == 1 else 1 - index
            frame = 4 * at_y + 2 * at_x + at_core
            project(frame, side, number * 4 + other_core * 2 + index)
            return 0

        lax.fori_loop(0, 2, body, 0)

    stage(0, 0)
    gather_copy(6).wait()
    stage(0, 1)
    for block in range(2, 6):
        modulate(block)
    for number, arrivals in ((1, (0, 1)), (2, (2, 3)), (3, (4, 5))):
        for index in arrivals:
            gather_copy(index).wait()
            if number == 1:
                gather_copy(index + 4).start()
            gather_copy(index + 7).start()
        stage(number, 0)
        for index in arrivals:
            gather_copy(index + 7).wait()
        stage(number, 1)
    outs = [
        pltpu.make_async_copy(source, target, load_sem.at[place])
        for place, (source, target) in enumerate(((q_all, q_hbm), (k_all, k_hbm), (v_all, v_hbm)))
    ]
    for copy in outs:
        copy.start()
    for item in range(16):
        out_copy(0, low, item).wait()
    for copy in outs:
        copy.wait()


def front_part(hidden, cond, rope, query_weight, key_weight, value_weight, modulation_weight):
    tokens, width = hidden.shape
    frames = rope.shape[0]
    dma = pltpu.SemaphoreType.DMA
    bf16, f32 = jnp.bfloat16, jnp.float32
    in_hbm = pl.BlockSpec(memory_space=pltpu.HBM)
    block = jax.ShapeDtypeStruct((frames, tokens, 128), bf16)
    return pl.pallas_call(
        front_kernel,
        out_shape=(
            jax.ShapeDtypeStruct((frames, tokens, width), bf16),
            block,
            block,
            block,
            jax.ShapeDtypeStruct((8, width), f32),
        ),
        in_specs=[in_hbm, IN_VMEM, IN_VMEM] + [in_hbm] * 4,
        out_specs=(in_hbm,) * 4 + (IN_VMEM,),
        scratch_shapes=[
            pltpu.VMEM((frames, tokens, width), bf16),
            pltpu.VMEM((frames, tokens, width), bf16),
            pltpu.VMEM((frames, tokens, 128), bf16),
            pltpu.VMEM((frames, tokens, 128), bf16),
            pltpu.VMEM((frames, tokens, 128), bf16),
            pltpu.VMEM((width, 384), bf16),
            pltpu.VMEM((6, width, width), bf16),
            pltpu.VMEM((8, width), bf16),
            pltpu.VMEM((frames, 8, width), bf16),
            pltpu.VMEM((6, frames * 8, width), f32),
            dma((4,)),
            dma((6,)),
            dma((16,)),
            dma((8,)),
            dma((8,)),
            dma((13,)),
            dma((13,)),
        ],
        compiler_params=pltpu.CompilerParams(
            collective_id=1, has_side_effects=True, vmem_limit_bytes=67043328
        ),
        name="front_part",
    )(hidden, cond, rope, query_weight, key_weight, value_weight, modulation_weight)


def per_device(
    hidden_in,
    frame_cond,
    query_weight,
    key_weight,
    value_weight,
    output_weight,
    up_weight,
    down_weight,
    modulation_weight,
    clip_lengths,
    patch_valid,
    cotangent,
):
    tok_dev, model_width = hidden_in.shape
    group_tokens = patch_valid.shape[0]
    frames = group_tokens // PATCHES
    head_index = lax.axis_index("head")
    n_dp = lax.axis_size("dp")
    table, first_frames, rope, bias = tables_part(clip_lengths, patch_valid)
    normed_group, head_query, head_key, head_value, modulation = front_part(
        hidden_in, frame_cond, rope, query_weight, key_weight, value_weight, modulation_weight
    )
    attended, logsum = attend_forward(
        first_frames,
        *[array.reshape(group_tokens, 128) for array in (head_query, head_key, head_value)],
        bias,
    )
    results = back_part(
        n_dp,
        (table, attended, logsum, hidden_in, cotangent, modulation, rope, frame_cond),
        (
            head_query,
            head_key,
            head_value,
            bias.reshape(frames, PATCHES, 128),
            normed_group,
            output_weight,
            up_weight,
            down_weight,
            query_weight,
            key_weight,
            value_weight,
            modulation_weight,
        ),
    )
    (block_out, grad_input, statistics, gq, gk, gv, go, gup, gdown, gmod, gcond) = results
    (grad_input, gmod, block_out, gup, gdown, gq, gk, gv, go, gcond, statistics) = finish(
        (grad_input, gmod, block_out, gup, gdown, gq, gk, gv, go, gcond, statistics)
    )
    return (
        block_out,
        grad_input,
        gcond,
        gq,
        gk,
        gv,
        go,
        gup,
        gdown,
        gmod,
        statistics,
    )


def solution(mesh):
    in_specs = (
        P(("dp", "head"), None),
        P(("dp", "head"), None),
        P(),
        P(),
        P(),
        P(),
        P(),
        P(),
        P(),
        P("dp", None),
        P("dp"),
        P(("dp", "head"), None),
    )
    out_specs = (
        P(("dp", "head"), None),
        P(("dp", "head"), None),
        P(("dp", "head"), None),
        P(("dp", "head"), None),
        P(("dp", "head"), None),
        P(("dp", "head"), None),
        P(("dp", "head"), None),
        P(("dp", "head"), None),
        P(("dp", "head"), None),
        P(("dp", "head"), None),
        P(("dp", "head"), None),
    )
    return jax.shard_map(
        per_device, mesh=mesh, in_specs=in_specs, out_specs=out_specs, check_vma=False
    )
```

```python
import math

import jax
import jax.numpy as jnp
import numpy as np
from jax import lax
from jax.experimental import pallas as pl
from jax.experimental.pallas import tpu as pltpu
from jax.sharding import PartitionSpec as P

HEADS = 16
HEAD_DIM = 64
PATCHES = 256


EPSILON = 1e-06
MASKED = -1e30


def dot_nt(left, right):
    return lax.dot_general(
        left, right, (((1,), (1,)), ((), ())), preferred_element_type=jnp.float32
    )


def dot_nn(left, right):
    return lax.dot_general(
        left, right, (((1,), (0,)), ((), ())), preferred_element_type=jnp.float32
    )


def head_parts(block):
    lane = lax.broadcasted_iota(jnp.int32, block.shape, 1)
    zero = jnp.zeros_like(block)
    return jnp.where(lane < HEAD_DIM, block, zero), jnp.where(lane < HEAD_DIM, zero, block)


def key_bias(bias_ref, key_frame, frame):
    half = bias_ref[pl.ds(key_frame * PATCHES, PATCHES), :]
    bias = jnp.concatenate([half, half], axis=1)
    row = lax.broadcasted_iota(jnp.int32, bias.shape, 0)
    column = lax.broadcasted_iota(jnp.int32, bias.shape, 1)
    own = (row == column) & (key_frame == frame)
    return jnp.where(own, 0.0, bias)


def attend_forward_kernel(first_ref, q_ref, k_ref, v_ref, bias_ref, o_ref, lse_ref, scores):
    frames = q_ref.shape[0] // PATCHES

    def one_frame(frame, _):
        rows = pl.ds(frame * PATCHES, PATCHES)
        parts = head_parts(q_ref[rows, :] * jnp.bfloat16(0.125))
        first = first_ref[frame]

        def score(key_frame, tops):
            keys = k_ref[pl.ds(key_frame * PATCHES, PATCHES), :]
            bias = key_bias(bias_ref, key_frame, frame)
            new = []
            for head in range(2):
                value = dot_nt(keys, parts[head]) + bias
                scores[head, key_frame - first] = value
                new.append(jnp.maximum(tops[head], jnp.max(value, axis=0, keepdims=True)))
            return tuple(new)

        low = jnp.full((1, PATCHES), MASKED, jnp.float32)
        tops = lax.fori_loop(first, frame + 1, score, (low, low))

        def weigh(key_frame, carry):
            turned = v_ref[pl.ds(key_frame * PATCHES, PATCHES), :].T
            totals, sums = [], []
            for head in range(2):
                value = jnp.exp(scores[head, key_frame - first] - tops[head])
                totals.append(carry[head] + jnp.sum(value, axis=0, keepdims=True))
                sums.append(
                    carry[2 + head]
                    + dot_nn(
                        turned[head * HEAD_DIM : (head + 1) * HEAD_DIM, :],
                        value.astype(jnp.bfloat16),
                    )
                )
            return (*totals, *sums)

        zero = jnp.zeros((1, PATCHES), jnp.float32)
        empty = jnp.zeros((HEAD_DIM, PATCHES), jnp.float32)
        carry = lax.fori_loop(first, frame + 1, weigh, (zero, zero, empty, empty))
        totals = carry[:2]
        sums = [carry[2 + head] * (1.0 / totals[head]) for head in range(2)]
        o_ref[rows, :] = jnp.concatenate(sums, axis=0).T.astype(jnp.bfloat16)
        for head in range(2):
            lse_ref[frame, head : head + 1, :] = tops[head] + jnp.log(totals[head])
        return 0

    lax.fori_loop(0, frames, one_frame, 0)


IN_SMEM = pl.BlockSpec(memory_space=pltpu.SMEM)
IN_VMEM = pl.BlockSpec(memory_space=pltpu.VMEM)
IN_PLACE = pl.BlockSpec(memory_space=pl.ANY)
MESH_ID = pl.DeviceIdType.MESH


def attend_forward(first, queries, keys, values, bias):
    tokens, width = queries.shape
    frames = tokens // PATCHES
    return pl.pallas_call(
        attend_forward_kernel,
        out_shape=(
            jax.ShapeDtypeStruct((tokens, width), jnp.bfloat16),
            jax.ShapeDtypeStruct((frames, 2, PATCHES), jnp.float32),
        ),
        in_specs=[IN_SMEM] + [IN_VMEM] * 4,
        out_specs=(IN_VMEM, IN_VMEM),
        scratch_shapes=[pltpu.VMEM((2, 4, PATCHES, PATCHES), jnp.float32)],
        name="attend_forward",
    )(first, queries, keys, values, bias)


SLOTS = 17
BLOCK = 256


def peer_head(head, flips):
    core = lax.rem(head, 2)
    second = lax.rem(lax.div(head, 2), 2)
    third = lax.div(head, 4)
    if flips % 2:
        core = 1 - core
    if flips // 2 % 2:
        second = 1 - second
    if flips // 4:
        third = 1 - third
    return 4 * third + 2 * second + core


def remote(source, target, send, receive, where):
    return pltpu.make_async_remote_copy(
        src_ref=source,
        dst_ref=target,
        send_sem=send,
        recv_sem=receive,
        device_id=where,
        device_id_type=MESH_ID,
    )


def gelu_and_slope(value):
    square = value * value
    inner = 0.7978845608028654 * value * (1.0 + 0.044715 * square)
    bend = jnp.tanh(inner)
    half = 0.5 * (1.0 + bend)
    slope = half + 0.5 * value * (1.0 - bend * bend) * (
        0.7978845608028654 * (1.0 + 0.134145 * square)
    )
    return value * half, slope


def turn_pairs(values):
    lane = lax.rem(lax.broadcasted_iota(jnp.int32, values.shape, 1), HEAD_DIM)
    up = pltpu.roll(values, 128 - HEAD_DIM // 2, 1)
    down = pltpu.roll(values, HEAD_DIM // 2, 1)
    return jnp.where(lane < HEAD_DIM // 2, up, down)


def back_kernel(n_dp, *refs):
    (
        table,
        att_own,
        lse_ref,
        x_ref,
        cot_ref,
        mod_ref,
        rope_ref,
        cond_ref,
        q_hbm,
        k_hbm,
        v_hbm,
        bias_hbm,
        n1_hbm,
        wo_hbm,
        up_hbm,
        down_hbm,
        wq_hbm,
        wk_hbm,
        wv_hbm,
        wmod_hbm,
        block_hbm,
        gin_ref,
        stat_ref,
        gq_ref,
        gk_ref,
        gv_ref,
        go_ref,
        gup_ref,
        gdown_ref,
        gmod_hbm,
        gcond_ref,
        valid_ref,
        att_fr,
        do_own,
        from_core,
        from_first,
        from_second,
        from_dp,
        core_out,
        da_send,
        lhs,
        dmlp,
        dhid,
        dattn,
        mid,
        rows_ref,
        z_send,
        z_recv,
        p_send,
        p_recv,
        load_sem,
        a2a_send,
        a2a_recv,
        core_send,
        core_recv,
        first_send,
        first_recv,
        second_send,
        second_recv,
        dp_send,
        dp_recv,
        row_send,
        row_recv,
        row_dp_send,
        row_dp_recv,
        z_send_sem,
        z_recv_sem,
        mod_sem,
    ) = refs
    tokens, width = x_ref.shape
    frames = q_hbm.shape[0]
    hidden_width = up_hbm.shape[1]
    tiles = hidden_width // width
    chunks = width // BLOCK
    small = width // (n_dp * 8)
    large = hidden_width // (n_dp * 8)
    half_rows = n_dp * 4 * small
    group = lax.axis_index("dp")
    head = lax.axis_index("head")
    core = lax.rem(head, 2)
    xbit = lax.rem(lax.div(head, 2), 2)
    ybit = lax.div(head, 4)
    core_peer, x_peer, y_peer = peer_head(head, 1), peer_head(head, 2), peer_head(head, 4)
    dp_peers = [lax.rem(group + hop, n_dp) for hop in range(1, n_dp)]
    others = range(1, 8)

    barrier = pltpu.get_barrier_semaphore()
    for flips in others:
        pl.semaphore_signal(
            barrier, inc=1, device_id=(group, peer_head(head, flips)), device_id_type=MESH_ID
        )
    for peer in dp_peers:
        pl.semaphore_signal(barrier, inc=1, device_id=(peer, head), device_id_type=MESH_ID)

    pl.semaphore_wait(barrier, 7 + len(dp_peers))

    own_rows = pl.ds(head * tokens, tokens)
    own_lanes = pl.ds(head * 128, 128)

    def att_copy(flips):
        peer = peer_head(head, flips)
        return remote(
            att_own.at[pl.ds(peer * tokens, tokens), :],
            att_fr.at[:, own_lanes],
            a2a_send.at[0, flips],
            a2a_recv.at[0, flips],
            (group, peer),
        )

    def grad_copy(flips):
        peer = peer_head(head, flips)
        return remote(
            da_send.at[:, pl.ds(peer * 128, 128)],
            do_own.at[head],
            a2a_send.at[1, flips],
            a2a_recv.at[1, flips],
            (group, peer),
        )

    first_up = large // small
    first_out = first_up + tiles
    count = first_out + 3

    def slot_of(unit):
        return unit

    def lhs_of(unit):
        if unit < first_up:
            return unit
        return first_up if unit < first_out else first_up + 1

    def core_copy(unit):
        return remote(
            core_out.at[unit % 2],
            from_core.at[slot_of(unit)],
            core_send.at[unit],
            core_recv.at[unit],
            (group, core_peer),
        )

    def x_leads(unit):
        return unit % 2 == 0

    def first_copy(unit):
        slot = slot_of(unit)
        if x_leads(unit):
            source, peer = from_core.at[slot, :, :, 1 - xbit], x_peer
        else:
            source, peer = from_core.at[slot, :, 1 - ybit], y_peer
        return remote(
            source, from_first.at[slot], first_send.at[unit], first_recv.at[unit], (group, peer)
        )

    def second_copy(unit):
        slot = slot_of(unit)
        if x_leads(unit):
            source, peer = from_core.at[slot, :, 1 - ybit, xbit], y_peer
        else:
            source, peer = from_core.at[slot, :, ybit, 1 - xbit], x_peer
        return remote(
            source, from_second.at[slot], second_send.at[unit], second_recv.at[unit], (group, peer)
        )

    def dp_copy(unit, hop):
        peer = dp_peers[hop]
        return remote(
            from_core.at[slot_of(unit), peer, ybit, xbit],
            from_dp.at[unit, hop],
            dp_send.at[unit, hop],
            dp_recv.at[unit, hop],
            (peer, head),
        )

    def added(left, right):
        return (left.astype(jnp.float32) + right.astype(jnp.float32)).astype(jnp.bfloat16)

    def put(target, lanes, value, unit):
        value = value.astype(jnp.bfloat16)
        if unit <= first_out:
            target[:, :, :, :, lanes] = value.reshape(n_dp, 2, 2, small, BLOCK)
        else:
            value = value.reshape(4, n_dp, small, BLOCK)
            for chip in range(4):
                target[:, chip // 2, chip % 2, :, lanes] = value[chip]

    def got(source, lanes, unit):
        if unit <= first_out:
            return source[:, :, :, :, lanes].reshape(half_rows, BLOCK)
        return jnp.concatenate(
            [
                source[:, chip // 2, chip % 2, :, lanes].reshape(half_rows // 4, BLOCK)
                for chip in range(4)
            ],
            axis=0,
        )

    def produce(unit, product):
        if unit >= 2:
            core_copy(unit - 2).wait_send()

        def body(chunk, _):
            lanes = pl.ds(pl.multiple_of(chunk * BLOCK, BLOCK), BLOCK)
            put(core_out.at[unit % 2], lanes, product(unit, 1 - core, chunk), unit)
            return 0

        lax.fori_loop(0, chunks, body, 0)
        core_copy(unit).start()

    def take_core(unit, product):
        core_copy(unit).wait_recv()
        place = from_core.at[slot_of(unit)]

        def body(chunk, _):
            lanes = pl.ds(pl.multiple_of(chunk * BLOCK, BLOCK), BLOCK)
            value = product(unit, core, chunk) + got(place, lanes, unit).astype(jnp.float32)
            put(place, lanes, value, unit)
            return 0

        lax.fori_loop(0, chunks, body, 0)
        first_copy(unit).start()

    def take_first(unit):
        first_copy(unit).wait()
        slot = slot_of(unit)

        def body(index, _):
            at_dp = lax.div(index, 2)
            other = lax.rem(index, 2)
            at_y, at_x = (other, xbit) if x_leads(unit) else (ybit, other)
            from_core[slot, at_dp, at_y, at_x] = added(
                from_core[slot, at_dp, at_y, at_x], from_first[slot, at_dp, other]
            )
            return 0

        lax.fori_loop(0, n_dp * 2, body, 0)
        second_copy(unit).start()

    def take_second(unit):
        second_copy(unit).wait()
        slot = slot_of(unit)

        def body(at_dp, _):
            from_core[slot, at_dp, ybit, xbit] = added(
                from_core[slot, at_dp, ybit, xbit], from_second[slot, at_dp]
            )
            return 0

        lax.fori_loop(0, n_dp, body, 0)
        for hop in range(n_dp - 1):
            dp_copy(unit, hop).start()

    def take_dp(unit):
        for hop in range(n_dp - 1):
            dp_copy(unit, hop).wait()
        total = from_core[slot_of(unit), group, ybit, xbit].astype(jnp.float32)
        for hop in range(n_dp - 1):
            total = total + from_dp[unit, hop].astype(jnp.float32)
        if unit < first_up:
            gdown_ref[unit * small : (unit + 1) * small, :] = total
        elif unit < first_out:
            place = (unit - first_up) * width
            gup_ref[:, place : place + width] = total
        else:
            go_ref[...] = total

    def turned_rows(index, source):
        for chunk in range(chunks):
            value = source[:, chunk * BLOCK : (chunk + 1) * BLOCK].T
            value = value.reshape(BLOCK // (2 * small), 2, small, tokens)
            for side in range(2):
                lhs[index, side, chunk * BLOCK // 2 : (chunk + 1) * BLOCK // 2, :] = value[
                    :, side
                ].reshape(BLOCK // 2, tokens)

    shift_one, scale_one, gate_one = (mod_ref[row : row + 1, :] for row in range(3))
    shift_two, scale_two, gate_two = (mod_ref[row : row + 1, :] for row in range(3, 6))
    step_rows = 32
    steps = tokens // step_rows

    def row_block(index):
        return pl.ds(pl.multiple_of(index * step_rows, step_rows), step_rows)

    def lane_block(chunk):
        return pl.ds(pl.multiple_of(chunk * BLOCK, BLOCK), BLOCK)

    def masked_square(values, rows):
        counted = jnp.where(valid_ref[rows, :1] < -1.0, 0.0, 1.0)
        sums = jnp.sum(values * values, axis=1, keepdims=True) * counted
        return jnp.sum(sums, axis=0, keepdims=True)

    one = jnp.zeros((1, 1), jnp.float32)
    row_zero = jnp.zeros((1, width), jnp.float32)

    valid_load = pltpu.make_async_copy(bias_hbm.at[head], valid_ref, load_sem.at[15])
    valid_load.start()
    for flips in others:
        att_copy(flips).start()
    att_fr[:, own_lanes] = att_own[own_rows, :]

    def weight_product(unit, side, chunk):
        if unit < first_up:
            right = dmlp[:, lane_block(chunk)]
        elif unit < first_out:
            start = (unit - first_up) * width + chunk * BLOCK
            right = dhid[:, pl.ds(pl.multiple_of(start, BLOCK), BLOCK)]
        else:
            right = dattn[:, lane_block(chunk)]
        return dot_nn(lhs[lhs_of(unit), side], right)

    def run_plan(point, product=weight_product):
        for kind, unit in PLAN.get(point, ()):
            if kind == "P":
                produce(unit, product)
            elif kind == "C":
                take_core(unit, product)
            elif kind == "F":
                take_first(unit)
            elif kind == "S":
                take_second(unit)
            else:
                take_dp(unit)

    half = tokens // 2

    def mlp_part(up, down, act, dn2, wo, ba, n2):
        wo_load = pltpu.make_async_copy(wo_hbm, wo, load_sem.at[0])
        wo_load.start()
        up_loads = [
            pltpu.make_async_copy(
                up_hbm.at[:, pl.ds(tile * width, width)],
                up.at[:, pl.ds(tile * width, width)],
                load_sem.at[1 + tile],
            )
            for tile in range(tiles)
        ]
        down_loads = [
            pltpu.make_async_copy(
                down_hbm.at[pl.ds(tile * width, width), :],
                down.at[pl.ds(tile * width, width), :],
                load_sem.at[1 + tiles + tile],
            )
            for tile in range(tiles)
        ]
        for tile in range(tiles):
            up_loads[tile].start()
            down_loads[tile].start()

        valid_load.wait()
        wo_load.wait()
        for flips in others:
            att_copy(flips).wait()
        turned_rows(first_up + 1, att_fr)

        def project(chunk, _):
            lanes = lane_block(chunk)
            ba[:, lanes] = dot_nn(att_fr[...], wo[:, lanes])
            return 0

        lax.fori_loop(0, chunks, project, 0)

        def second_norm(index, total):
            rows = row_block(index)
            branch = gate_one * ba[rows, :]
            value = x_ref[rows, :].astype(jnp.float32) + branch
            mid[rows, :] = value
            scale = lax.rsqrt(jnp.mean(value * value, axis=1, keepdims=True) + EPSILON)
            n2[rows, :] = (value * scale * (1.0 + scale_two) + shift_two).astype(jnp.bfloat16)
            dmlp[rows, :] = (gate_two * cot_ref[rows, :].astype(jnp.float32)).astype(jnp.bfloat16)
            return total + masked_square(branch, rows)

        stat_attn = lax.fori_loop(0, steps, second_norm, one)
        turned_rows(first_up, n2)

        pairs = BLOCK // (2 * large)

        def feed(index, _):
            @pl.when(lax.rem(index, chunks) == 0)
            def _():
                tile = lax.div(index, chunks)
                pltpu.make_async_copy(
                    up_hbm.at[:, pl.ds(0, width)],
                    up.at[:, pl.ds(0, width)],
                    load_sem.at[1 + tile],
                ).wait()
                pltpu.make_async_copy(
                    down_hbm.at[pl.ds(0, width), :],
                    down.at[pl.ds(0, width), :],
                    load_sem.at[1 + tiles + tile],
                ).wait()

            lanes = lane_block(index)
            active, slope = gelu_and_slope(dot_nn(n2[...], up[:, lanes]))
            active = active.astype(jnp.bfloat16)
            act[:, lanes] = active
            grad = dot_nt(dmlp[...], down[lanes, :])
            dhid[:, lanes] = (grad * slope).astype(jnp.bfloat16)
            turned = active.T.reshape(pairs, 2, first_up, small, tokens)
            where = pl.ds(pl.multiple_of(index * pairs * small, pairs * small), pairs * small)
            for unit in range(first_up):
                for side in range(2):
                    lhs[unit, side, where, :] = turned[:, side, unit].reshape(
                        pairs * small, tokens
                    )
            return 0

        lax.fori_loop(0, hidden_width // BLOCK, feed, 0)

        run_plan("fed")

        def to_normed(chunk, _):
            lanes = lane_block(chunk)
            dn2[:, lanes] = dot_nt(dhid[...], up[lanes, :])
            return 0

        lax.fori_loop(0, chunks, to_normed, 0)
        run_plan("normed")

        def second_norm_back(index, sums):
            shift_sum, scale_sum, gate_sum = sums
            rows = row_block(index)
            value = mid[rows, :]
            scale = lax.rsqrt(jnp.mean(value * value, axis=1, keepdims=True) + EPSILON)
            normed = value * scale
            grad = dn2[rows, :]
            shift_sum = shift_sum + jnp.sum(grad, axis=0, keepdims=True)
            scale_sum = scale_sum + jnp.sum(grad * normed, axis=0, keepdims=True)
            inner = grad * (1.0 + scale_two)
            mean = jnp.mean(inner * normed, axis=1, keepdims=True)
            total = cot_ref[rows, :].astype(jnp.float32) + scale * (inner - normed * mean)
            dn2[rows, :] = total
            gate_sum = gate_sum + jnp.sum(total * ba[rows, :], axis=0, keepdims=True)
            dattn[rows, :] = (gate_one * total).astype(jnp.bfloat16)
            return shift_sum, scale_sum, gate_sum

        shift_two_grad, scale_two_grad, gate_one_grad = lax.fori_loop(
            0, steps, second_norm_back, (row_zero, row_zero, row_zero)
        )

        def to_attended(chunk, _):
            lanes = lane_block(chunk)
            da_send[:, lanes] = dot_nt(dattn[...], wo[lanes, :]).astype(jnp.bfloat16)
            return 0

        lax.fori_loop(0, chunks, to_attended, 0)
        for flips in others:
            grad_copy(flips).start()
        do_own[head] = da_send[:, own_lanes]

        run_plan("attended")

        def branch_out(chunk, _):
            lanes = lane_block(chunk)
            ba[:, lanes] = dot_nn(act[...], down[:, lanes])
            return 0

        lax.fori_loop(0, chunks, branch_out, 0)
        run_plan("branch")

        def outputs(index, sums):
            gate_sum, stat_mlp, stat_out = sums
            rows = row_block(index)
            raw = ba[rows, :]
            branch = gate_two * raw
            value = mid[rows, :] + branch
            n2[rows, :] = value.astype(jnp.bfloat16)
            gate_sum = gate_sum + jnp.sum(
                cot_ref[rows, :].astype(jnp.float32) * raw, axis=0, keepdims=True
            )
            stat_mlp = stat_mlp + masked_square(branch, rows)
            stat_out = stat_out + masked_square(value, rows)
            mid[rows, :] = dn2[rows, :]
            return gate_sum, stat_mlp, stat_out

        gate_two_grad, stat_mlp, stat_out = lax.fori_loop(0, steps, outputs, (row_zero, one, one))
        lane = lax.broadcasted_iota(jnp.int32, stat_ref.shape, 1)
        stats = jnp.where(lane == 0, stat_attn, jnp.where(lane == 1, stat_mlp, stat_out))
        stat_ref[...] = jnp.sqrt(stats / (tokens * width) + EPSILON)
        for row, vector in (
            (3, gate_one_grad),
            (4, shift_two_grad),
            (5, scale_two_grad),
            (6, gate_two_grad),
        ):
            gin_ref[row : row + 1, :] = vector
        block_copy = pltpu.make_async_copy(n2, block_hbm, load_sem.at[0])
        block_copy.start()
        run_plan("outputs")
        block_copy.wait()

    pl.run_scoped(
        mlp_part,
        pltpu.VMEM((width, hidden_width), jnp.bfloat16),
        pltpu.VMEM((hidden_width, width), jnp.bfloat16),
        pltpu.VMEM((tokens, hidden_width), jnp.bfloat16),
        pltpu.VMEM((tokens, width), jnp.float32),
        pltpu.VMEM((width, width), jnp.bfloat16),
        pltpu.VMEM((tokens, width), jnp.float32),
        pltpu.VMEM((tokens, width), jnp.bfloat16),
    )
    saved_rows = [gin_ref[row : row + 1, :] for row in range(3, 7)]

    def attention_part(
        q_ref,
        k_ref,
        v_ref,
        bias_ref,
        n1_group,
        w_own,
        dq_slots,
        dk_slots,
        dv_slots,
        deltas,
        d_all,
        d_turned,
        dn1,
        cond_sum,
    ):
        pieces = [
            (q_hbm, q_ref),
            (k_hbm, k_ref),
            (v_hbm, v_ref),
            (bias_hbm, bias_ref),
            (wq_hbm.at[:, own_lanes], w_own.at[:, pl.ds(0, 128)]),
            (wk_hbm.at[:, own_lanes], w_own.at[:, pl.ds(128, 128)]),
            (wv_hbm.at[:, own_lanes], w_own.at[:, pl.ds(256, 128)]),
        ]
        loads = [
            pltpu.make_async_copy(source, target, load_sem.at[1 + place])
            for place, (source, target) in enumerate(pieces)
        ]
        for copy in loads:
            copy.start()

        pages = frames // 2

        class mod_load:
            def __init__(self, block):
                self.copies = [
                    pltpu.make_async_copy(
                        wmod_hbm.at[pl.ds(page * tokens, tokens), pl.ds(block * width, width)],
                        n1_group.at[block % 2 * pages + page],
                        mod_sem.at[block, page],
                    )
                    for page in range(pages)
                ]

            def start(self):
                for copy in self.copies:
                    copy.start()

            def wait(self):
                for copy in self.copies:
                    copy.wait()

        group_load = pltpu.make_async_copy(n1_hbm, n1_group, load_sem.at[0])
        group_load.start()
        run_plan("scope")
        for flips in others:
            grad_copy(flips).wait()
        for copy in loads:
            copy.wait()
        for slots in (dq_slots, dk_slots, dv_slots):
            slots[SLOTS] = jnp.zeros(slots.shape[1:], jnp.float32)

        def frame_delta(frame, _):
            rows = pl.ds(pl.multiple_of(frame * tokens, tokens), tokens)
            product = (
                do_own[frame].astype(jnp.float32) * att_own[rows, :].astype(jnp.float32)
            ).T
            for part in range(2):
                deltas[frame, part : part + 1, :] = jnp.sum(
                    product[part * HEAD_DIM : (part + 1) * HEAD_DIM, :], axis=0, keepdims=True
                )
            return 0

        lax.fori_loop(0, frames, frame_delta, 0)

        def one_slot(index, _):
            frame = table[index]
            key_frame = table[SLOTS + index]
            q_parts = head_parts(q_ref[frame] * jnp.bfloat16(0.125))
            do_parts = head_parts(do_own[frame])
            keys = k_ref[key_frame]
            values = v_ref[key_frame]
            turned = keys.T
            half = bias_ref[key_frame]
            row = lax.broadcasted_iota(jnp.int32, (tokens, tokens), 0)
            column = lax.broadcasted_iota(jnp.int32, (tokens, tokens), 1)
            same = table[2 * SLOTS + 8 * frames + index].astype(jnp.float32)
            keep = 1.0 - jnp.where(row == column, 1.0, 0.0) * same
            bias = jnp.concatenate([half, half], axis=1) * keep
            dv = dk = None
            dq = []
            for part in range(2):
                lse = lse_ref[frame, part : part + 1, :]
                delta = deltas[frame, part : part + 1, :]
                probs = jnp.exp(dot_nt(keys, q_parts[part]) + bias - lse)
                prob_grad = dot_nt(values, do_parts[part])
                score_grad = (probs * (prob_grad - delta)).astype(jnp.bfloat16)
                dv_part = dot_nn(probs.astype(jnp.bfloat16), do_parts[part])
                dk_part = dot_nn(score_grad, q_parts[part])
                dv = dv_part if dv is None else dv + dv_part
                dk = dk_part if dk is None else dk + dk_part
                dq.append(
                    dot_nn(turned[part * HEAD_DIM : (part + 1) * HEAD_DIM, :], score_grad)
                )
            dv_slots[index] = dv
            dk_slots[index] = dk
            dq_slots[index] = jnp.concatenate(dq, axis=0)
            for place in range(SLOTS):
                if PLAN.get(place):
                    pl.when(index == place)(lambda place=place: run_plan(place))
            return 0

        lax.fori_loop(0, SLOTS, one_slot, 0)

        def summed(slots, start, frame):
            total = slots[table[start + 4 * frame]]
            for way in range(1, 4):
                total = total + slots[table[start + 4 * frame + way]]
            return total

        def combine(frame, _):
            side, chip = lax.rem(frame, 2), lax.div(frame, 2)
            cosine = rope_ref[frame, 0:1, :]
            sine = rope_ref[frame, 1:2, :]

            def turned_back(value):
                value = value.astype(jnp.bfloat16).astype(jnp.float32)
                return (value * cosine - turn_pairs(value) * sine).astype(jnp.bfloat16)

            start = 2 * SLOTS + 4 * frames
            parts = (
                turned_back(summed(dq_slots, 2 * SLOTS, frame).T * 0.125),
                turned_back(summed(dk_slots, start, frame)),
                summed(dv_slots, start, frame).astype(jnp.bfloat16),
            )
            where = pl.ds(pl.multiple_of(frame * tokens, tokens), tokens)
            for place, part in enumerate(parts):
                d_all[side, chip, :, place * 128 : (place + 1) * 128] = part
                d_turned[place * 128 : (place + 1) * 128, where] = part.T
            return 0

        lax.fori_loop(0, frames, combine, 0)

        def normed_product(unit, side, chunk):
            first = (unit - first_out - 1) * half
            left = d_all[side, :, first : first + half, :].reshape(half_rows, 384)
            return dot_nt(left, w_own[lane_block(chunk), :])

        def normed_plan(point):
            run_plan(
                point,
                lambda unit, *where: (normed_product if unit > first_out else weight_product)(
                    unit, *where
                ),
            )

        normed_plan("combined")
        group_load.wait()

        piece = width // n_dp

        def own_columns(chunk, _):
            right = n1_group[:, :, lane_block(chunk)].reshape(frames * tokens, BLOCK)
            value = dot_nn(d_turned[...], right).astype(jnp.bfloat16)
            for part in range(BLOCK // piece):
                z_send[chunk * (BLOCK // piece) + part] = value[
                    :, part * piece : (part + 1) * piece
                ]
            return 0

        lax.fori_loop(0, chunks, own_columns, 0)
        mod_load(2).start()
        mod_load(3).start()
        z_copies = [
            remote(
                z_send.at[dp_peers[hop]],
                z_recv.at[hop],
                z_send_sem.at[hop],
                z_recv_sem.at[hop],
                (dp_peers[hop], head),
            )
            for hop in range(n_dp - 1)
        ]
        for copy in z_copies:
            copy.start()
        normed_plan("columns")

        def cond_block(block, vector, first):
            vector = vector.astype(jnp.bfloat16).astype(jnp.float32)

            def body(index, _):
                rows = pl.ds(pl.multiple_of(index * 64, 64), 64)
                page = block % 2 * pages + lax.div(index, tokens // 64)
                inside = pl.ds(pl.multiple_of(lax.rem(index, tokens // 64) * 64, 64), 64)
                total = jnp.zeros((64, 128), jnp.float32) if first else cond_sum[rows, :]
                for lanes in range(0, width, 128):
                    total = total + n1_group[page, inside, lanes : lanes + 128].astype(
                        jnp.float32
                    ) * vector[:, lanes : lanes + 128]
                cond_sum[rows, :] = total
                return 0

            lax.fori_loop(0, width // 64, body, 0)

        mod_load(2).wait()
        cond_block(2, saved_rows[0], True)
        mod_load(4).start()
        mod_load(3).wait()
        cond_block(3, saved_rows[1], False)
        mod_load(5).start()
        normed_plan("cond1")
        mod_load(4).wait()
        cond_block(4, saved_rows[2], False)
        mod_load(0).start()
        mod_load(5).wait()
        cond_block(5, saved_rows[3], False)
        mod_load(1).start()
        normed_plan("cond2")

        for copy in z_copies:
            copy.wait()
        total = z_send[group].astype(jnp.float32)
        for hop in range(n_dp - 1):
            total = total + z_recv[hop].astype(jnp.float32)
        p_send[...] = total.T.reshape(8, small, 384)

        def part_copy(flips):
            peer = peer_head(head, flips)
            return remote(
                p_send.at[peer],
                p_recv.at[head],
                a2a_send.at[2, flips],
                a2a_recv.at[2, flips],
                (group, peer),
            )

        for flips in others:
            part_copy(flips).start()
        p_recv[head] = p_send[head]

        for unit in (first_out + 1, first_out + 2):
            second_copy(unit).wait()
            value = from_core[slot_of(unit), :, ybit, xbit].astype(jnp.float32)
            value = value + from_second[slot_of(unit)].astype(jnp.float32)
            first = (unit - first_out - 1) * half
            dn1[first : first + half, :] = value.reshape(half, width)

        def first_norm_back(index, sums):
            shift_sum, scale_sum = sums
            rows = row_block(index)
            value = x_ref[rows, :].astype(jnp.float32)
            scale = lax.rsqrt(jnp.mean(value * value, axis=1, keepdims=True) + EPSILON)
            normed = value * scale
            grad = dn1[rows, :]
            shift_sum = shift_sum + jnp.sum(grad, axis=0, keepdims=True)
            scale_sum = scale_sum + jnp.sum(grad * normed, axis=0, keepdims=True)
            inner = grad * (1.0 + scale_one)
            mean = jnp.mean(inner * normed, axis=1, keepdims=True)
            gin_ref[rows, :] = mid[rows, :] + scale * (inner - normed * mean)
            return shift_sum, scale_sum

        shift_one_grad, scale_one_grad = lax.fori_loop(
            0, steps, first_norm_back, (row_zero, row_zero)
        )
        cond = cond_ref[...].astype(jnp.float32)
        gate = 1.0 / (1.0 + jnp.exp(-cond))
        vectors = jnp.concatenate(
            [
                cond * gate,
                shift_one_grad,
                scale_one_grad,
                *saved_rows,
                row_zero,
            ],
            axis=0,
        )
        rows_ref[group, ybit, xbit, core] = vectors.astype(jnp.bfloat16)

        mine = rows_ref.at[group, ybit, xbit, core]
        row_dp = [
            remote(mine, mine, row_dp_send.at[hop], row_dp_recv.at[hop], (dp_peers[hop], head))
            for hop in range(n_dp - 1)
        ]
        y_part = rows_ref.at[:, ybit, xbit, core]
        x_part = rows_ref.at[:, :, xbit, core]
        core_part = rows_ref.at[:, :, :, core]
        row_y = remote(y_part, y_part, row_send.at[0], row_recv.at[0], (group, y_peer))
        row_x = remote(x_part, x_part, row_send.at[1], row_recv.at[1], (group, x_peer))
        row_core = remote(core_part, core_part, row_send.at[2], row_recv.at[2], (group, core_peer))
        for copy in row_dp:
            copy.start()
        run_plan("rows")
        mod_load(0).wait()
        cond_block(0, shift_one_grad, False)
        mod_load(1).wait()
        cond_block(1, scale_one_grad, False)
        gcond_ref[...] = jnp.sum(cond_sum[...].T, axis=0, keepdims=True) * (
            gate * (1.0 + cond * (1.0 - gate))
        )
        for copy in row_dp:
            copy.wait()
        row_y.start()
        run_plan("row_y")
        row_y.wait()
        row_x.start()
        run_plan("row_x")
        row_x.wait()
        row_core.start()
        for flips in others:
            part_copy(flips).wait()
        for block in range(8):
            for place, target in enumerate((gq_ref, gk_ref, gv_ref)):
                target[:, block * 128 : (block + 1) * 128] = p_recv[
                    block, :, place * 128 : (place + 1) * 128
                ]
        run_plan("row_core")
        row_core.wait()
        everyone = rows_ref[...].reshape(n_dp * 64, width)
        device = group * 8 + head
        wanted = lax.broadcasted_iota(jnp.int32, (small, width), 0) + device * small
        column = lax.broadcasted_iota(jnp.int32, (small, width), 1)
        picked = dot_nt(jnp.where(wanted == column, 1.0, 0.0).astype(jnp.bfloat16), everyone)
        place = lax.rem(lax.broadcasted_iota(jnp.int32, picked.shape, 1), 8)
        picked = jnp.where(place == 0, picked, 0.0)
        mod_out = []
        for block in range(6):
            left = pltpu.roll(picked, 1 + block, 1).astype(jnp.bfloat16)
            dn1[block * small : (block + 1) * small, :] = dot_nn(left, everyone)
            mod_out.append(
                pltpu.make_async_copy(
                    dn1.at[pl.ds(block * small, small), :],
                    gmod_hbm.at[:, pl.ds(block * width, width)],
                    load_sem.at[block],
                )
            )
            mod_out[-1].start()
        run_plan("end")
        for copy in mod_out:
            copy.wait()
        for unit in (count - 2, count - 1):
            core_copy(unit).wait_send()

    pl.run_scoped(
        attention_part,
        pltpu.VMEM((frames, tokens, 128), jnp.bfloat16),
        pltpu.VMEM((frames, tokens, 128), jnp.bfloat16),
        pltpu.VMEM((frames, tokens, 128), jnp.bfloat16),
        pltpu.VMEM((frames, tokens, 128), jnp.float32),
        pltpu.VMEM((frames, tokens, width), jnp.bfloat16),
        pltpu.VMEM((width, 384), jnp.bfloat16),
        pltpu.VMEM((SLOTS + 1, 128, tokens), jnp.float32),
        pltpu.VMEM((SLOTS + 1, tokens, 128), jnp.float32),
        pltpu.VMEM((SLOTS + 1, tokens, 128), jnp.float32),
        pltpu.VMEM((frames, 2, tokens), jnp.float32),
        pltpu.VMEM((2, frames // 2, tokens, 384), jnp.bfloat16),
        pltpu.VMEM((384, frames * tokens), jnp.bfloat16),
        pltpu.VMEM((tokens, width), jnp.float32),
        pltpu.VMEM((width, 128), jnp.float32),
    )


PLAN = {
    "fed": [("P", 0), ("P", 1)],
    "normed": [("C", 0), ("C", 1)],
    "attended": [("P", 2), ("P", 3)],
    "branch": [("C", 2), ("C", 3)],
    "outputs": [("P", 4), ("P", 5)],
    "scope": [("F", 0), ("F", 1)],
    2: [("P", 6)],
    4: [("P", 7)],
    6: [("P", 8)],
    12: [("C", 4)],
    13: [("C", 5)],
    "combined": [("P", 9), ("P", 10), ("S", 0), ("S", 1), ("F", 2), ("F", 3), ("C", 9), ("C", 10)],
    "columns": [("C", 8)],
    "cond2": [("F", 4), ("F", 5), ("S", 2), ("S", 3), ("F", 9), ("F", 10), ("C", 6), ("C", 7), ("S", 4), ("S", 5), ("F", 8), ("D", 0), ("D", 1)],
    "rows": [("D", 2), ("D", 3)],
    "row_y": [("D", 4), ("D", 5)],
    "row_x": [("F", 6), ("F", 7), ("S", 8)],
    "end": [("S", 6), ("S", 7), ("D", 8), ("D", 6), ("D", 7)],
}


def back_part(n_dp, vmem_operands, hbm_operands):
    table, attended, lse, hidden = vmem_operands[:4]
    hbm_up = hbm_operands[6]
    tokens, width = hidden.shape
    group_tokens = attended.shape[0]
    frames = group_tokens // tokens
    hidden_width = hbm_up.shape[1]
    devices = n_dp * 8
    small, large = width // devices, hidden_width // devices
    first_up = large // small
    tiles = hidden_width // width
    units = first_up + tiles + 3
    dma = pltpu.SemaphoreType.DMA
    f32, bf16 = jnp.float32, jnp.bfloat16
    shape = jax.ShapeDtypeStruct
    return pl.pallas_call(
        lambda *refs: back_kernel(n_dp, *refs),
        out_shape=(
            shape((tokens, width), bf16),
            shape((tokens, width), f32),
            shape((8, 128), f32),
            *[shape((small, width), f32)] * 4,
            shape((small, hidden_width), f32),
            shape((large, width), f32),
            shape((small, 6 * width), f32),
            shape((1, width), f32),
        ),
        in_specs=[IN_SMEM]
        + [IN_VMEM] * (len(vmem_operands) - 1)
        + [IN_PLACE] * len(hbm_operands),
        out_specs=(IN_PLACE, *[IN_VMEM] * 8, IN_PLACE, IN_VMEM),
        scratch_shapes=[
            pltpu.VMEM((tokens, 128), f32),
            pltpu.VMEM((tokens, width), bf16),
            pltpu.VMEM((frames, tokens, 128), bf16),
            pltpu.VMEM((units, n_dp, 2, 2, small, width), bf16),
            pltpu.VMEM((units, n_dp, 2, small, width), bf16),
            pltpu.VMEM((units, n_dp, small, width), bf16),
            pltpu.VMEM((units - 2, n_dp - 1, small, width), bf16),
            pltpu.VMEM((2, n_dp, 2, 2, small, width), bf16),
            pltpu.VMEM((tokens, width), bf16),
            pltpu.VMEM((first_up + 2, 2, width // 2, tokens), bf16),
            pltpu.VMEM((tokens, width), bf16),
            pltpu.VMEM((tokens, hidden_width), bf16),
            pltpu.VMEM((tokens, width), bf16),
            pltpu.VMEM((tokens, width), f32),
            pltpu.VMEM((n_dp, 2, 2, 2, 8, width), bf16),
            pltpu.VMEM((n_dp, 384, width // n_dp), bf16),
            pltpu.VMEM((n_dp - 1, 384, width // n_dp), bf16),
            pltpu.VMEM((8, small, 384), f32),
            pltpu.VMEM((8, small, 384), f32),
            dma((16,)),
            dma((3, 8)),
            dma((3, 8)),
            *[dma((units,))] * 6,
            dma((units, n_dp - 1)),
            dma((units, n_dp - 1)),
            dma((3,)),
            dma((3,)),
            dma((n_dp - 1,)),
            dma((n_dp - 1,)),
            dma((n_dp - 1,)),
            dma((n_dp - 1,)),
            dma((6, frames // 2)),
        ],
        compiler_params=pltpu.CompilerParams(
            collective_id=0, has_side_effects=True, vmem_limit_bytes=67043328
        ),
        name="back_part",
    )(*vmem_operands, *hbm_operands)


def finish_kernel(*refs):
    count = len(refs) // 3
    sources, targets = refs[:count], refs[count : 2 * count]
    held, (load_sem, store_sem) = refs[2 * count : 3 * count], refs[3 * count :]
    loads = [
        pltpu.make_async_copy(source, room, load_sem.at[place])
        for place, (source, room) in enumerate(zip(sources, held))
    ]
    stores = [
        pltpu.make_async_copy(room, target, store_sem.at[place])
        for place, (room, target) in enumerate(zip(held, targets))
    ]
    for copy in loads:
        copy.start()
    for place in range(count - 1):
        loads[place].wait()
        stores[place].start()
    loads[-1].wait()
    targets[-1][...] = held[-1][0:1, 0:3]
    for copy in stores[:-1]:
        copy.wait()


def finish(arrays):
    shapes = [jax.ShapeDtypeStruct(array.shape, array.dtype) for array in arrays]
    held = [pltpu.VMEM(array.shape, array.dtype) for array in arrays]
    shapes[-1] = jax.ShapeDtypeStruct((1, 3), jnp.float32)
    return pl.pallas_call(
        finish_kernel,
        out_shape=tuple(shapes),
        in_specs=[IN_PLACE] * len(arrays),
        out_specs=(*[IN_PLACE] * (len(arrays) - 1), IN_VMEM),
        scratch_shapes=[
            *held,
            pltpu.SemaphoreType.DMA((len(arrays),)),
            pltpu.SemaphoreType.DMA((len(arrays),)),
        ],
        name="finish",
    )(*arrays)


def tables_kernel(lengths, valid_ref, wave_ref, table, first_ref, rope_ref, bias_ref):
    frames = rope_ref.shape[0]
    ends = [lengths[0, 0]]
    for clip in range(1, lengths.shape[1] - 1):
        ends.append(ends[-1] + lengths[0, clip])
    columns = 2 * SLOTS + 4 * frames
    for slot in range(SLOTS):
        table[slot] = 0
        table[SLOTS + slot] = 0
    for frame in range(frames):
        for way in range(1, 4):
            table[columns + 4 * frame + way] = SLOTS
    used = jnp.int32(0)
    for frame in range(frames):
        first = jnp.int32(0)
        for end in ends:
            first = jnp.where(end <= frame, end, first)
        first_ref[frame] = first
        cosine, sine = wave_ref[0, 0:1, :], wave_ref[0, 1:2, :]
        for place in range(1, wave_ref.shape[0]):
            here = frame - first == place
            cosine = jnp.where(here, wave_ref[place, 0:1, :], cosine)
            sine = jnp.where(here, wave_ref[place, 1:2, :], sine)
        rope_ref[frame, 0:1, :] = cosine
        rope_ref[frame, 1:2, :] = sine
        for back in range(4):
            if back > frame:
                table[2 * SLOTS + 4 * frame + back] = SLOTS
                continue
            held = frame - back >= first
            slot = jnp.where(held, used, SLOTS)
            table[2 * SLOTS + 4 * frame + back] = slot
            table[columns + 4 * (frame - back) + back] = slot

            @pl.when(held)
            def _(slot=slot, frame=frame, back=back):
                table[slot] = frame
                table[SLOTS + slot] = frame - back

            used = used + jnp.where(held, 1, 0)
    for slot in range(SLOTS):
        table[columns + 4 * frames + slot] = jnp.where(table[slot] == table[SLOTS + slot], 1, 0)
    for row in range(valid_ref.shape[0]):
        keep = jnp.broadcast_to(valid_ref[row : row + 1, :], (128, 128)).astype(jnp.float32)
        bias_ref[row * 128 : (row + 1) * 128, :] = jnp.where(keep.T > 0.5, 0.0, MASKED)


def tables_part(lengths, valid):
    group_tokens = valid.shape[0]
    frames = group_tokens // PATCHES
    powers = 10000.0 ** (-np.arange(HEAD_DIM // 2, dtype=np.float64) / (HEAD_DIM // 2))
    angles = np.arange(4, dtype=np.float32)[:, None] * powers.astype(np.float32)[None]
    cosine, sine = np.cos(angles), np.sin(angles)
    wave = np.stack(
        [np.concatenate([cosine] * 4, axis=1), np.concatenate([-sine, sine] * 2, axis=1)], axis=1
    ).astype(np.float32)
    return pl.pallas_call(
        tables_kernel,
        out_shape=(
            jax.ShapeDtypeStruct((3 * SLOTS + 8 * frames,), jnp.int32),
            jax.ShapeDtypeStruct((frames,), jnp.int32),
            jax.ShapeDtypeStruct((frames, 2, 128), jnp.float32),
            jax.ShapeDtypeStruct((group_tokens, 128), jnp.float32),
        ),
        in_specs=[IN_SMEM, IN_VMEM, IN_VMEM],
        out_specs=(IN_SMEM, IN_SMEM, IN_VMEM, IN_VMEM),
        name="tables",
    )(lengths, valid.reshape(group_tokens // 128, 128), jnp.asarray(wave))


def front_kernel(*refs):
    (
        x_hbm,
        cond_ref,
        rope_ref,
        wq_hbm,
        wk_hbm,
        wv_hbm,
        wmod_hbm,
        n1_hbm,
        q_hbm,
        k_hbm,
        v_hbm,
        mod_ref,
        x_all,
        n1_all,
        q_all,
        k_all,
        v_all,
        w_own,
        wmod,
        cond_own,
        cond_all,
        steer,
        load_sem,
        mod_sem,
        out_sem,
        cond_send,
        cond_recv,
        gather_send,
        gather_recv,
    ) = refs
    tokens, width = x_hbm.shape
    frames = x_all.shape[0]
    half = tokens // 2
    group = lax.axis_index("dp")
    head = lax.axis_index("head")
    core = lax.rem(head, 2)
    xbit = lax.rem(lax.div(head, 2), 2)
    ybit = lax.div(head, 4)
    core_peer, x_peer, y_peer = peer_head(head, 1), peer_head(head, 2), peer_head(head, 4)
    diagonal = peer_head(head, 6)
    others = range(1, 8)
    barrier = pltpu.get_barrier_semaphore()
    for flips in others:
        pl.semaphore_signal(
            barrier, inc=1, device_id=(group, peer_head(head, flips)), device_id_type=MESH_ID
        )
    own_lanes = pl.ds(head * 128, 128)
    mod_loads = [
        pltpu.make_async_copy(
            wmod_hbm.at[:, pl.ds(block * width, width)], wmod.at[block], mod_sem.at[block]
        )
        for block in range(6)
    ]
    loads = [pltpu.make_async_copy(x_hbm, x_all.at[head], load_sem.at[0])] + [
        pltpu.make_async_copy(
            source.at[:, own_lanes], w_own.at[:, pl.ds(place * 128, 128)], load_sem.at[1 + place]
        )
        for place, source in enumerate((wq_hbm, wk_hbm, wv_hbm))
    ]
    for copy in mod_loads[:2] + loads + mod_loads[2:]:
        copy.start()
    value = cond_ref[...].astype(jnp.float32)
    act = jnp.broadcast_to(value / (1.0 + jnp.exp(-value)), (8, width)).astype(jnp.bfloat16)
    cond_own[...] = act
    cond_all[head] = act

    low, high = pl.ds(0, half), pl.ds(half, half)

    def gather_copy(index):
        if index == 0:
            source, target, peer = x_hbm.at[low], x_all.at[head, low], x_peer
        elif index == 1:
            source, target, peer = x_hbm.at[high], x_all.at[head, high], y_peer
        elif index == 2:
            source, target, peer = x_hbm.at[low], x_all.at[head, low], y_peer
        elif index == 3:
            source, target, peer = x_hbm.at[high], x_all.at[head, high], x_peer
        elif index == 4:
            source, target, peer = x_all.at[x_peer, low], x_all.at[x_peer, low], y_peer
        elif index == 5:
            source, target, peer = x_all.at[y_peer, high], x_all.at[y_peer, high], x_peer
        elif index == 6:
            source, target, peer = x_hbm, x_all.at[head], core_peer
        else:
            block = (x_peer, y_peer, y_peer, x_peer, diagonal, diagonal)[index - 7]
            rows = (low, high, low, high, low, high)[index - 7]
            source, target, peer = x_all.at[block, rows], x_all.at[block, rows], core_peer
        return remote(
            source, target, gather_send.at[index], gather_recv.at[index], (group, peer)
        )

    def cond_copy(flips):
        peer = peer_head(head, flips)
        return remote(
            cond_own, cond_all.at[head], cond_send.at[flips], cond_recv.at[flips], (group, peer)
        )

    pl.semaphore_wait(barrier, 7)
    for flips in others:
        cond_copy(flips).start()
    for index in (0, 1, 6, 2, 3):
        gather_copy(index).start()

    for flips in others:
        cond_copy(flips).wait()
    everyone = cond_all[...].reshape(frames * 8, width)

    def modulate(block):
        mod_loads[block].wait()

        def body(chunk, _):
            lanes = pl.ds(pl.multiple_of(chunk * BLOCK, BLOCK), BLOCK)
            steer[block, :, lanes] = dot_nn(everyone, wmod[block, :, lanes])
            return 0

        lax.fori_loop(0, width // BLOCK, body, 0)
        mod_ref[block : block + 1, :] = steer[block, pl.ds(pl.multiple_of(head * 8, 8), 8), :][0:1]

    modulate(0)
    modulate(1)
    for copy in loads:
        copy.wait()

    def out_copy(frame, rows, item):
        return pltpu.make_async_copy(
            n1_all.at[frame, rows], n1_hbm.at[frame, rows], out_sem.at[item]
        )

    def project(frame, side, item):
        steer_rows = pl.ds(pl.multiple_of(frame * 8, 8), 8)
        shift, scaling = steer[0, steer_rows, :][0:1], steer[1, steer_rows, :][0:1]

        def norm(index, _):
            rows = pl.ds(pl.multiple_of(side * half + index * 32, 32), 32)
            value = x_all[frame, rows, :].astype(jnp.float32)
            scale = lax.rsqrt(jnp.mean(value * value, axis=1, keepdims=True) + EPSILON)
            n1_all[frame, rows, :] = (value * scale * (1.0 + scaling) + shift).astype(
                jnp.bfloat16
            )
            return 0

        lax.fori_loop(0, half // 32, norm, 0)
        rows = pl.ds(pl.multiple_of(side * half, half), half)
        out_copy(frame, rows, item).start()
        value = dot_nn(n1_all[frame, rows, :], w_own[...])
        cosine, sine = rope_ref[frame, 0:1, :], rope_ref[frame, 1:2, :]
        for place, target in enumerate((q_all, k_all, v_all)):
            part = value[:, place * 128 : (place + 1) * 128]
            if place < 2:
                part = part * cosine + turn_pairs(part) * sine
            target[frame, rows, :] = part.astype(jnp.bfloat16)

    def stage(number, other_core):
        at_core = 1 - core if other_core else core

        def body(index, _):
            if number == 0:
                at_x, at_y, side = xbit, ybit, index
            elif number == 3:
                at_x, at_y, side = 1 - xbit, 1 - ybit, index
            else:
                at_x = xbit + (1 - index) * (1 - 2 * xbit)
                at_y = ybit + index * (1 - 2 * ybit)
                side = index if number == 1 else 1 - index
            frame = 4 * at_y + 2 * at_x + at_core
            project(frame, side, number * 4 + other_core * 2 + index)
            return 0

        lax.fori_loop(0, 2, body, 0)

    stage(0, 0)
    gather_copy(6).wait()
    stage(0, 1)
    for block in range(2, 6):
        modulate(block)
    for number, arrivals in ((1, (0, 1)), (2, (2, 3)), (3, (4, 5))):
        for index in arrivals:
            gather_copy(index).wait()
            if number == 1:
                gather_copy(index + 4).start()
            gather_copy(index + 7).start()
        stage(number, 0)
        for index in arrivals:
            gather_copy(index + 7).wait()
        stage(number, 1)
    outs = [
        pltpu.make_async_copy(source, target, load_sem.at[place])
        for place, (source, target) in enumerate(((q_all, q_hbm), (k_all, k_hbm), (v_all, v_hbm)))
    ]
    for copy in outs:
        copy.start()
    for item in range(16):
        out_copy(0, low, item).wait()
    for copy in outs:
        copy.wait()


def front_part(hidden, cond, rope, query_weight, key_weight, value_weight, modulation_weight):
    tokens, width = hidden.shape
    frames = rope.shape[0]
    dma = pltpu.SemaphoreType.DMA
    bf16, f32 = jnp.bfloat16, jnp.float32
    in_hbm = pl.BlockSpec(memory_space=pltpu.HBM)
    block = jax.ShapeDtypeStruct((frames, tokens, 128), bf16)
    return pl.pallas_call(
        front_kernel,
        out_shape=(
            jax.ShapeDtypeStruct((frames, tokens, width), bf16),
            block,
            block,
            block,
            jax.ShapeDtypeStruct((8, width), f32),
        ),
        in_specs=[in_hbm, IN_VMEM, IN_VMEM] + [in_hbm] * 4,
        out_specs=(in_hbm,) * 4 + (IN_VMEM,),
        scratch_shapes=[
            pltpu.VMEM((frames, tokens, width), bf16),
            pltpu.VMEM((frames, tokens, width), bf16),
            pltpu.VMEM((frames, tokens, 128), bf16),
            pltpu.VMEM((frames, tokens, 128), bf16),
            pltpu.VMEM((frames, tokens, 128), bf16),
            pltpu.VMEM((width, 384), bf16),
            pltpu.VMEM((6, width, width), bf16),
            pltpu.VMEM((8, width), bf16),
            pltpu.VMEM((frames, 8, width), bf16),
            pltpu.VMEM((6, frames * 8, width), f32),
            dma((4,)),
            dma((6,)),
            dma((16,)),
            dma((8,)),
            dma((8,)),
            dma((13,)),
            dma((13,)),
        ],
        compiler_params=pltpu.CompilerParams(
            collective_id=1, has_side_effects=True, vmem_limit_bytes=67043328
        ),
        name="front_part",
    )(hidden, cond, rope, query_weight, key_weight, value_weight, modulation_weight)


def per_device(
    hidden_in,
    frame_cond,
    query_weight,
    key_weight,
    value_weight,
    output_weight,
    up_weight,
    down_weight,
    modulation_weight,
    clip_lengths,
    patch_valid,
    cotangent,
):
    tok_dev, model_width = hidden_in.shape
    group_tokens = patch_valid.shape[0]
    frames = group_tokens // PATCHES
    head_index = lax.axis_index("head")
    n_dp = lax.axis_size("dp")
    table, first_frames, rope, bias = tables_part(clip_lengths, patch_valid)
    normed_group, head_query, head_key, head_value, modulation = front_part(
        hidden_in, frame_cond, rope, query_weight, key_weight, value_weight, modulation_weight
    )
    attended, logsum = attend_forward(
        first_frames,
        *[array.reshape(group_tokens, 128) for array in (head_query, head_key, head_value)],
        bias,
    )
    results = back_part(
        n_dp,
        (table, attended, logsum, hidden_in, cotangent, modulation, rope, frame_cond),
        (
            head_query,
            head_key,
            head_value,
            bias.reshape(frames, PATCHES, 128),
            normed_group,
            output_weight,
            up_weight,
            down_weight,
            query_weight,
            key_weight,
            value_weight,
            modulation_weight,
        ),
    )
    (block_out, grad_input, statistics, gq, gk, gv, go, gup, gdown, gmod, gcond) = results
    (grad_input, gmod, block_out, gup, gdown, gq, gk, gv, go, gcond, statistics) = finish(
        (grad_input, gmod, block_out, gup, gdown, gq, gk, gv, go, gcond, statistics)
    )
    return (
        block_out,
        grad_input,
        gcond,
        gq,
        gk,
        gv,
        go,
        gup,
        gdown,
        gmod,
        statistics,
    )


def solution(mesh):
    in_specs = (
        P(("dp", "head"), None),
        P(("dp", "head"), None),
        P(),
        P(),
        P(),
        P(),
        P(),
        P(),
        P(),
        P("dp", None),
        P("dp"),
        P(("dp", "head"), None),
    )
    out_specs = (
        P(("dp", "head"), None),
        P(("dp", "head"), None),
        P(("dp", "head"), None),
        P(("dp", "head"), None),
        P(("dp", "head"), None),
        P(("dp", "head"), None),
        P(("dp", "head"), None),
        P(("dp", "head"), None),
        P(("dp", "head"), None),
        P(("dp", "head"), None),
        P(("dp", "head"), None),
    )
    return jax.shard_map(
        per_device, mesh=mesh, in_specs=in_specs, out_specs=out_specs, check_vma=False
    )
```
